32 devices in a mesh: dp: 4 (over z), fsdp: 8 (over y, x, core).
Axes of the slice: x: 2, y: 2, z: 4, core: 2. Of those that a mesh axis runs over, the one named last changes fastest.
Arguments:
- tokens: bfloat16 [32, 512, 1024], P(('dp', 'fsdp')), may hold values from -6 to 6
- memory: bfloat16 [32, 512, 1024], P(('dp', 'fsdp')), may hold values from -6 to 6
- compressed: bfloat16 [32, 512, 1024], P(('dp', 'fsdp')), may hold values from -6 to 6
- mem_fill: int32 [32], P(('dp', 'fsdp')), may hold values from 0 to 512, as said below
- cmem_fill: int32 [32], P(('dp', 'fsdp')), may hold values from 0 to 512, as said below
- pad_mask: int32 [32, 512], P(('dp', 'fsdp')), may hold values from 0 to 1, as said below
- first_gain: bfloat16 [1024], P('fsdp'), may hold values from 0.5 to 1.5
- first_shift: bfloat16 [1024], P('fsdp'), may hold values from -1.5 to 1.5
- query_weight: bfloat16 [1024, 1024], P('fsdp'), may hold values from -0.1875 to 0.1875
- key_weight: bfloat16 [1024, 1024], P('fsdp'), may hold values from -0.1875 to 0.1875
- value_weight: bfloat16 [1024, 1024], P('fsdp'), may hold values from -0.1875 to 0.1875
- position_weight: bfloat16 [1024, 1024], P('fsdp'), may hold values from -0.1875 to 0.1875
- content_bias: bfloat16 [1024], P('fsdp'), may hold values from -3 to 3
- position_bias: bfloat16 [1024], P('fsdp'), may hold values from -3 to 3
- output_weight: bfloat16 [1024, 1024], P('fsdp'), may hold values from -0.75 to 0.75
- second_gain: bfloat16 [1024], P('fsdp'), may hold values from 0.5 to 1.5
- second_shift: bfloat16 [1024], P('fsdp'), may hold values from -1.5 to 1.5
- inner_weight: bfloat16 [1024, 4096], P('fsdp'), may hold values from -0.1875 to 0.1875
- inner_bias: bfloat16 [4096], P('fsdp'), may hold values from -3 to 3
- outer_weight: bfloat16 [4096, 1024], P('fsdp'), may hold values from -0.125 to 0.125
- outer_bias: bfloat16 [1024], P('fsdp'), may hold values from -3 to 3
- conv_weight: bfloat16 [3072, 1024], P('fsdp'), may hold values from -0.109375 to 0.109375
- conv_bias: bfloat16 [1024], P('fsdp'), may hold values from -3 to 3
- out_grad: bfloat16 [32, 512, 1024], P(('dp', 'fsdp')), may hold values from -6 to 6
- comp_grad: bfloat16 [32, 170, 1024], P(('dp', 'fsdp')), may hold values from -6 to 6
Outputs:
- out_tokens: bfloat16 [32, 512, 1024], P(('dp', 'fsdp'))
- token_gradient: float32 [32, 512, 1024], P(('dp', 'fsdp'))
- new_compressed: bfloat16 [32, 170, 1024], P(('dp', 'fsdp'))
- first_gain_gradient: float32 [1024], P('fsdp')
- first_shift_gradient: float32 [1024], P('fsdp')
- query_gradient: float32 [1024, 1024], P('fsdp')
- key_gradient: float32 [1024, 1024], P('fsdp')
- value_gradient: float32 [1024, 1024], P('fsdp')
- position_gradient: float32 [1024, 1024], P('fsdp')
- content_bias_gradient: float32 [1024], P('fsdp')
- position_bias_gradient: float32 [1024], P('fsdp')
- output_gradient: float32 [1024, 1024], P('fsdp')
- second_gain_gradient: float32 [1024], P('fsdp')
- second_shift_gradient: float32 [1024], P('fsdp')
- inner_gradient: float32 [1024, 4096], P('fsdp')
- inner_bias_gradient: float32 [4096], P('fsdp')
- outer_gradient: float32 [4096, 1024], P('fsdp')
- outer_bias_gradient: float32 [1024], P('fsdp')
- conv_gradient: float32 [3072, 1024], P('fsdp')
- conv_bias_gradient: float32 [1024], P('fsdp')
The draws below stay inside these ranges and needn't reach their ends.
Inputs may be any that keep to these rules, and one draw needn't show every extreme that they name: The valid memory rows of a stream are its last mem_fill rows; in every draw some stream has a full memory. The valid compressed rows of a stream are its last cmem_fill rows; in every draw some stream has a full compressed memory. `pad_mask`: each stream's real tokens are a prefix of one or more tokens; in every draw some stream has no padding.
All inputs are finite; a program needn't handle non-finite values.
Results may differ from the reference program's by a relative error of at most 0.022.
Values may be sent and summed in bfloat16 or wider, within the bound.
A program may use at most 256 MiB of HBM per device.

```python
import math
import jax
import jax.numpy as jnp
from jax import lax

D = 1024
HEADS = 8
DH = 128
FF = 4096
SEG = 512
MEM = 512
CMEM = 512
RATE = 3
STREAMS = 32
NC = 170
KEYS = 1536


def skewed_fill(key, count, most):
    first, second = jax.random.split(key)
    drawn = jax.random.randint(first, (count,), 0, most + 1, dtype=jnp.int32)
    filled = drawn * drawn // most * drawn // most
    spot = jax.random.randint(second, (), 0, count, dtype=jnp.int32)
    return jnp.where(jnp.arange(count, dtype=jnp.int32) == spot, most, filled).astype(jnp.int32)


def draw_mem_fill(key, part):
    return skewed_fill(jax.random.fold_in(key, 11), STREAMS, MEM)


def draw_cmem_fill(key, part):
    return skewed_fill(jax.random.fold_in(key, 23), STREAMS, CMEM)


def draw_pad_mask(key, part):
    first, second = jax.random.split(jax.random.fold_in(key, 37))
    drawn = jax.random.randint(first, (STREAMS,), 0, SEG, dtype=jnp.int32)
    length = SEG - drawn * drawn // SEG * drawn // SEG
    spot = jax.random.randint(second, (), 0, STREAMS, dtype=jnp.int32)
    length = jnp.where(jnp.arange(STREAMS, dtype=jnp.int32) == spot, SEG, length)
    return (jnp.arange(SEG, dtype=jnp.int32)[None, :] < length[:, None]).astype(jnp.int32)


def block_scale(own_key, shape, cuts, smallest, high):
    level, own = 1.0, jax.random.fold_in(own_key, 6)
    for axis_at, shards_of in cuts:
        steps = jnp.exp(jax.random.uniform(jax.random.fold_in(own, axis_at), (shards_of,), jnp.float32, smallest / len(cuts), high / len(cuts)))
        level = level * jnp.repeat(steps, shape[axis_at] // shards_of).reshape([-1 if axis == axis_at else 1 for axis in range(len(shape))])
    return level


def bell_draw(own_key, shape, scale, bound, pieces=(), kind=jnp.bfloat16):
    values = scale * jax.random.normal(own_key, shape, jnp.float32)
    if pieces:
        values = values * block_scale(own_key, shape, pieces, -0.22, 0.18)
    return jnp.clip(values, -bound, bound).astype(kind)


def setup_inputs(seed: int = 0) -> dict:
    arg_keys = jax.random.split(jax.random.key(seed), 26)
    tokens = bell_draw(arg_keys[0], (STREAMS, SEG, D), 1.0, 6.0, ((0, 32),))
    memory = bell_draw(arg_keys[1], (STREAMS, MEM, D), 1.0, 6.0, ((0, 32),))
    compressed = bell_draw(arg_keys[2], (STREAMS, CMEM, D), 1.0, 6.0, ((0, 32),))
    mem_fill = draw_mem_fill(jax.random.fold_in(arg_keys[25], 71), 0)
    cmem_fill = draw_cmem_fill(jax.random.fold_in(arg_keys[25], 71), 0)
    pad_mask = draw_pad_mask(jax.random.fold_in(arg_keys[25], 71), 0)
    first_gain = jnp.clip(1.0 + 0.1 * jax.random.normal(arg_keys[6], (D,), jnp.float32), 0.5, 1.5).astype(jnp.bfloat16)
    first_shift = bell_draw(arg_keys[7], (D,), 0.3, 1.5, ((0, 8),))
    query_weight = bell_draw(arg_keys[8], (D, D), D ** -0.5, 0.1875, ((0, 8),))
    key_weight = bell_draw(arg_keys[9], (D, D), D ** -0.5, 0.1875, ((0, 8),))
    value_weight = bell_draw(arg_keys[10], (D, D), D ** -0.5, 0.1875, ((0, 8),))
    position_weight = bell_draw(arg_keys[11], (D, D), D ** -0.5, 0.1875, ((0, 8),))
    content_bias = bell_draw(arg_keys[12], (D,), 0.5, 3.0, ((0, 8),))
    position_bias = bell_draw(arg_keys[13], (D,), 0.5, 3.0, ((0, 8),))
    output_weight = bell_draw(arg_keys[14], (D, D), (D // 16) ** -0.5, 0.75, ((0, 8),))
    second_gain = jnp.clip(1.0 + 0.1 * jax.random.normal(arg_keys[15], (D,), jnp.float32), 0.5, 1.5).astype(jnp.bfloat16)
    second_shift = bell_draw(arg_keys[16], (D,), 0.3, 1.5, ((0, 8),))
    inner_weight = bell_draw(arg_keys[17], (D, FF), D ** -0.5, 0.1875, ((0, 8),))
    inner_bias = bell_draw(arg_keys[18], (FF,), 0.5, 3.0, ((0, 8),))
    outer_weight = bell_draw(arg_keys[19], (FF, D), (FF // 2) ** -0.5, 0.125, ((0, 8),))
    outer_bias = bell_draw(arg_keys[20], (D,), 0.5, 3.0, ((0, 8),))
    conv_weight = bell_draw(arg_keys[21], (RATE * D, D), (RATE * D) ** -0.5, 0.109375, ((0, 8),))
    conv_bias = bell_draw(arg_keys[22], (D,), 0.5, 3.0, ((0, 8),))
    out_grad = bell_draw(arg_keys[23], (STREAMS, SEG, D), 1.0, 6.0, ((0, 32),))
    comp_grad = bell_draw(arg_keys[24], (STREAMS, NC, D), 1.0, 6.0, ((0, 32),))
    return dict(tokens=tokens, memory=memory, compressed=compressed, mem_fill=mem_fill, cmem_fill=cmem_fill, pad_mask=pad_mask, first_gain=first_gain, first_shift=first_shift, query_weight=query_weight, key_weight=key_weight, value_weight=value_weight, position_weight=position_weight, content_bias=content_bias, position_bias=position_bias, output_weight=output_weight, second_gain=second_gain, second_shift=second_shift, inner_weight=inner_weight, inner_bias=inner_bias, outer_weight=outer_weight, outer_bias=outer_bias, conv_weight=conv_weight, conv_bias=conv_bias, out_grad=out_grad, comp_grad=comp_grad)


@jax.custom_vjp
def low(v):
    return lax.optimization_barrier(v.astype(jnp.bfloat16)).astype(jnp.float32)

@jax.custom_vjp
def low_back(v):
    return v

def low_keep(v):
    return (low(v), None)

def low_pass(kept, grad):
    return (grad,)

def back_keep(v):
    return (v, None)

def back_low(kept, grad):
    return (low(grad),)
low.defvjp(low_keep, low_pass)
low_back.defvjp(back_keep, back_low)
EPSILON = 1e-05
MASKED = -1000000000.0
HIGH = lax.Precision.HIGHEST

def smooth_gate(values):
    return jax.nn.gelu(values, approximate=True)

def layer_norm(rows, gain, shift):
    center = lax.optimization_barrier(jnp.mean(rows, axis=-1, keepdims=True))
    centered = rows - center
    spread = lax.optimization_barrier(jnp.mean(centered * centered, axis=-1, keepdims=True))
    return centered * lax.rsqrt(spread + EPSILON) * gain + shift

def positions(count, width):
    distance = (count - 1 - jnp.arange(count, dtype=jnp.int32)).astype(jnp.float32)
    rates = jnp.exp(jnp.arange(0, width, 2, dtype=jnp.int32).astype(jnp.float32) * (-math.log(10000.0) / width))
    angle = distance[:, None] * rates[None, :]
    return jnp.concatenate([jnp.sin(angle), jnp.cos(angle)], axis=1)

def rel_shift(table):
    leading, rows, cols = table.shape
    padded = jnp.pad(table, ((0, 0), (0, 0), (1, 0)))
    folded = padded.reshape(leading, cols + 1, rows)
    return folded[:, 1:, :].reshape(leading, rows, cols)

def key_mask(mem_fill, cmem_fill, pad_mask, cmem_rows, mem_rows):
    seg_rows = pad_mask.shape[-1]
    mem_fill = mem_fill.astype(jnp.int32)
    cmem_fill = cmem_fill.astype(jnp.int32)
    comp_valid = jnp.arange(cmem_rows, dtype=jnp.int32)[None, :] >= (cmem_rows - cmem_fill)[:, None]
    mem_valid = jnp.arange(mem_rows, dtype=jnp.int32)[None, :] >= (mem_rows - mem_fill)[:, None]
    keyvalid = jnp.concatenate([comp_valid, mem_valid, pad_mask.astype(jnp.int32) == 1], axis=1)
    column = jnp.arange(cmem_rows + mem_rows + seg_rows, dtype=jnp.int32)[None, :]
    own = (cmem_rows + mem_rows + jnp.arange(seg_rows, dtype=jnp.int32))[:, None]
    return (column <= own)[None] & (keyvalid[:, None, :] | (column == own)[None])

def split_heads(array):
    return array.reshape(array.shape[0], HEADS, DH)

def stream_layer(params, pos_low, tokens, memory, compressed, mem_fill, cmem_fill, pad_mask):
    first_gain, first_shift, query_weight, key_weight, value_weight, position_weight, content_bias, position_bias, output_weight, second_gain, second_shift, inner_weight, inner_bias, outer_weight, outer_bias = params
    seg_rows = tokens.shape[0]
    whole = jnp.concatenate([compressed, memory, tokens], axis=0)
    normed = low(layer_norm(whole, first_gain, first_shift))
    query = low_back(jnp.dot(normed[-seg_rows:], query_weight, precision=HIGH))
    query_u = low(query + content_bias)
    query_v = low(query + position_bias)
    keys = low(low_back(jnp.dot(normed, key_weight, precision=HIGH)))
    values = low(low_back(jnp.dot(normed, value_weight, precision=HIGH)))
    relative = low(low_back(jnp.dot(pos_low, position_weight, precision=HIGH)))
    content = jnp.einsum('ihd,jhd->hij', split_heads(query_u), split_heads(keys), precision=HIGH)
    position = rel_shift(jnp.einsum('ihd,jhd->hij', split_heads(query_v), split_heads(relative), precision=HIGH))
    logits = low_back(content + position)
    allowed = key_mask(mem_fill[None], cmem_fill[None], pad_mask[None], CMEM, MEM)[0]
    scores = jnp.where(allowed[None], logits * (1.0 / math.sqrt(DH)), MASKED)
    top = lax.optimization_barrier(jnp.max(scores, axis=-1, keepdims=True))
    expo = jnp.exp(scores - top)
    weights = low(expo / lax.optimization_barrier(jnp.sum(expo, axis=-1, keepdims=True)))
    mixed = jnp.einsum('hij,jhd->ihd', weights, split_heads(values), precision=HIGH).reshape(seg_rows, D)
    mixed = low(low_back(mixed))
    hidden = tokens + low_back(jnp.dot(mixed, output_weight, precision=HIGH))
    inner = low(layer_norm(hidden, second_gain, second_shift))
    preact = low_back(jnp.dot(inner, inner_weight, precision=HIGH) + inner_bias)
    active = low(smooth_gate(preact))
    return hidden + jnp.dot(active, outer_weight, precision=HIGH) + outer_bias

def reference(tokens, memory, compressed, mem_fill, cmem_fill, pad_mask, first_gain, first_shift, query_weight, key_weight, value_weight, position_weight, content_bias, position_bias, output_weight, second_gain, second_shift, inner_weight, inner_bias, outer_weight, outer_bias, conv_weight, conv_bias, out_grad, comp_grad):
    params = tuple((item.astype(jnp.float32) for item in (first_gain, first_shift, query_weight, key_weight, value_weight, position_weight, content_bias, position_bias, output_weight, second_gain, second_shift, inner_weight, inner_bias, outer_weight, outer_bias)))
    conv_params = (conv_weight.astype(jnp.float32), conv_bias.astype(jnp.float32))
    memory_wide = memory.astype(jnp.float32)
    compressed_wide = compressed.astype(jnp.float32)
    fills = mem_fill.astype(jnp.int32)
    cfills = cmem_fill.astype(jnp.int32)
    masks = pad_mask.astype(jnp.int32)
    pos_low = low(positions(KEYS, D))
    mem_valid = (jnp.arange(MEM, dtype=jnp.int32)[None, :] >= (MEM - fills)[:, None]).astype(jnp.float32)
    start = MEM - RATE * NC
    group_last = (start + RATE * jnp.arange(NC, dtype=jnp.int32) + RATE - 1).astype(jnp.int32)
    group_valid = (group_last[None, :] >= (MEM - fills)[:, None]).astype(jnp.float32)
    taps = (memory_wide * mem_valid[..., None])[:, start:, :].reshape(STREAMS, NC, RATE * D)

    def forward(token_rows, layer_params, comp_params):

        @jax.checkpoint
        def step(carry, inputs):
            return (carry, stream_layer(layer_params, pos_low, *inputs))
        carry, result = lax.scan(step, jnp.zeros((), dtype=jnp.float32), (token_rows, memory_wide, compressed_wide, fills, cfills, masks))
        made = (jnp.einsum('bnk,kd->bnd', taps, comp_params[0], precision=HIGH) + comp_params[1]) * group_valid[..., None]
        return (result, made)
    (result, made), pull = jax.vjp(forward, tokens.astype(jnp.float32), params, conv_params)
    token_gradient, layer_grads, conv_grads = pull((out_grad.astype(result.dtype), comp_grad.astype(made.dtype)))
    share = 1.0 / STREAMS
    layer_grads = tuple((item * share for item in layer_grads))
    conv_grads = tuple((item * share for item in conv_grads))
    return (result.astype(jnp.bfloat16), token_gradient, made.astype(jnp.bfloat16), layer_grads[0], layer_grads[1], layer_grads[2], layer_grads[3], layer_grads[4], layer_grads[5], layer_grads[6], layer_grads[7], layer_grads[8], layer_grads[9], layer_grads[10], layer_grads[11], layer_grads[12], layer_grads[13], layer_grads[14], conv_grads[0], conv_grads[1])
```

```python
import math

import jax
import jax.numpy as jnp
from jax import lax
from jax.experimental import pallas as pl
from jax.experimental.pallas import tpu as pltpu
from jax.sharding import PartitionSpec as P

HEADS = 8
DH = 128
RATE = 3
BLK = 128
NEG = -1.2e10
f32 = jnp.float32
bf16 = jnp.bfloat16


EPSILON = 1e-05
MASKED = -1000000000.0


def smooth_gate(values):
    return jax.nn.gelu(values, approximate=True)


def norm_parts(rows, gain, shift):
    center = jnp.mean(rows, axis=-1, keepdims=True)
    centered = rows - center
    spread = lax.rsqrt(jnp.mean(centered * centered, axis=-1, keepdims=True) + EPSILON)
    scaled = centered * spread
    return (scaled * gain.astype(jnp.float32) + shift.astype(jnp.float32), scaled, spread)


def norm_back(grad, scaled, spread, gain):
    inner = grad * gain.astype(jnp.float32)
    return spread * (
        inner
        - jnp.mean(inner, axis=-1, keepdims=True)
        - scaled * jnp.mean(inner * scaled, axis=-1, keepdims=True)
    )


def positions(count, width):
    distance = (count - 1 - jnp.arange(count, dtype=jnp.int32)).astype(jnp.float32)
    rates = jnp.exp(
        jnp.arange(0, width, 2, dtype=jnp.int32).astype(jnp.float32) * (-math.log(10000.0) / width)
    )
    angle = distance[:, None] * rates[None, :]
    return jnp.concatenate([jnp.sin(angle), jnp.cos(angle)], axis=1)


def dot_nt(a,b): return lax.dot_general(a,b,(((1,),(1,)),((),())),preferred_element_type=f32)
def dot_nn(a,b): return lax.dot_general(a,b,(((1,),(0,)),((),())),preferred_element_type=f32)

def attn_fwd_kernel(qu_ref,qv_ref,k_ref,v_ref,r_ref,bias_ref,o_ref,p_ref):
    seg=qu_ref.shape[0]; total=k_ref.shape[0]; old=total-seg
    c=math.log2(math.e)/math.sqrt(DH)
    for ib in range(seg//BLK):
        rows=pl.ds(ib*BLK,BLK)
        L=old+(ib+1)*BLK
        qu=qu_ref[rows,:]; qv=qv_ref[rows,:]
        raw=dot_nt(qv,r_ref[pl.ds(total-L,L),:])
        z=dot_nt(qu,k_ref[pl.ds(0,L),:])+pltpu.roll(raw,L-(BLK-1),axis=1,stride=1,stride_axis=0)
        M=L-BLK
        za=z[:,:M]+bias_ref[:,:M]
        rr=lax.broadcasted_iota(jnp.int32,(BLK,BLK),0); cc=lax.broadcasted_iota(jnp.int32,(BLK,BLK),1)
        zb=z[:,M:]
        zb=jnp.where(cc==rr,zb,jnp.where(cc<rr,zb+bias_ref[:,pl.ds(M,BLK)],NEG))
        top=jnp.maximum(jnp.max(za,axis=1,keepdims=True),jnp.max(zb,axis=1,keepdims=True))
        ea=jnp.exp2((za-top)*c); eb=jnp.exp2((zb-top)*c)
        inv=1.0/(jnp.sum(ea,axis=1,keepdims=True)+jnp.sum(eb,axis=1,keepdims=True))
        pa=(ea*inv).astype(bf16); pb=(eb*inv).astype(bf16)
        p_ref[0,rows,pl.ds(0,M)]=pa
        p_ref[0,rows,pl.ds(M,BLK)]=pb
        o_ref[rows,:]=(dot_nn(pa,v_ref[pl.ds(0,M),:])+dot_nn(pb,v_ref[pl.ds(M,BLK),:])).astype(bf16)

def attn_fwd(qu,qv,k,v,r,bias):
    seg,width=qu.shape; total=k.shape[0]; heads=width//DH
    col=lambda n: pl.BlockSpec((n,DH),lambda h:(0,h))
    return pl.pallas_call(attn_fwd_kernel,grid=(heads,),
        in_specs=[col(seg),col(seg),col(total),col(total),col(total),pl.BlockSpec((1,total),lambda h:(0,0))],
        out_specs=[col(seg),pl.BlockSpec((1,seg,total),lambda h:(h,0,0))],
        out_shape=[jax.ShapeDtypeStruct((seg,width),bf16),jax.ShapeDtypeStruct((heads,seg,total),bf16)],
        cost_estimate=pl.CostEstimate(flops=6*seg*total*width,bytes_accessed=2*(3*seg*width+3*total*width+heads*seg*total),transcendentals=heads*seg*total),
        compiler_params=pltpu.CompilerParams(vmem_limit_bytes=40<<20),name="attn_fwd")(qu,qv,k,v,r,bias)

def attn_bwd_kernel(qu_ref,qv_ref,qut_ref,qvrt_ref,k_ref,v_ref,r_ref,p_ref,g_ref,gt_ref,dq_ref,dkt_ref,dvt_ref,drt_ref,sums_ref,dk_acc,dv_acc,dr_acc):
    seg=g_ref.shape[0]; total=k_ref.shape[0]; old=total-seg
    scale=1.0/math.sqrt(DH)
    rr=lax.broadcasted_iota(jnp.int32,(BLK,BLK),0); cc=lax.broadcasted_iota(jnp.int32,(BLK,BLK),1)
    flip=(rr+cc==BLK-1).astype(bf16)
    su=jnp.zeros((1,DH),f32); sv=jnp.zeros((1,DH),f32)
    nb=seg//BLK
    for ib in range(nb-1,-1,-1):
        rows=pl.ds(ib*BLK,BLK)
        L=old+(ib+1)*BLK
        g=g_ref[rows,:]; gt=gt_ref[:,rows]; qut=qut_ref[:,rows]
        plow=p_ref[0,rows,pl.ds(0,L)]
        p=plow.astype(f32)
        dp=dot_nt(g,v_ref[pl.ds(0,L),:])
        d=jnp.sum(p*dp,axis=1,keepdims=True)
        dz=(p*(dp-d)*scale).astype(bf16)
        dvt=dot_nn(gt,plow)
        dkt=dot_nn(qut,dz)
        dqu=dot_nn(dz,k_ref[pl.ds(0,L),:])
        rev=dot_nn(flip,dz)
        raw=pltpu.roll(rev,0,axis=1,stride=1,stride_axis=0).astype(bf16)
        T=pl.ds(total-L,L)
        dqv_rev=dot_nn(raw,r_ref[T,:])
        qvr=dot_nt(qvrt_ref[:,rows],flip).astype(bf16)
        drt=dot_nn(qvr,raw)
        dqv=lax.dot_general(flip.astype(f32),dqv_rev,(((1,),(0,)),((),())),preferred_element_type=f32,precision=lax.Precision.HIGHEST)
        su+=jnp.sum(dqu,axis=0,keepdims=True); sv+=jnp.sum(dqv,axis=0,keepdims=True)
        dq_ref[rows,:]=(dqu+dqv).astype(bf16)
        J=pl.ds(0,L)
        if ib==nb-1:
            dv_acc[...]=dvt; dk_acc[...]=dkt; dr_acc[...]=drt
        else:
            dv_acc[:,J]+=dvt; dk_acc[:,J]+=dkt; dr_acc[:,T]+=drt
    dkt_ref[...]=dk_acc[...].astype(bf16); dvt_ref[...]=dv_acc[...].astype(bf16); drt_ref[...]=dr_acc[...].astype(bf16)
    sums_ref[0:1,:]=su; sums_ref[1:2,:]=sv

def attn_bwd(qu,qv,k,v,r,p,g):
    seg,width=qu.shape; total=k.shape[0]; heads=width//DH
    col=lambda n: pl.BlockSpec((n,DH),lambda h:(0,h))
    row=lambda n: pl.BlockSpec((DH,n),lambda h:(h,0))
    return pl.pallas_call(attn_bwd_kernel,grid=(heads,),
        in_specs=[col(seg),col(seg),row(seg),row(seg),col(total),col(total),col(total),pl.BlockSpec((1,seg,total),lambda h:(h,0,0)),col(seg),row(seg)],
        out_specs=[col(seg),row(total),row(total),row(total),pl.BlockSpec((8,DH),lambda h:(0,h))],
        out_shape=[jax.ShapeDtypeStruct((seg,width),bf16)]+[jax.ShapeDtypeStruct((width,total),bf16)]*3+[jax.ShapeDtypeStruct((8,width),f32)],
        scratch_shapes=[pltpu.VMEM((DH,total),f32)]*3,
        cost_estimate=pl.CostEstimate(flops=16*seg*total*width,bytes_accessed=2*(5*seg*width+6*total*width+heads*seg*total),transcendentals=0),
        compiler_params=pltpu.CompilerParams(vmem_limit_bytes=40<<20),name="attn_bwd")(qu,qv,qu.T,qv.T,k,v,r,p,g,g.T)


def per_device(
    tokens,
    memory,
    compressed,
    mem_fill,
    cmem_fill,
    pad_mask,
    first_gain,
    first_shift,
    query_weight,
    key_weight,
    value_weight,
    position_weight,
    content_bias,
    position_bias,
    output_weight,
    second_gain,
    second_shift,
    inner_weight,
    inner_bias,
    outer_weight,
    outer_bias,
    conv_weight,
    conv_bias,
    out_grad,
    comp_grad,
):
    f32 = jnp.float32
    bf16 = jnp.bfloat16
    streams, seg_rows, width = tokens.shape
    mem_rows = memory.shape[1]
    cmem_rows = compressed.shape[1]
    total = cmem_rows + mem_rows + seg_rows
    scale = 1.0 / math.sqrt(DH)
    share = 1.0 / (streams * lax.axis_size("dp") * lax.axis_size("fsdp"))
    (
        full_first_gain,
        full_first_shift,
        full_query,
        full_keys,
        full_values,
        full_position,
        full_content,
        full_posbias,
        full_output,
    ) = (
        lax.all_gather(first_gain, "fsdp", axis=0, tiled=True),
        lax.all_gather(first_shift, "fsdp", axis=0, tiled=True),
        lax.all_gather(query_weight, "fsdp", axis=0, tiled=True),
        lax.all_gather(key_weight, "fsdp", axis=0, tiled=True),
        lax.all_gather(value_weight, "fsdp", axis=0, tiled=True),
        lax.all_gather(position_weight, "fsdp", axis=0, tiled=True),
        lax.all_gather(content_bias, "fsdp", axis=0, tiled=True),
        lax.all_gather(position_bias, "fsdp", axis=0, tiled=True),
        lax.all_gather(output_weight, "fsdp", axis=0, tiled=True),
    )
    whole = jnp.concatenate([compressed, memory, tokens], axis=1).astype(f32)
    normed, scaled_one, spread_one = norm_parts(whole, full_first_gain, full_first_shift)
    normed_low = normed.astype(bf16)
    own_rows = normed_low[:, total - seg_rows :]
    query = jnp.einsum("bsd,de->bse", own_rows, full_query, preferred_element_type=f32)
    query_u = (query + full_content.astype(f32)).astype(bf16)
    query_v = (query + full_posbias.astype(f32)).astype(bf16)
    keys = jnp.einsum("bsd,de->bse", normed_low, full_keys, preferred_element_type=f32).astype(bf16)
    values = jnp.einsum("bsd,de->bse", normed_low, full_values, preferred_element_type=f32).astype(
        bf16
    )
    pos_low = positions(total, width).astype(bf16)
    relative = jnp.dot(pos_low, full_position, preferred_element_type=f32).astype(bf16)

    valid = jnp.concatenate(
        [
            jnp.arange(cmem_rows, dtype=jnp.int32) >= cmem_rows - cmem_fill[0],
            jnp.arange(mem_rows, dtype=jnp.int32) >= mem_rows - mem_fill[0],
            pad_mask[0] == 1,
        ]
    )
    bias = jnp.where(valid, 0.0, NEG).astype(f32)[None]
    mixed_one, prob_low = attn_fwd(query_u[0], query_v[0], keys[0], values[0], relative, bias)
    mixed_low = mixed_one[None]
    attended = jnp.einsum("bsd,de->bse", mixed_low, full_output, preferred_element_type=f32)
    hidden = tokens.astype(f32) + attended
    (
        full_second_gain,
        full_second_shift,
        full_inner,
        full_inner_bias,
        full_outer,
        full_outer_bias,
        full_conv,
        full_conv_bias,
    ) = (
        lax.all_gather(second_gain, "fsdp", axis=0, tiled=True),
        lax.all_gather(second_shift, "fsdp", axis=0, tiled=True),
        lax.all_gather(inner_weight, "fsdp", axis=0, tiled=True),
        lax.all_gather(inner_bias, "fsdp", axis=0, tiled=True),
        lax.all_gather(outer_weight, "fsdp", axis=0, tiled=True),
        lax.all_gather(outer_bias, "fsdp", axis=0, tiled=True),
        lax.all_gather(conv_weight, "fsdp", axis=0, tiled=True),
        lax.all_gather(conv_bias, "fsdp", axis=0, tiled=True),
    )
    inner_norm, scaled_two, spread_two = norm_parts(hidden, full_second_gain, full_second_shift)
    inner_low = inner_norm.astype(bf16)
    preact = jnp.einsum(
        "bsd,df->bsf", inner_low, full_inner, preferred_element_type=f32
    ) + full_inner_bias.astype(f32)
    active = smooth_gate(preact).astype(bf16)
    result = (
        hidden
        + jnp.einsum("bsf,fd->bsd", active, full_outer, preferred_element_type=f32)
        + full_outer_bias.astype(f32)
    )
    groups = mem_rows // RATE
    start = mem_rows - RATE * groups
    mem_valid = (
        jnp.arange(mem_rows, dtype=jnp.int32)[None, :] >= (mem_rows - mem_fill)[:, None]
    ).astype(bf16)
    taps = (memory * mem_valid[..., None])[:, start:, :].reshape(streams, groups, RATE * width)
    group_valid = (start + RATE * jnp.arange(groups, dtype=jnp.int32) + RATE - 1)[None, :] >= (
        mem_rows - mem_fill
    )[:, None]
    made = (
        jnp.einsum("bnk,kd->bnd", taps, full_conv, preferred_element_type=f32)
        + full_conv_bias.astype(f32)
    ) * group_valid[..., None].astype(f32)
    back_second_gain, back_inner, back_outer = (
        lax.all_gather(second_gain, "fsdp", axis=0, tiled=True),
        lax.all_gather(inner_weight, "fsdp", axis=0, tiled=True),
        lax.all_gather(outer_weight, "fsdp", axis=0, tiled=True),
    )
    grad_wide = out_grad.astype(f32)
    outer_grad = jnp.einsum("bsf,bsd->fd", active, out_grad, preferred_element_type=f32)
    outer_bias_grad = jnp.sum(grad_wide, axis=(0, 1))
    active_grad = jnp.einsum("bsd,fd->bsf", out_grad, back_outer, preferred_element_type=f32)
    gate_pull = jax.vjp(smooth_gate, preact)[1]
    preact_grad = gate_pull(active_grad)[0].astype(bf16)
    inner_grad = jnp.einsum("bsd,bsf->df", inner_low, preact_grad, preferred_element_type=f32)
    inner_bias_grad = jnp.sum(preact_grad.astype(f32), axis=(0, 1))
    inner_norm_grad = jnp.einsum("bsf,df->bsd", preact_grad, back_inner, preferred_element_type=f32)
    second_gain_grad = jnp.sum(inner_norm_grad * scaled_two, axis=(0, 1))
    second_shift_grad = jnp.sum(inner_norm_grad, axis=(0, 1))
    hidden_grad = grad_wide + norm_back(inner_norm_grad, scaled_two, spread_two, back_second_gain)
    made_grad = comp_grad * group_valid[..., None].astype(bf16)
    conv_grad = jnp.einsum("bnk,bnd->kd", taps, made_grad, preferred_element_type=f32)
    conv_bias_grad = jnp.sum(made_grad.astype(f32), axis=(0, 1))
    ffn_parts = (
        lax.psum_scatter(
            second_gain_grad.astype(jnp.bfloat16), "fsdp", scatter_dimension=0, tiled=True
        ).astype(jnp.float32),
        lax.psum_scatter(
            second_shift_grad.astype(jnp.bfloat16), "fsdp", scatter_dimension=0, tiled=True
        ).astype(jnp.float32),
        lax.psum_scatter(
            inner_grad.astype(jnp.bfloat16), "fsdp", scatter_dimension=0, tiled=True
        ).astype(jnp.float32),
        lax.psum_scatter(
            inner_bias_grad.astype(jnp.bfloat16), "fsdp", scatter_dimension=0, tiled=True
        ).astype(jnp.float32),
        lax.psum_scatter(
            outer_grad.astype(jnp.bfloat16), "fsdp", scatter_dimension=0, tiled=True
        ).astype(jnp.float32),
        lax.psum_scatter(
            outer_bias_grad.astype(jnp.bfloat16), "fsdp", scatter_dimension=0, tiled=True
        ).astype(jnp.float32),
        lax.psum_scatter(
            conv_grad.astype(jnp.bfloat16), "fsdp", scatter_dimension=0, tiled=True
        ).astype(jnp.float32),
        lax.psum_scatter(
            conv_bias_grad.astype(jnp.bfloat16), "fsdp", scatter_dimension=0, tiled=True
        ).astype(jnp.float32),
    )
    ffn_done = (
        lax.psum(ffn_parts[0].astype(jnp.bfloat16), "dp").astype(jnp.float32),
        lax.psum(ffn_parts[1].astype(jnp.bfloat16), "dp").astype(jnp.float32),
        lax.psum(ffn_parts[2].astype(jnp.bfloat16), "dp").astype(jnp.float32),
        lax.psum(ffn_parts[3].astype(jnp.bfloat16), "dp").astype(jnp.float32),
        lax.psum(ffn_parts[4].astype(jnp.bfloat16), "dp").astype(jnp.float32),
        lax.psum(ffn_parts[5].astype(jnp.bfloat16), "dp").astype(jnp.float32),
        lax.psum(ffn_parts[6].astype(jnp.bfloat16), "dp").astype(jnp.float32),
        lax.psum(ffn_parts[7].astype(jnp.bfloat16), "dp").astype(jnp.float32),
    )
    back_first_gain, back_query, back_keys, back_values, back_output = (
        lax.all_gather(first_gain, "fsdp", axis=0, tiled=True),
        lax.all_gather(query_weight, "fsdp", axis=0, tiled=True),
        lax.all_gather(key_weight, "fsdp", axis=0, tiled=True),
        lax.all_gather(value_weight, "fsdp", axis=0, tiled=True),
        lax.all_gather(output_weight, "fsdp", axis=0, tiled=True),
    )
    hidden_low = hidden_grad.astype(bf16)
    output_grad = jnp.einsum("bsd,bse->de", mixed_low, hidden_low, preferred_element_type=f32)
    mixed_grad = jnp.einsum(
        "bse,de->bsd", hidden_low, back_output, preferred_element_type=f32
    ).astype(bf16)

    query_low, keys_t, values_t, relative_t, sums = attn_bwd(
        query_u[0], query_v[0], keys[0], values[0], relative, prob_low, mixed_grad[0]
    )
    query_low_grad = query_low[None]
    keys_grad, values_grad = keys_t.T[None], values_t.T[None]
    content_grad, posbias_grad = sums[0], sums[1]
    position_grad = jnp.einsum("ld,el->de", pos_low, relative_t, preferred_element_type=f32)
    query_grad = jnp.einsum("bsd,bse->de", own_rows, query_low_grad, preferred_element_type=f32)
    key_grad = jnp.einsum("bsd,bse->de", normed_low, keys_grad, preferred_element_type=f32)
    value_grad = jnp.einsum("bsd,bse->de", normed_low, values_grad, preferred_element_type=f32)
    normed_grad = jnp.einsum("bse,de->bsd", keys_grad, back_keys, preferred_element_type=f32)
    normed_grad = normed_grad + jnp.einsum(
        "bse,de->bsd", values_grad, back_values, preferred_element_type=f32
    )
    own_grad = jnp.einsum("bse,de->bsd", query_low_grad, back_query, preferred_element_type=f32)
    normed_grad = normed_grad + jnp.pad(own_grad, ((0, 0), (total - seg_rows, 0), (0, 0)))
    first_gain_grad = jnp.sum(normed_grad * scaled_one, axis=(0, 1))
    first_shift_grad = jnp.sum(normed_grad, axis=(0, 1))
    whole_grad = norm_back(normed_grad, scaled_one, spread_one, back_first_gain)
    token_gradient = hidden_grad + whole_grad[:, total - seg_rows :]
    attn_parts = (
        lax.psum_scatter(
            first_gain_grad.astype(jnp.bfloat16), "fsdp", scatter_dimension=0, tiled=True
        ).astype(jnp.float32),
        lax.psum_scatter(
            first_shift_grad.astype(jnp.bfloat16), "fsdp", scatter_dimension=0, tiled=True
        ).astype(jnp.float32),
        lax.psum_scatter(
            query_grad.astype(jnp.bfloat16), "fsdp", scatter_dimension=0, tiled=True
        ).astype(jnp.float32),
        lax.psum_scatter(
            key_grad.astype(jnp.bfloat16), "fsdp", scatter_dimension=0, tiled=True
        ).astype(jnp.float32),
        lax.psum_scatter(
            value_grad.astype(jnp.bfloat16), "fsdp", scatter_dimension=0, tiled=True
        ).astype(jnp.float32),
        lax.psum_scatter(
            position_grad.astype(jnp.bfloat16), "fsdp", scatter_dimension=0, tiled=True
        ).astype(jnp.float32),
        lax.psum_scatter(
            content_grad.astype(jnp.bfloat16), "fsdp", scatter_dimension=0, tiled=True
        ).astype(jnp.float32),
        lax.psum_scatter(
            posbias_grad.astype(jnp.bfloat16), "fsdp", scatter_dimension=0, tiled=True
        ).astype(jnp.float32),
        lax.psum_scatter(
            output_grad.astype(jnp.bfloat16), "fsdp", scatter_dimension=0, tiled=True
        ).astype(jnp.float32),
    )
    attn_done = (
        lax.psum(attn_parts[0].astype(jnp.bfloat16), "dp").astype(jnp.float32),
        lax.psum(attn_parts[1].astype(jnp.bfloat16), "dp").astype(jnp.float32),
        lax.psum(attn_parts[2].astype(jnp.bfloat16), "dp").astype(jnp.float32),
        lax.psum(attn_parts[3].astype(jnp.bfloat16), "dp").astype(jnp.float32),
        lax.psum(attn_parts[4].astype(jnp.bfloat16), "dp").astype(jnp.float32),
        lax.psum(attn_parts[5].astype(jnp.bfloat16), "dp").astype(jnp.float32),
        lax.psum(attn_parts[6].astype(jnp.bfloat16), "dp").astype(jnp.float32),
        lax.psum(attn_parts[7].astype(jnp.bfloat16), "dp").astype(jnp.float32),
        lax.psum(attn_parts[8].astype(jnp.bfloat16), "dp").astype(jnp.float32),
    )
    attn_mean = tuple((item * share for item in attn_done))
    ffn_mean = tuple((item * share for item in ffn_done))
    return (
        result.astype(bf16),
        token_gradient,
        made.astype(bf16),
        attn_mean[0],
        attn_mean[1],
        attn_mean[2],
        attn_mean[3],
        attn_mean[4],
        attn_mean[5],
        attn_mean[6],
        attn_mean[7],
        attn_mean[8],
        ffn_mean[0],
        ffn_mean[1],
        ffn_mean[2],
        ffn_mean[3],
        ffn_mean[4],
        ffn_mean[5],
        ffn_mean[6],
        ffn_mean[7],
    )


def solution(mesh):
    in_specs = (
        P(("dp", "fsdp"), None, None),
        P(("dp", "fsdp"), None, None),
        P(("dp", "fsdp"), None, None),
        P(("dp", "fsdp")),
        P(("dp", "fsdp")),
        P(("dp", "fsdp"), None),
        P("fsdp"),
        P("fsdp"),
        P("fsdp", None),
        P("fsdp", None),
        P("fsdp", None),
        P("fsdp", None),
        P("fsdp"),
        P("fsdp"),
        P("fsdp", None),
        P("fsdp"),
        P("fsdp"),
        P("fsdp", None),
        P("fsdp"),
        P("fsdp", None),
        P("fsdp"),
        P("fsdp", None),
        P("fsdp"),
        P(("dp", "fsdp"), None, None),
        P(("dp", "fsdp"), None, None),
    )
    out_specs = (
        P(("dp", "fsdp"), None, None),
        P(("dp", "fsdp"), None, None),
        P(("dp", "fsdp"), None, None),
        P("fsdp"),
        P("fsdp"),
        P("fsdp", None),
        P("fsdp", None),
        P("fsdp", None),
        P("fsdp", None),
        P("fsdp"),
        P("fsdp"),
        P("fsdp", None),
        P("fsdp"),
        P("fsdp"),
        P("fsdp", None),
        P("fsdp"),
        P("fsdp", None),
        P("fsdp"),
        P("fsdp", None),
        P("fsdp"),
    )
    return jax.shard_map(
        per_device, mesh=mesh, in_specs=in_specs, out_specs=out_specs, check_vma=False
    )
```

```python
import functools
import math

import jax
import jax.numpy as jnp
from jax import lax
from jax.experimental import pallas as pl
from jax.experimental.pallas import tpu as pltpu
from jax.sharding import PartitionSpec as P

HEADS = 8
DH = 128
RATE = 3
BLK = 128
NEG = -1.2e10
f32 = jnp.float32
bf16 = jnp.bfloat16


EPSILON = 1e-05
MASKED = -1000000000.0


def smooth_gate(values):
    return jax.nn.gelu(values, approximate=True)


def norm_parts(rows, gain, shift):
    center = jnp.mean(rows, axis=-1, keepdims=True)
    centered = rows - center
    spread = lax.rsqrt(jnp.mean(centered * centered, axis=-1, keepdims=True) + EPSILON)
    scaled = centered * spread
    return (scaled * gain.astype(jnp.float32) + shift.astype(jnp.float32), scaled, spread)


def norm_back(grad, scaled, spread, gain):
    inner = grad * gain.astype(jnp.float32)
    return spread * (
        inner
        - jnp.mean(inner, axis=-1, keepdims=True)
        - scaled * jnp.mean(inner * scaled, axis=-1, keepdims=True)
    )


def positions(count, width):
    distance = (count - 1 - jnp.arange(count, dtype=jnp.int32)).astype(jnp.float32)
    rates = jnp.exp(
        jnp.arange(0, width, 2, dtype=jnp.int32).astype(jnp.float32) * (-math.log(10000.0) / width)
    )
    angle = distance[:, None] * rates[None, :]
    return jnp.concatenate([jnp.sin(angle), jnp.cos(angle)], axis=1)


def dot_nt(a,b): return lax.dot_general(a,b,(((1,),(1,)),((),())),preferred_element_type=f32)
def dot_nn(a,b): return lax.dot_general(a,b,(((1,),(0,)),((),())),preferred_element_type=f32)

def attn_fwd_kernel(qu_ref,qv_ref,k_ref,v_ref,r_ref,bias_ref,o_ref,p_ref):
    seg=qu_ref.shape[0]; total=k_ref.shape[0]; old=total-seg
    c=math.log2(math.e)/math.sqrt(DH)
    for ib in range(seg//BLK):
        rows=pl.ds(ib*BLK,BLK)
        L=old+(ib+1)*BLK
        qu=qu_ref[rows,:]; qv=qv_ref[rows,:]
        raw=dot_nt(qv,r_ref[pl.ds(total-L,L),:])
        z=dot_nt(qu,k_ref[pl.ds(0,L),:])+pltpu.roll(raw,L-(BLK-1),axis=1,stride=1,stride_axis=0)
        M=L-BLK
        za=z[:,:M]+bias_ref[:,:M]
        rr=lax.broadcasted_iota(jnp.int32,(BLK,BLK),0); cc=lax.broadcasted_iota(jnp.int32,(BLK,BLK),1)
        zb=z[:,M:]
        zb=jnp.where(cc==rr,zb,jnp.where(cc<rr,zb+bias_ref[:,pl.ds(M,BLK)],NEG))
        top=jnp.maximum(jnp.max(za,axis=1,keepdims=True),jnp.max(zb,axis=1,keepdims=True))
        ea=jnp.exp2((za-top)*c); eb=jnp.exp2((zb-top)*c)
        inv=1.0/(jnp.sum(ea,axis=1,keepdims=True)+jnp.sum(eb,axis=1,keepdims=True))
        pa=(ea*inv).astype(bf16); pb=(eb*inv).astype(bf16)
        p_ref[0,rows,pl.ds(0,M)]=pa
        p_ref[0,rows,pl.ds(M,BLK)]=pb
        o_ref[rows,:]=(dot_nn(pa,v_ref[pl.ds(0,M),:])+dot_nn(pb,v_ref[pl.ds(M,BLK),:])).astype(bf16)

def attn_fwd(qu,qv,k,v,r,bias,first,heads):
    seg,width=qu.shape[0],heads*DH; total=k.shape[0]
    col=lambda n: pl.BlockSpec((n,DH),lambda h:(0,h+first))
    out=lambda n: pl.BlockSpec((n,DH),lambda h:(0,h))
    return pl.pallas_call(attn_fwd_kernel,grid=(heads,),
        in_specs=[col(seg),col(seg),col(total),col(total),col(total),pl.BlockSpec((1,total),lambda h:(0,0))],
        out_specs=[out(seg),pl.BlockSpec((1,seg,total),lambda h:(h,0,0))],
        out_shape=[jax.ShapeDtypeStruct((seg,width),bf16),jax.ShapeDtypeStruct((heads,seg,total),bf16)],
        cost_estimate=pl.CostEstimate(flops=6*seg*total*width,bytes_accessed=2*(3*seg*width+3*total*width+heads*seg*total),transcendentals=heads*seg*total),
        compiler_params=pltpu.CompilerParams(vmem_limit_bytes=40<<20),name="attn_fwd")(qu,qv,k,v,r,bias)

def attn_bwd_kernel(qu_ref,qv_ref,qut_ref,qvrt_ref,k_ref,v_ref,r_ref,p_ref,g_ref,gt_ref,dq_ref,dkt_ref,dvt_ref,drt_ref,sums_ref,dk_acc,dv_acc,dr_acc):
    seg=g_ref.shape[0]; total=k_ref.shape[0]; old=total-seg
    scale=1.0/math.sqrt(DH)
    rr=lax.broadcasted_iota(jnp.int32,(BLK,BLK),0); cc=lax.broadcasted_iota(jnp.int32,(BLK,BLK),1)
    flip=(rr+cc==BLK-1).astype(bf16)
    su=jnp.zeros((1,DH),f32); sv=jnp.zeros((1,DH),f32)
    nb=seg//BLK
    for ib in range(nb-1,-1,-1):
        rows=pl.ds(ib*BLK,BLK)
        L=old+(ib+1)*BLK
        g=g_ref[rows,:]; gt=gt_ref[:,rows]; qut=qut_ref[:,rows]
        plow=p_ref[0,rows,pl.ds(0,L)]
        p=plow.astype(f32)
        dp=dot_nt(g,v_ref[pl.ds(0,L),:])
        d=jnp.sum(p*dp,axis=1,keepdims=True)
        dz=(p*(dp-d)*scale).astype(bf16)
        dvt=dot_nn(gt,plow)
        dkt=dot_nn(qut,dz)
        dqu=dot_nn(dz,k_ref[pl.ds(0,L),:])
        rev=dot_nn(flip,dz)
        raw=pltpu.roll(rev,0,axis=1,stride=1,stride_axis=0).astype(bf16)
        T=pl.ds(total-L,L)
        dqv_rev=dot_nn(raw,r_ref[T,:])
        qvr=dot_nt(qvrt_ref[:,rows],flip).astype(bf16)
        drt=dot_nn(qvr,raw)
        dqv=lax.dot_general(flip.astype(f32),dqv_rev,(((1,),(0,)),((),())),preferred_element_type=f32,precision=lax.Precision.HIGHEST)
        su+=jnp.sum(dqu,axis=0,keepdims=True); sv+=jnp.sum(dqv,axis=0,keepdims=True)
        dq_ref[rows,:]=(dqu+dqv).astype(bf16)
        J=pl.ds(0,L)
        if ib==nb-1:
            dv_acc[...]=dvt; dk_acc[...]=dkt; dr_acc[...]=drt
        else:
            dv_acc[:,J]+=dvt; dk_acc[:,J]+=dkt; dr_acc[:,T]+=drt
    dkt_ref[...]=dk_acc[...].astype(bf16); dvt_ref[...]=dv_acc[...].astype(bf16); drt_ref[...]=dr_acc[...].astype(bf16)
    sums_ref[0:1,:]=su; sums_ref[1:2,:]=sv

def attn_bwd(qu,qv,qut,qvt,k,v,r,p,g,gt,first,heads):
    seg,width=qu.shape[0],heads*DH; total=k.shape[0]
    col=lambda n: pl.BlockSpec((n,DH),lambda h:(0,h+first))
    row=lambda n: pl.BlockSpec((DH,n),lambda h:(h+first,0))
    out=lambda n: pl.BlockSpec((n,DH),lambda h:(0,h))
    rowout=lambda n: pl.BlockSpec((DH,n),lambda h:(h,0))
    return pl.pallas_call(attn_bwd_kernel,grid=(heads,),
        in_specs=[col(seg),col(seg),row(seg),row(seg),col(total),col(total),col(total),pl.BlockSpec((1,seg,total),lambda h:(h,0,0)),col(seg),row(seg)],
        out_specs=[out(seg),rowout(total),rowout(total),rowout(total),pl.BlockSpec((8,DH),lambda h:(0,h))],
        out_shape=[jax.ShapeDtypeStruct((seg,width),bf16)]+[jax.ShapeDtypeStruct((width,total),bf16)]*3+[jax.ShapeDtypeStruct((8,width),f32)],
        scratch_shapes=[pltpu.VMEM((DH,total),f32)]*3,
        cost_estimate=pl.CostEstimate(flops=16*seg*total*width,bytes_accessed=2*(5*seg*width+6*total*width+heads*seg*total),transcendentals=0),
        compiler_params=pltpu.CompilerParams(vmem_limit_bytes=40<<20),name="attn_bwd")(qu,qv,qut,qvt,k,v,r,p,g,gt)


def hop(value, move):
    dp, fsdp = lax.axis_size("dp"), lax.axis_size("fsdp")
    pairs = []
    for z in range(dp):
        for f in range(fsdp):
            to = move(z, f)
            if to is not None:
                pairs.append((z * fsdp + f, to[0] * fsdp + to[1]))
    return lax.ppermute(value, ("dp", "fsdp"), pairs)


def assemble_kernel(count, places, index_ref, *refs):
    parts = len(places)
    slots, outs = refs[:count], refs[count : count + parts]
    whole, arrive, leave = refs[count + parts : -2], refs[-2], refs[-1]
    coming, going = [], []
    for s in range(count):
        for p, (start, rows) in enumerate(places):
            at = pl.ds(pl.multiple_of(index_ref[s] * rows, 16), rows)
            n = s * parts + p
            coming.append(
                pltpu.make_async_copy(
                    slots[s].at[pl.ds(start, rows), :], whole[p].at[at, :], arrive.at[n]
                )
            )
            going.append(
                pltpu.make_async_copy(whole[p].at[at, :], outs[p].at[at, :], leave.at[n])
            )
    for copy in coming:
        copy.start()
    for copy, onward in zip(coming, going):
        copy.wait()
        onward.start()
    for onward in going:
        onward.wait()


def assemble(slots, index, heights):
    count, cols, dtype = len(slots), slots[0].shape[1], slots[0].dtype
    places, start = [], 0
    for rows in heights:
        places.append((start, rows))
        start += rows
    moved = 2 * count * start * cols * 2
    return pl.pallas_call(
        functools.partial(assemble_kernel, count, tuple(places)),
        grid_spec=pltpu.PrefetchScalarGridSpec(
            num_scalar_prefetch=1,
            grid=(1,),
            in_specs=[pl.BlockSpec(memory_space=pl.ANY)] * count,
            out_specs=[pl.BlockSpec(memory_space=pl.ANY)] * len(heights),
            scratch_shapes=[pltpu.VMEM((count * rows, cols), dtype) for rows in heights]
            + [pltpu.SemaphoreType.DMA((count * len(heights),))] * 2,
        ),
        out_shape=[jax.ShapeDtypeStruct((count * rows, cols), dtype) for rows in heights],
        cost_estimate=pl.CostEstimate(flops=0, bytes_accessed=moved, transcendentals=0),
        compiler_params=pltpu.CompilerParams(vmem_limit_bytes=16 << 20),
        name="assemble",
    )(index, *slots)


def cut(*values):
    return lax.optimization_barrier(values)


def first_hop(w):
    return hop(w, lambda z, f: (z, f ^ (4 if z % 2 else 2)))


def second_hop(w):
    return hop(w, lambda z, f: (z, f ^ (2 if z % 2 else 4)))


def plane_hop(w):
    return hop(w, lambda z, f: (z ^ 1, f))


def core_hop(w):
    return hop(w, lambda z, f: (z, f ^ 1))


def x_hop(w):
    return hop(w, lambda z, f: (z, f ^ 2))


def y_hop(w):
    return hop(w, lambda z, f: (z, f ^ 4))


def inward_hop(w):
    to = {0: 1, 3: 2}
    return hop(w, lambda z, f: (to[z], f) if z in to else None)


def middle_hop(w):
    return hop(w, lambda z, f: (3 - z, f) if z in (1, 2) else None)


def outward_hop(w):
    to = {1: 0, 2: 3}
    return hop(w, lambda z, f: (to[z], f) if z in to else None)


def slot_index():
    odd = lax.axis_index("dp") % 2
    near = 2 + 2 * odd
    masks = jnp.stack([0 * odd, near, 6 - near, 0 * odd + 6])
    return (lax.axis_index("fsdp") ^ jnp.concatenate([masks, masks ^ 1])).astype(jnp.int32)


def gather(shards):
    return [lax.all_gather(w, "fsdp", axis=0, tiled=True) for w in shards]


def reduce(grads, share):
    done = []
    for g in grads:
        part = lax.psum_scatter(g, "fsdp", scatter_dimension=0, tiled=True)
        done.append(lax.psum(part, "dp").astype(f32) * share)
    return done


def add_rows(out, parts, scale=None):
    rows = out.shape[0]
    height = 32 if rows % 32 == 0 else 16

    def one(i, carry):
        at = pl.ds(pl.multiple_of(i * height, height), height)
        total = parts[0][at, :].astype(f32)
        for part in parts[1:]:
            total = total + part[at, :].astype(f32)
        if scale is not None:
            total = total * scale
        out[at, :] = total.astype(out.dtype)
        return carry

    lax.fori_loop(0, rows // height, one, 0)


FULL_BUFFERS = ("mine", "theirs", "far", "half_x", "half_y", "to_y", "to_x", "got_y", "got_x")
LINE_BUFFERS = ("own", "end", "pair", "mid", "whole", "last", "out")


def tail_scratch(plan):
    shapes = []
    for full, rows, cols in plan:
        line = [pltpu.VMEM((rows, cols), bf16)] * 6 + [pltpu.VMEM((rows, cols), f32)]
        if full:
            half = pltpu.VMEM((rows // 2, cols), bf16)
            one = pltpu.VMEM((rows, cols), bf16)
            shapes += [pltpu.VMEM((4, rows, cols), bf16)] * 2 + [one, half, half] + [one] * 4
        shapes += line
        shapes += [pltpu.SemaphoreType.DMA((n,)) for n in (4, 11, 11, 1)]
    return shapes


def tail_kernel(plan, sources, share, count, *refs):
    grads, outs, scratch = refs[:count], refs[count : 2 * count], refs[2 * count :]
    z, f = lax.axis_index("dp"), lax.axis_index("fsdp")
    chip, core = f // 2, f % 2
    middle = (z == 1) | (z == 2)
    edge = jnp.logical_not(middle)
    inward = jnp.where(z < 2, 1, 2)
    outward = jnp.where(z < 2, 0, 3)
    mesh = pl.DeviceIdType.MESH
    sibling, by_x, by_y = (z, f ^ 1), (z, f ^ 2), (z, f ^ 4)
    items, at = [], 0
    for n, (full, rows, cols) in enumerate(plan):
        names = (FULL_BUFFERS if full else ()) + LINE_BUFFERS + ("local", "sent", "came", "stored")
        b = dict(zip(names, scratch[at : at + len(names)]))
        at += len(names)
        b.update(full=full, rows=rows, source=grads[sources[n][0]], first=sources[n][1])
        b.update(target=outs[sources[n][0]])
        items.append(b)

    def copy(b, n, src, dst, device):
        return pltpu.make_async_remote_copy(
            src_ref=src,
            dst_ref=dst,
            send_sem=b["sent"].at[n],
            recv_sem=b["came"].at[n],
            device_id=device,
            device_id_type=mesh,
        )

    def rows_of(b):
        return pl.ds(b["first"], b["rows"])

    def across_cores(b, s):
        block = (chip ^ (3 - s)) * 2 + 1 - core
        return copy(b, s, b["source"].at[block, rows_of(b), :], b["theirs"].at[s], sibling)

    def load(b, s):
        if not b["full"]:
            src, dst = b["source"].at[rows_of(b), :], b["own"]
        else:
            block = (chip ^ (3 - s)) * 2 + core
            src, dst = b["source"].at[block, rows_of(b), :], b["mine"].at[s]
        return pltpu.make_async_copy(src, dst, b["local"].at[s])

    def halves_out(b):
        half = b["rows"] // 2
        return (
            copy(b, 4, b["far"].at[pl.ds(0, half), :], b["half_x"], by_x),
            copy(b, 5, b["far"].at[pl.ds(half, half), :], b["half_y"], by_y),
        )

    def near_out(b):
        return copy(b, 6, b["to_y"], b["got_y"], by_y), copy(b, 7, b["to_x"], b["got_x"], by_x)

    def go_in(b):
        return copy(b, 8, b["own"], b["end"], (inward, f))

    def go_mid(b):
        return copy(b, 9, b["pair"], b["mid"], (3 - z, f))

    def go_out(b):
        return copy(b, 10, b["whole"], b["last"], (outward, f))

    def store(b):
        return pltpu.make_async_copy(b["out"], b["target"].at[rows_of(b), :], b["stored"].at[0])

    def begin(b):
        if b["full"]:
            for s in range(4):
                across_cores(b, s).start()
                load(b, s).start()
        else:
            load(b, 0).start()

    def arrived(b, s):
        across_cores(b, s).wait_recv()
        load(b, s).wait()

    def far_phase(b):
        arrived(b, 0)
        add_rows(b["far"], [b["mine"].at[0], b["theirs"].at[0]])
        for c in halves_out(b):
            c.start()

    def near_phase(b):
        half = b["rows"] // 2
        low, high = pl.ds(0, half), pl.ds(half, half)
        arrived(b, 1)
        arrived(b, 2)
        x_half, y_half = halves_out(b)
        x_half.wait_recv()
        y_half.wait_recv()
        mine, theirs = b["mine"], b["theirs"]
        add_rows(b["to_y"].at[low, :], [mine.at[1, low, :], theirs.at[1, low, :], b["half_x"]])
        add_rows(b["to_y"].at[high, :], [mine.at[1, high, :], theirs.at[1, high, :]])
        add_rows(b["to_x"].at[low, :], [mine.at[2, low, :], theirs.at[2, low, :]])
        add_rows(b["to_x"].at[high, :], [mine.at[2, high, :], theirs.at[2, high, :], b["half_y"]])
        for c in near_out(b):
            c.start()

    def own_phase(b):
        arrived(b, 3)
        for c in near_out(b):
            c.wait_recv()
        add_rows(b["own"], [b["mine"].at[3], b["theirs"].at[3], b["got_x"], b["got_y"]])

    def line_in(b):
        if not b["full"]:
            load(b, 0).wait()

        @pl.when(edge)
        def _():
            go_in(b).start()

    def line_mid(b):
        @pl.when(middle)
        def _():
            go_in(b).wait_recv()
            add_rows(b["pair"], [b["own"], b["end"]])
            go_mid(b).start()

    def line_out(b):
        @pl.when(middle)
        def _():
            go_mid(b).wait_recv()
            add_rows(b["whole"], [b["pair"], b["mid"]])
            go_out(b).start()
            add_rows(b["out"], [b["whole"]], share)
            store(b).start()

    def line_last(b):
        @pl.when(edge)
        def _():
            go_out(b).wait_recv()
            add_rows(b["out"], [b["last"]], share)
            store(b).start()

    barrier = pltpu.get_barrier_semaphore()
    for device in (sibling, by_x, by_y):
        pl.semaphore_signal(barrier, inc=1, device_id=device, device_id_type=mesh)

    @pl.when(middle)
    def _():
        pl.semaphore_signal(barrier, inc=1, device_id=(outward, f), device_id_type=mesh)
        pl.semaphore_signal(barrier, inc=1, device_id=(3 - z, f), device_id_type=mesh)
        pl.semaphore_wait(barrier, 5)

    @pl.when(edge)
    def _():
        pl.semaphore_signal(barrier, inc=1, device_id=(inward, f), device_id_type=mesh)
        pl.semaphore_wait(barrier, 4)

    wide = [b for b in items if b["full"]]
    queue = [b for b in items if not b["full"]]
    for b in queue:
        begin(b)
    ready = 2
    line = []
    slot = 0
    while sum(b is not None for b in line) < len(items):
        due = [b for n, b in enumerate(wide) if n + ready <= slot and not any(b is q for q in line)]
        left = [b for b in queue if not any(b is q for q in line)]
        if left and (not due or slot % 2 == 0):
            line.append(left[0])
        elif due:
            line.append(due[0])
        else:
            line.append(None)
        slot += 1
    for b in wide[:2]:
        begin(b)
    for t in range(len(line) + 3):
        if t + 2 < len(wide):
            begin(wide[t + 2])
        if t < len(wide):
            far_phase(wide[t])
        if 0 <= t - 1 < len(wide):
            near_phase(wide[t - 1])
        if 0 <= t - 2 < len(wide):
            own_phase(wide[t - 2])
        for phase, back in ((line_in, 0), (line_mid, 1), (line_out, 2), (line_last, 3)):
            if 0 <= t - back < len(line) and line[t - back] is not None:
                phase(line[t - back])
    for b in items:
        if b["full"]:
            for s in range(4):
                across_cores(b, s).wait_send()
            for c in halves_out(b) + near_out(b):
                c.wait_send()
        store(b).wait()

    @pl.when(edge)
    def _():
        for b in items:
            go_in(b).wait_send()

    @pl.when(middle)
    def _():
        for b in items:
            go_mid(b).wait_send()
            go_out(b).wait_send()


def reduce_tail(fulls, shards, share, number):
    plan, sources, arrays, shapes = [], [], [], []
    for full, group in ((True, fulls), (False, shards)):
        for g, pieces in group:
            rows, cols = g.shape[0] // (8 if full else 1), g.shape[1]
            for p in range(pieces):
                plan.append((full, rows // pieces, cols))
                sources.append((len(arrays), p * (rows // pieces)))
            arrays.append(g.reshape(8, rows, cols) if full else g)
            shapes.append(jax.ShapeDtypeStruct((rows, cols), f32))
    return pl.pallas_call(
        functools.partial(tail_kernel, tuple(plan), tuple(sources), share, len(arrays)),
        in_specs=[pl.BlockSpec(memory_space=pl.ANY)] * len(arrays),
        out_specs=[pl.BlockSpec(memory_space=pl.ANY)] * len(arrays),
        out_shape=shapes,
        scratch_shapes=tail_scratch(plan),
        compiler_params=pltpu.CompilerParams(
            collective_id=number, has_side_effects=True, vmem_limit_bytes=56 << 20
        ),
        name="reduce_tail",
    )(*arrays)


def pack_vectors(vectors, parts):
    flat = jnp.concatenate([v.reshape(parts, -1) for v in vectors], axis=1)
    width = 1024
    lines = 32 * (-(-flat.shape[1] // (32 * width)))
    flat = jnp.pad(flat, ((0, 0), (0, lines * width - flat.shape[1])))
    return flat.reshape(parts * lines, width)


def unpack_vectors(table, parts, sizes):
    flat = table.reshape(parts, -1)
    result, start = [], 0
    for size in sizes:
        result.append(flat[:, start : start + size].reshape(parts * size))
        start += size
    return result


def per_device_plain(
    tokens,
    memory,
    compressed,
    mem_fill,
    cmem_fill,
    pad_mask,
    first_gain,
    first_shift,
    query_weight,
    key_weight,
    value_weight,
    position_weight,
    content_bias,
    position_bias,
    output_weight,
    second_gain,
    second_shift,
    inner_weight,
    inner_bias,
    outer_weight,
    outer_bias,
    conv_weight,
    conv_bias,
    out_grad,
    comp_grad,
):
    streams, seg_rows, width = tokens.shape
    mem_rows = memory.shape[1]
    cmem_rows = compressed.shape[1]
    total = cmem_rows + mem_rows + seg_rows
    shards = lax.axis_size("fsdp")
    share = 1.0 / (streams * lax.axis_size("dp") * shards)
    vectors = (
        first_gain,
        first_shift,
        content_bias,
        position_bias,
        second_gain,
        second_shift,
        inner_bias,
        outer_bias,
        conv_bias,
    )
    sizes = [v.shape[0] for v in vectors]

    groups = mem_rows // RATE
    start = mem_rows - RATE * groups
    mem_valid = (
        jnp.arange(mem_rows, dtype=jnp.int32)[None, :] >= (mem_rows - mem_fill)[:, None]
    ).astype(bf16)
    taps = (memory * mem_valid[..., None])[:, start:, :].reshape(streams * groups, RATE * width)
    group_valid = (
        (start + RATE * jnp.arange(groups, dtype=jnp.int32) + RATE - 1)[None, :]
        >= (mem_rows - mem_fill)[:, None]
    ).reshape(streams * groups, 1)
    made_grad = comp_grad.reshape(streams * groups, width) * group_valid.astype(bf16)
    conv_grad = jnp.einsum("nk,nd->kd", taps, made_grad, preferred_element_type=f32).astype(bf16)
    conv_bias_grad = jnp.sum(made_grad.astype(f32), axis=0)

    query_w, key_w, value_w, table = gather(
        [query_weight, key_weight, value_weight, pack_vectors(vectors, 1)]
    )
    (gain_one, shift_one, content_b, position_b, gain_two, shift_two, inner_b, outer_b, conv_b) = (
        unpack_vectors(table, shards, sizes)
    )
    position_w, output_w = gather([position_weight, output_weight])
    (inner_w,) = gather([inner_weight])
    (outer_w,) = gather([outer_weight])
    (conv_w,) = gather([conv_weight])

    whole = jnp.concatenate([compressed[0], memory[0], tokens[0]], axis=0).astype(f32)
    normed, scaled_one, spread_one = norm_parts(whole, gain_one, shift_one)
    normed_low = normed.astype(bf16)
    own_rows = normed_low[total - seg_rows :]
    query = jnp.dot(own_rows, query_w, preferred_element_type=f32)
    query_u = (query + content_b.astype(f32)).astype(bf16)
    query_v = (query + position_b.astype(f32)).astype(bf16)
    keys = jnp.dot(normed_low, key_w, preferred_element_type=f32).astype(bf16)
    values = jnp.dot(normed_low, value_w, preferred_element_type=f32).astype(bf16)
    pos_low = positions(total, width).astype(bf16)
    relative = jnp.dot(pos_low, position_w, preferred_element_type=f32).astype(bf16)
    valid = jnp.concatenate(
        [
            jnp.arange(cmem_rows, dtype=jnp.int32) >= cmem_rows - cmem_fill[0],
            jnp.arange(mem_rows, dtype=jnp.int32) >= mem_rows - mem_fill[0],
            pad_mask[0] == 1,
        ]
    )
    bias = jnp.where(valid, 0.0, NEG).astype(f32)[None]
    mixed, prob_low = attn_fwd(query_u, query_v, keys, values, relative, bias, 0, HEADS)
    hidden = tokens[0].astype(f32) + jnp.dot(mixed, output_w, preferred_element_type=f32)
    inner_norm, scaled_two, spread_two = norm_parts(hidden, gain_two, shift_two)
    inner_low = inner_norm.astype(bf16)
    preact = jnp.dot(inner_low, inner_w, preferred_element_type=f32) + inner_b.astype(f32)
    active = smooth_gate(preact).astype(bf16)
    result = (
        hidden
        + jnp.dot(active, outer_w, preferred_element_type=f32)
        + outer_b.astype(f32)
    )
    made = (
        jnp.dot(taps, conv_w, preferred_element_type=f32) + conv_b.astype(f32)
    ) * group_valid.astype(f32)

    grad = out_grad[0]
    grad_wide = grad.astype(f32)
    outer_grad = jnp.einsum("sf,sd->fd", active, grad, preferred_element_type=f32).astype(bf16)
    (outer_mean,) = reduce([outer_grad], share)
    outer_bias_grad = jnp.sum(grad_wide, axis=0)
    active_grad = jnp.einsum("sd,fd->sf", grad, outer_w, preferred_element_type=f32)
    gate_pull = jax.vjp(smooth_gate, preact)[1]
    preact_grad = gate_pull(active_grad)[0].astype(bf16)
    inner_grad = jnp.einsum("sd,sf->df", inner_low, preact_grad, preferred_element_type=f32).astype(
        bf16
    )
    (inner_mean,) = reduce([inner_grad], share)
    (conv_mean,) = reduce([conv_grad], share)
    inner_bias_grad = jnp.sum(preact_grad.astype(f32), axis=0)
    inner_norm_grad = jnp.einsum("sf,df->sd", preact_grad, inner_w, preferred_element_type=f32)
    second_gain_grad = jnp.sum(inner_norm_grad * scaled_two, axis=0)
    second_shift_grad = jnp.sum(inner_norm_grad, axis=0)
    hidden_grad = grad_wide + norm_back(inner_norm_grad, scaled_two, spread_two, gain_two)

    hidden_low = hidden_grad.astype(bf16)
    output_grad = jnp.einsum("sd,se->de", mixed, hidden_low, preferred_element_type=f32).astype(bf16)
    mixed_grad = jnp.einsum("se,de->sd", hidden_low, output_w, preferred_element_type=f32).astype(
        bf16
    )
    query_low, keys_t, values_t, relative_t, sums = attn_bwd(
        query_u,
        query_v,
        query_u.T,
        query_v.T,
        keys,
        values,
        relative,
        prob_low,
        mixed_grad,
        mixed_grad.T,
        0,
        HEADS,
    )
    position_grad = jnp.einsum("ld,el->de", pos_low, relative_t, preferred_element_type=f32).astype(
        bf16
    )
    query_grad = jnp.einsum("sd,se->de", own_rows, query_low, preferred_element_type=f32).astype(
        bf16
    )
    key_grad = jnp.einsum("sd,es->de", normed_low, keys_t, preferred_element_type=f32).astype(bf16)
    value_grad = jnp.einsum("sd,es->de", normed_low, values_t, preferred_element_type=f32).astype(
        bf16
    )
    normed_grad = jnp.einsum("es,de->sd", keys_t, key_w, preferred_element_type=f32)
    normed_grad = normed_grad + jnp.einsum(
        "es,de->sd", values_t, value_w, preferred_element_type=f32
    )
    own_grad = jnp.einsum("se,de->sd", query_low, query_w, preferred_element_type=f32)
    normed_grad = normed_grad + jnp.pad(own_grad, ((total - seg_rows, 0), (0, 0)))
    first_gain_grad = jnp.sum(normed_grad * scaled_one, axis=0)
    first_shift_grad = jnp.sum(normed_grad, axis=0)
    own = slice(total - seg_rows, None)
    token_gradient = hidden_grad + norm_back(
        normed_grad[own], scaled_one[own], spread_one[own], gain_one
    )
    vector_grads = (
        first_gain_grad,
        first_shift_grad,
        sums[0],
        sums[1],
        second_gain_grad,
        second_shift_grad,
        inner_bias_grad,
        outer_bias_grad,
        conv_bias_grad,
    )
    packed = pack_vectors([v.astype(bf16) for v in vector_grads], shards)
    (output_mean,) = reduce([output_grad], share)
    query_mean, key_mean, value_mean, position_mean, table_mean = reduce(
        [query_grad, key_grad, value_grad, position_grad, packed], share
    )
    (
        first_gain_mean,
        first_shift_mean,
        content_mean,
        posbias_mean,
        second_gain_mean,
        second_shift_mean,
        inner_bias_mean,
        outer_bias_mean,
        conv_bias_mean,
    ) = unpack_vectors(table_mean, 1, sizes)
    return (
        result.astype(bf16)[None],
        token_gradient[None],
        made.astype(bf16)[None],
        first_gain_mean,
        first_shift_mean,
        query_mean,
        key_mean,
        value_mean,
        position_mean,
        content_mean,
        posbias_mean,
        output_mean,
        second_gain_mean,
        second_shift_mean,
        inner_mean,
        inner_bias_mean,
        outer_mean,
        outer_bias_mean,
        conv_mean,
        conv_bias_mean,
    )


def per_device_direct(
    tokens,
    memory,
    compressed,
    mem_fill,
    cmem_fill,
    pad_mask,
    first_gain,
    first_shift,
    query_weight,
    key_weight,
    value_weight,
    position_weight,
    content_bias,
    position_bias,
    output_weight,
    second_gain,
    second_shift,
    inner_weight,
    inner_bias,
    outer_weight,
    outer_bias,
    conv_weight,
    conv_bias,
    out_grad,
    comp_grad,
):
    streams, seg_rows, width = tokens.shape
    mem_rows = memory.shape[1]
    cmem_rows = compressed.shape[1]
    total = cmem_rows + mem_rows + seg_rows
    old = total - seg_rows
    shards = lax.axis_size("fsdp")
    share = 1.0 / (streams * lax.axis_size("dp") * shards)
    lower = HEADS // 2
    edge = lower * DH
    index = slot_index()
    vectors = (
        first_gain,
        first_shift,
        content_bias,
        position_bias,
        second_gain,
        second_shift,
        inner_bias,
        outer_bias,
        conv_bias,
    )
    sizes = [v.shape[0] for v in vectors]
    rows = query_weight.shape[0]
    pack_1 = jnp.concatenate([query_weight, key_weight, value_weight, pack_vectors(vectors, 1)], axis=0)
    pack_2 = jnp.concatenate([position_weight, output_weight], axis=0)

    first_1 = first_hop(pack_1)
    whole = jnp.concatenate([compressed[0], memory[0], tokens[0]], axis=0).astype(f32)
    center = jnp.mean(whole, axis=-1, keepdims=True)
    spread_one = lax.rsqrt(jnp.mean((whole - center) ** 2, axis=-1, keepdims=True) + EPSILON)
    scaled_one = (whole - center) * spread_one
    groups = mem_rows // RATE
    start = mem_rows - RATE * groups
    mem_valid = (jnp.arange(mem_rows, dtype=jnp.int32) >= mem_rows - mem_fill[0]).astype(bf16)
    taps = (memory[0] * mem_valid[:, None])[start:, :].reshape(groups, RATE * width)
    group_valid = (
        start + RATE * jnp.arange(groups, dtype=jnp.int32) + RATE - 1 >= mem_rows - mem_fill[0]
    )[:, None]
    made_grad = comp_grad[0] * group_valid.astype(bf16)
    conv_grad = jnp.einsum("nk,nd->kd", taps, made_grad, preferred_element_type=f32).astype(bf16)
    conv_bias_grad = jnp.sum(made_grad.astype(f32), axis=0)
    first_1, scaled_one, conv_grad, taps, pack_2, pack_1 = cut(
        first_1, scaled_one, conv_grad, taps, pack_2, pack_1
    )

    second_1, across_1 = second_hop(first_1), plane_hop(first_1)
    first_2 = first_hop(pack_2)
    core_1a, core_1b = core_hop(pack_1), core_hop(first_1)
    pos_low = positions(total, width).astype(bf16)
    second_1, across_1, first_2, core_1a, core_1b, pos_low, inner_weight = cut(
        second_1, across_1, first_2, core_1a, core_1b, pos_low, inner_weight
    )

    core_1c, core_1d = core_hop(across_1), core_hop(second_1)
    second_2, across_2 = second_hop(first_2), plane_hop(first_2)
    core_2a, core_2b = core_hop(pack_2), core_hop(first_2)
    first_3 = first_hop(inner_weight)
    query_w, key_w, value_w, table = assemble(
        [pack_1, first_1, across_1, second_1, core_1a, core_1b, core_1c, core_1d],
        index,
        [rows, rows, rows, pack_1.shape[0] - 3 * rows],
    )
    (gain_one, shift_one, content_b, position_b, gain_two, shift_two, inner_b, outer_b, conv_b) = (
        unpack_vectors(table, shards, sizes)
    )
    normed_low = (scaled_one * gain_one.astype(f32) + shift_one.astype(f32)).astype(bf16)
    own_rows = normed_low[old:]
    query = jnp.dot(own_rows, query_w, preferred_element_type=f32)
    query_u = (query + content_b.astype(f32)).astype(bf16)
    query_v = (query + position_b.astype(f32)).astype(bf16)
    keys = jnp.dot(normed_low, key_w, preferred_element_type=f32).astype(bf16)
    values = jnp.dot(normed_low, value_w, preferred_element_type=f32).astype(bf16)
    (second_2, across_2, core_2a, core_2b, first_3, query_u, query_v, keys, values, outer_weight) = cut(
        second_2, across_2, core_2a, core_2b, first_3, query_u, query_v, keys, values, outer_weight
    )

    core_2c, core_2d = core_hop(across_2), core_hop(second_2)
    second_3, across_3 = second_hop(first_3), plane_hop(first_3)
    core_3a, core_3b = core_hop(inner_weight), core_hop(first_3)
    first_4 = first_hop(outer_weight)
    position_w, output_w = assemble(
        [pack_2, first_2, across_2, second_2, core_2a, core_2b, core_2c, core_2d], index, [rows, rows]
    )
    relative = jnp.dot(pos_low, position_w, preferred_element_type=f32).astype(bf16)
    valid = jnp.concatenate(
        [
            jnp.arange(cmem_rows, dtype=jnp.int32) >= cmem_rows - cmem_fill[0],
            jnp.arange(mem_rows, dtype=jnp.int32) >= mem_rows - mem_fill[0],
            pad_mask[0] == 1,
        ]
    )
    bias = jnp.where(valid, 0.0, NEG).astype(f32)[None]
    mixed_a, prob_a = attn_fwd(query_u, query_v, keys, values, relative, bias, 0, lower)
    second_3, across_3, core_3a, core_3b, first_4, mixed_a, prob_a, conv_weight = cut(
        second_3, across_3, core_3a, core_3b, first_4, mixed_a, prob_a, conv_weight
    )

    core_3c, core_3d = core_hop(across_3), core_hop(second_3)
    second_4, across_4 = second_hop(first_4), plane_hop(first_4)
    core_4a, core_4b = core_hop(outer_weight), core_hop(first_4)
    first_5 = first_hop(conv_weight)
    mixed_b, prob_b = attn_fwd(
        query_u, query_v, keys, values, relative, bias, lower, HEADS - lower
    )
    mixed = jnp.concatenate([mixed_a, mixed_b], axis=1)
    hidden = tokens[0].astype(f32) + jnp.dot(mixed, output_w, preferred_element_type=f32)
    inner_norm, scaled_two, spread_two = norm_parts(hidden, gain_two, shift_two)
    inner_low = inner_norm.astype(bf16)
    (second_4, across_4, core_4a, core_4b, first_5, core_3c, core_3d, inner_low, hidden, prob_b) = cut(
        second_4, across_4, core_4a, core_4b, first_5, core_3c, core_3d, inner_low, hidden, prob_b
    )

    core_4c, core_4d = core_hop(across_4), core_hop(second_4)
    second_5, across_5 = second_hop(first_5), plane_hop(first_5)
    core_5a, core_5b = core_hop(conv_weight), core_hop(first_5)
    (inner_w,) = assemble(
        [inner_weight, first_3, across_3, second_3, core_3a, core_3b, core_3c, core_3d], index, [rows]
    )
    preact = jnp.dot(inner_low, inner_w, preferred_element_type=f32) + inner_b.astype(f32)
    active = smooth_gate(preact).astype(bf16)
    (second_5, across_5, core_5a, core_5b, core_4c, core_4d, preact, active, conv_grad) = cut(
        second_5, across_5, core_5a, core_5b, core_4c, core_4d, preact, active, conv_grad
    )

    grad = out_grad[0]
    grad_wide = grad.astype(f32)
    core_5c, core_5d = core_hop(across_5), core_hop(second_5)
    conv_part = lax.psum_scatter(conv_grad, "fsdp", scatter_dimension=0, tiled=True)
    outer_grad = jnp.einsum("sf,sd->fd", active, grad, preferred_element_type=f32).astype(bf16)
    outer_bias_grad = jnp.sum(grad_wide, axis=0)
    core_5c, core_5d, outer_grad = cut(core_5c, core_5d, outer_grad)

    outer_part = lax.psum_scatter(outer_grad, "fsdp", scatter_dimension=0, tiled=True)
    (outer_w,) = assemble(
        [outer_weight, first_4, across_4, second_4, core_4a, core_4b, core_4c, core_4d],
        index,
        [outer_weight.shape[0]],
    )
    active_grad = jnp.einsum("sd,fd->sf", grad, outer_w, preferred_element_type=f32)
    gate_pull = jax.vjp(smooth_gate, preact)[1]
    preact_grad = gate_pull(active_grad)[0].astype(bf16)
    inner_bias_grad = jnp.sum(preact_grad.astype(f32), axis=0)
    inner_grad = jnp.einsum("sd,sf->df", inner_low, preact_grad, preferred_element_type=f32).astype(
        bf16
    )
    inner_grad, preact_grad = cut(inner_grad, preact_grad)

    inner_part = lax.psum_scatter(inner_grad, "fsdp", scatter_dimension=0, tiled=True)
    inner_norm_grad = jnp.einsum("sf,df->sd", preact_grad, inner_w, preferred_element_type=f32)
    second_gain_grad = jnp.sum(inner_norm_grad * scaled_two, axis=0)
    second_shift_grad = jnp.sum(inner_norm_grad, axis=0)
    hidden_grad = grad_wide + norm_back(inner_norm_grad, scaled_two, spread_two, gain_two)
    hidden_low = hidden_grad.astype(bf16)
    output_grad = jnp.einsum("sd,se->de", mixed, hidden_low, preferred_element_type=f32).astype(bf16)
    mixed_grad = jnp.einsum("se,de->sd", hidden_low, output_w, preferred_element_type=f32).astype(
        bf16
    )
    bwd = (query_u, query_v, query_u.T, query_v.T, keys, values, relative)
    query_a, keys_a, values_a, relative_a, sums_a = attn_bwd(
        *bwd, prob_a, mixed_grad, mixed_grad.T, 0, lower
    )
    query_b, keys_b, values_b, relative_b, sums_b = attn_bwd(
        *bwd, prob_b, mixed_grad, mixed_grad.T, lower, HEADS - lower
    )
    query_g = jnp.concatenate([query_a, query_b], axis=1)
    keys_g = jnp.concatenate([keys_a, keys_b], axis=0)
    values_g = jnp.concatenate([values_a, values_b], axis=0)
    relative_g = jnp.concatenate([relative_a, relative_b], axis=0)
    query_grad = jnp.einsum("sd,se->de", own_rows, query_g, preferred_element_type=f32).astype(bf16)
    key_grad = jnp.einsum("sd,es->de", normed_low, keys_g, preferred_element_type=f32).astype(bf16)
    value_grad = jnp.einsum("sd,es->de", normed_low, values_g, preferred_element_type=f32).astype(bf16)
    position_grad = jnp.einsum("ld,el->de", pos_low, relative_g, preferred_element_type=f32).astype(
        bf16
    )
    normed_grad = jnp.einsum("es,de->sd", keys_g, key_w, preferred_element_type=f32)
    normed_grad = normed_grad + jnp.einsum("es,de->sd", values_g, value_w, preferred_element_type=f32)
    own_grad = jnp.einsum("se,de->sd", query_g, query_w, preferred_element_type=f32)
    normed_grad = normed_grad + jnp.pad(own_grad, ((old, 0), (0, 0)))
    first_gain_grad = jnp.sum(normed_grad * scaled_one, axis=0)
    first_shift_grad = jnp.sum(normed_grad, axis=0)
    token_gradient = hidden_grad + norm_back(
        normed_grad[old:], scaled_one[old:], spread_one[old:], gain_one
    )
    vector_grads = (
        first_gain_grad,
        first_shift_grad,
        jnp.concatenate([sums_a[0], sums_b[0]]),
        jnp.concatenate([sums_a[1], sums_b[1]]),
        second_gain_grad,
        second_shift_grad,
        inner_bias_grad,
        outer_bias_grad,
        conv_bias_grad,
    )
    packed = pack_vectors([v.astype(bf16) for v in vector_grads], shards)
    result = (
        hidden + jnp.dot(active, outer_w, preferred_element_type=f32) + outer_b.astype(f32)
    ).astype(bf16)
    (conv_w,) = assemble(
        [conv_weight, first_5, across_5, second_5, core_5a, core_5b, core_5c, core_5d],
        index,
        [conv_weight.shape[0]],
    )
    made = (
        (jnp.dot(taps, conv_w, preferred_element_type=f32) + conv_b.astype(f32))
        * group_valid.astype(f32)
    ).astype(bf16)
    (
        query_mean,
        key_mean,
        value_mean,
        position_mean,
        output_mean,
        table_mean,
        conv_mean,
        outer_mean,
        inner_mean,
    ) = reduce_tail(
        [(g, 2) for g in (query_grad, key_grad, value_grad, position_grad, output_grad)]
        + [(packed, 1)],
        [(conv_part, 3), (outer_part, 4), (inner_part, 4)],
        share,
        1,
    )
    (
        first_gain_mean,
        first_shift_mean,
        content_mean,
        posbias_mean,
        second_gain_mean,
        second_shift_mean,
        inner_bias_mean,
        outer_bias_mean,
        conv_bias_mean,
    ) = unpack_vectors(table_mean, 1, sizes)
    return (
        result[None],
        token_gradient[None],
        made[None],
        first_gain_mean,
        first_shift_mean,
        query_mean,
        key_mean,
        value_mean,
        position_mean,
        content_mean,
        posbias_mean,
        output_mean,
        second_gain_mean,
        second_shift_mean,
        inner_mean,
        inner_bias_mean,
        outer_mean,
        outer_bias_mean,
        conv_mean,
        conv_bias_mean,
    )


def per_device(*arguments):
    if lax.axis_size("dp") == 4 and lax.axis_size("fsdp") == 8:
        return per_device_direct(*arguments)
    return per_device_plain(*arguments)


def solution(mesh):
    in_specs = (
        P(("dp", "fsdp"), None, None),
        P(("dp", "fsdp"), None, None),
        P(("dp", "fsdp"), None, None),
        P(("dp", "fsdp")),
        P(("dp", "fsdp")),
        P(("dp", "fsdp"), None),
        P("fsdp"),
        P("fsdp"),
        P("fsdp", None),
        P("fsdp", None),
        P("fsdp", None),
        P("fsdp", None),
        P("fsdp"),
        P("fsdp"),
        P("fsdp", None),
        P("fsdp"),
        P("fsdp"),
        P("fsdp", None),
        P("fsdp"),
        P("fsdp", None),
        P("fsdp"),
        P("fsdp", None),
        P("fsdp"),
        P(("dp", "fsdp"), None, None),
        P(("dp", "fsdp"), None, None),
    )
    out_specs = (
        P(("dp", "fsdp"), None, None),
        P(("dp", "fsdp"), None, None),
        P(("dp", "fsdp"), None, None),
        P("fsdp"),
        P("fsdp"),
        P("fsdp", None),
        P("fsdp", None),
        P("fsdp", None),
        P("fsdp", None),
        P("fsdp"),
        P("fsdp"),
        P("fsdp", None),
        P("fsdp"),
        P("fsdp"),
        P("fsdp", None),
        P("fsdp"),
        P("fsdp", None),
        P("fsdp"),
        P("fsdp", None),
        P("fsdp"),
    )
    return jax.shard_map(
        per_device, mesh=mesh, in_specs=in_specs, out_specs=out_specs, check_vma=False
    )
```

```python
import functools
import math

import jax
import jax.numpy as jnp
from jax import lax
from jax.experimental import pallas as pl
from jax.experimental.pallas import tpu as pltpu
from jax.sharding import PartitionSpec as P

HEADS = 8
DH = 128
RATE = 3
BLK = 128
NEG = -1.2e10
f32 = jnp.float32
bf16 = jnp.bfloat16


EPSILON = 1e-05
MASKED = -1000000000.0


def smooth_gate(values):
    return jax.nn.gelu(values, approximate=True)


def norm_parts(rows, gain, shift):
    center = jnp.mean(rows, axis=-1, keepdims=True)
    centered = rows - center
    spread = lax.rsqrt(jnp.mean(centered * centered, axis=-1, keepdims=True) + EPSILON)
    scaled = centered * spread
    return (scaled * gain.astype(jnp.float32) + shift.astype(jnp.float32), scaled, spread)


def norm_back(grad, scaled, spread, gain):
    inner = grad * gain.astype(jnp.float32)
    return spread * (
        inner
        - jnp.mean(inner, axis=-1, keepdims=True)
        - scaled * jnp.mean(inner * scaled, axis=-1, keepdims=True)
    )


def positions(count, width):
    distance = (count - 1 - jnp.arange(count, dtype=jnp.int32)).astype(jnp.float32)
    rates = jnp.exp(
        jnp.arange(0, width, 2, dtype=jnp.int32).astype(jnp.float32) * (-math.log(10000.0) / width)
    )
    angle = distance[:, None] * rates[None, :]
    return jnp.concatenate([jnp.sin(angle), jnp.cos(angle)], axis=1)


def dot_nt(a,b): return lax.dot_general(a,b,(((1,),(1,)),((),())),preferred_element_type=f32)
def dot_nn(a,b): return lax.dot_general(a,b,(((1,),(0,)),((),())),preferred_element_type=f32)

def attn_fwd_kernel(qu_ref,qv_ref,k_ref,v_ref,r_ref,bias_ref,o_ref,p_ref,beside=None):
    seg=qu_ref.shape[0]; total=k_ref.shape[0]; old=total-seg
    c=math.log2(math.e)/math.sqrt(DH)
    for ib in range(seg//BLK):
        if beside is not None: beside(ib)
        rows=pl.ds(ib*BLK,BLK)
        L=old+(ib+1)*BLK
        qu=qu_ref[rows,:]; qv=qv_ref[rows,:]
        raw=dot_nt(qv,r_ref[pl.ds(total-L,L),:])
        z=dot_nt(qu,k_ref[pl.ds(0,L),:])+pltpu.roll(raw,L-(BLK-1),axis=1,stride=1,stride_axis=0)
        M=L-BLK
        za=z[:,:M]+bias_ref[:,:M]
        rr=lax.broadcasted_iota(jnp.int32,(BLK,BLK),0); cc=lax.broadcasted_iota(jnp.int32,(BLK,BLK),1)
        zb=z[:,M:]
        zb=jnp.where(cc==rr,zb,jnp.where(cc<rr,zb+bias_ref[:,pl.ds(M,BLK)],NEG))
        top=jnp.maximum(jnp.max(za,axis=1,keepdims=True),jnp.max(zb,axis=1,keepdims=True))
        ea=jnp.exp2((za-top)*c); eb=jnp.exp2((zb-top)*c)
        inv=1.0/(jnp.sum(ea,axis=1,keepdims=True)+jnp.sum(eb,axis=1,keepdims=True))
        pa=(ea*inv).astype(bf16); pb=(eb*inv).astype(bf16)
        p_ref[0,rows,pl.ds(0,M)]=pa
        p_ref[0,rows,pl.ds(M,BLK)]=pb
        o_ref[rows,:]=(dot_nn(pa,v_ref[pl.ds(0,M),:])+dot_nn(pb,v_ref[pl.ds(M,BLK),:])).astype(bf16)

def attn_fwd_gather_kernel(pieces, *refs):
    shard, whole = refs[6], refs[9]
    local, sent, came = refs[10:]
    head = pl.program_id(0)
    height = shard.shape[0]
    rows = height // pieces
    moved = Gathering([(shard, n * rows, rows, whole, height) for n in range(pieces)], local, sent, came)

    @pl.when(head == 0)
    def _():
        moved.greet()
        for n in range(pieces):
            moved.begin(n)

    tiles = refs[0].shape[0] // BLK
    steps = {}
    for n in range(pieces):
        slot = 7 + (26 * n) // pieces
        steps.setdefault(slot, []).append((moved.onward, n))
        if n:
            steps.setdefault(slot, []).append((moved.last, n - 1))

    def beside(tile):
        for slot, phases in steps.items():
            if slot % tiles == tile:

                @pl.when(head == slot // tiles)
                def _(phases=phases):
                    for phase, n in phases:
                        phase(n)

    attn_fwd_kernel(*refs[:6], *refs[7:9], beside=beside)

    @pl.when(head == HEADS - 1)
    def _():
        moved.last(pieces - 1)
        for n in range(pieces):
            moved.complete(n)
        moved.drain()


def attn_fwd(qu, qv, k, v, r, bias, shard=None, pieces=8):
    seg, width = qu.shape
    total = k.shape[0]
    col = lambda n: pl.BlockSpec((n, DH), lambda h: (0, h))
    in_specs = [col(seg), col(seg), col(total), col(total), col(total)]
    in_specs += [pl.BlockSpec((1, total), lambda h: (0, 0))]
    out_specs = [col(seg), pl.BlockSpec((1, seg, total), lambda h: (h, 0, 0))]
    out_shape = [
        jax.ShapeDtypeStruct((seg, width), bf16),
        jax.ShapeDtypeStruct((HEADS, seg, total), bf16),
    ]
    cost = pl.CostEstimate(
        flops=6 * seg * total * width,
        bytes_accessed=2 * (3 * seg * width + 3 * total * width + HEADS * seg * total),
        transcendentals=HEADS * seg * total,
    )
    if shard is None:
        return pl.pallas_call(
            attn_fwd_kernel,
            grid=(HEADS,),
            in_specs=in_specs,
            out_specs=out_specs,
            out_shape=out_shape,
            cost_estimate=cost,
            compiler_params=pltpu.CompilerParams(vmem_limit_bytes=58 << 20),
            name="attn_fwd",
        )(qu, qv, k, v, r, bias)
    return pl.pallas_call(
        functools.partial(attn_fwd_gather_kernel, pieces),
        grid=(HEADS,),
        in_specs=in_specs + [pl.BlockSpec(shard.shape, lambda h: (0, 0))],
        out_specs=out_specs + [pl.BlockSpec(memory_space=pl.ANY)],
        out_shape=out_shape + [jax.ShapeDtypeStruct((8 * shard.shape[0], shard.shape[1]), bf16)],
        scratch_shapes=[pltpu.SemaphoreType.DMA((n * pieces,)) for n in (1, 7, 7)],
        cost_estimate=cost,
        compiler_params=pltpu.CompilerParams(
            collective_id=3, has_side_effects=True, vmem_limit_bytes=58 << 20
        ),
        name="attn_fwd_gather",
    )(qu, qv, k, v, r, bias, shard)


def attn_bwd_kernel(qu_ref,qv_ref,qut_ref,qvrt_ref,k_ref,v_ref,r_ref,p_ref,g_ref,gt_ref,dq_ref,dkt_ref,dvt_ref,drt_ref,sums_ref,dk_acc,dv_acc,dr_acc):
    seg=g_ref.shape[0]; total=k_ref.shape[0]; old=total-seg
    scale=1.0/math.sqrt(DH)
    rr=lax.broadcasted_iota(jnp.int32,(BLK,BLK),0); cc=lax.broadcasted_iota(jnp.int32,(BLK,BLK),1)
    flip=(rr+cc==BLK-1).astype(bf16)
    su=jnp.zeros((1,DH),f32); sv=jnp.zeros((1,DH),f32)
    nb=seg//BLK
    for ib in range(nb-1,-1,-1):
        rows=pl.ds(ib*BLK,BLK)
        L=old+(ib+1)*BLK
        g=g_ref[rows,:]; gt=gt_ref[:,rows]; qut=qut_ref[:,rows]
        plow=p_ref[0,rows,pl.ds(0,L)]
        p=plow.astype(f32)
        dp=dot_nt(g,v_ref[pl.ds(0,L),:])
        d=jnp.sum(p*dp,axis=1,keepdims=True)
        dz=(p*(dp-d)*scale).astype(bf16)
        dvt=dot_nn(gt,plow)
        dkt=dot_nn(qut,dz)
        dqu=dot_nn(dz,k_ref[pl.ds(0,L),:])
        rev=dot_nn(flip,dz)
        raw=pltpu.roll(rev,0,axis=1,stride=1,stride_axis=0).astype(bf16)
        T=pl.ds(total-L,L)
        dqv_rev=dot_nn(raw,r_ref[T,:])
        qvr=dot_nt(qvrt_ref[:,rows],flip).astype(bf16)
        drt=dot_nn(qvr,raw)
        dqv=lax.dot_general(flip.astype(f32),dqv_rev,(((1,),(0,)),((),())),preferred_element_type=f32,precision=lax.Precision.HIGHEST)
        su+=jnp.sum(dqu,axis=0,keepdims=True); sv+=jnp.sum(dqv,axis=0,keepdims=True)
        dq_ref[rows,:]=(dqu+dqv).astype(bf16)
        J=pl.ds(0,L)
        if ib==nb-1:
            dv_acc[...]=dvt; dk_acc[...]=dkt; dr_acc[...]=drt
        else:
            dv_acc[:,J]+=dvt; dk_acc[:,J]+=dkt; dr_acc[:,T]+=drt
    dkt_ref[...]=dk_acc[...].astype(bf16); dvt_ref[...]=dv_acc[...].astype(bf16); drt_ref[...]=dr_acc[...].astype(bf16)
    sums_ref[0:1,:]=su; sums_ref[1:2,:]=sv

def attn_bwd_sums_kernel(plan, sources, count, *refs):
    base, grads = refs[:10], refs[10 : 10 + count]
    refs = refs[10 + count :]
    results, outs, refs = refs[:5], refs[5 : 5 + count], refs[5 + count :]
    totals = refs[:3]
    sums = Sums(plan, sources, grads, outs, refs[3:])
    steps = sums.schedule()
    head = pl.program_id(0)
    per = -(-len(steps) // HEADS) if len(steps) > HEADS + 2 else 1

    for n in range(HEADS):

        @pl.when(head == n)
        def _(n=n):
            if n == 0:
                sums.greet()
            for step in steps[n * per : (n + 1) * per]:
                for phase, item in step:
                    phase(item)

    attn_bwd_kernel(*base, *results, *totals)

    @pl.when(head == HEADS - 1)
    def _():
        for step in steps[HEADS * per :]:
            for phase, item in step:
                phase(item)
        sums.drain()


def attn_bwd(qu, qv, k, v, r, p, g, grads=(), share=1.0):
    seg, width = qu.shape
    total = k.shape[0]
    col = lambda n: pl.BlockSpec((n, DH), lambda h: (0, h))
    row = lambda n: pl.BlockSpec((DH, n), lambda h: (h, 0))
    any_spec = pl.BlockSpec(memory_space=pl.ANY)
    in_specs = [col(seg), col(seg), row(seg), row(seg), col(total), col(total), col(total)]
    in_specs += [pl.BlockSpec((1, seg, total), lambda h: (h, 0, 0)), col(seg), row(seg)]
    out_specs = [col(seg), row(total), row(total), row(total), pl.BlockSpec((8, DH), lambda h: (0, h))]
    out_shape = [jax.ShapeDtypeStruct((seg, width), bf16)]
    out_shape += [jax.ShapeDtypeStruct((width, total), bf16)] * 3
    out_shape += [jax.ShapeDtypeStruct((8, width), f32)]
    scratch = [pltpu.VMEM((DH, total), f32)] * 3
    cost = pl.CostEstimate(
        flops=16 * seg * total * width,
        bytes_accessed=2 * (5 * seg * width + 6 * total * width + HEADS * seg * total),
        transcendentals=0,
    )
    operands = (qu, qv, qu.T, qv.T, k, v, r, p, g, g.T)
    if not grads:
        return pl.pallas_call(
            attn_bwd_kernel,
            grid=(HEADS,),
            in_specs=in_specs,
            out_specs=out_specs,
            out_shape=out_shape,
            scratch_shapes=scratch,
            cost_estimate=cost,
            compiler_params=pltpu.CompilerParams(vmem_limit_bytes=58 << 20),
            name="attn_bwd",
        )(*operands)
    plan, sources, arrays, shapes = sums_plan(grads, ())
    results = pl.pallas_call(
        functools.partial(attn_bwd_sums_kernel, plan, sources, len(arrays)),
        grid=(HEADS,),
        in_specs=in_specs + [any_spec] * len(arrays),
        out_specs=out_specs + [any_spec] * len(arrays),
        out_shape=out_shape + shapes,
        scratch_shapes=scratch + sums_scratch(plan),
        cost_estimate=cost,
        compiler_params=pltpu.CompilerParams(
            collective_id=4, has_side_effects=True, vmem_limit_bytes=58 << 20
        ),
        name="attn_bwd_sums",
    )(*operands, *arrays)
    return tuple(results[:5]) + tuple(total.astype(f32) * share for total in results[5:])


def cut(*values):
    return lax.optimization_barrier(values)


def positions_low(count, width):
    tile = 64
    rates = jnp.exp(
        jnp.arange(0, width, 2, dtype=jnp.int32).astype(f32) * (-math.log(10000.0) / width)
    )
    rates = jnp.concatenate([rates, rates])[None, :]
    upper = (jnp.arange(width, dtype=jnp.int32) < width // 2)[None, :]
    far = (count - 1 - tile * jnp.arange(count // tile, dtype=jnp.int32)).astype(f32)[:, None] * rates
    near = jnp.arange(tile, dtype=jnp.int32).astype(f32)[:, None] * rates
    sine, cosine = jnp.sin(far), jnp.cos(far)
    with_cos = jnp.where(upper, sine, cosine)[:, None, :]
    with_sin = jnp.where(upper, -cosine, sine)[:, None, :]
    near_cos, near_sin, with_cos, with_sin = cut(jnp.cos(near), jnp.sin(near), with_cos, with_sin)
    table = with_cos * near_cos[None] + with_sin * near_sin[None]
    return table.astype(bf16).reshape(count, width)


def hop(value, move):
    dp, fsdp = lax.axis_size("dp"), lax.axis_size("fsdp")
    pairs = []
    for z in range(dp):
        for f in range(fsdp):
            to = move(z, f)
            if to is not None:
                pairs.append((z * fsdp + f, to[0] * fsdp + to[1]))
    return lax.ppermute(value, ("dp", "fsdp"), pairs)


def inward_hop(w):
    to = {0: 1, 3: 2}
    return hop(w, lambda z, f: (to[z], f) if z in to else None)


def middle_hop(w):
    return hop(w, lambda z, f: (3 - z, f) if z in (1, 2) else None)


def outward_hop(w):
    to = {1: 0, 2: 3}
    return hop(w, lambda z, f: (to[z], f) if z in to else None)


def add(first, second):
    return (first.astype(f32) + second.astype(f32)).astype(bf16)


def finish(whole, last, share):
    plane = lax.axis_index("dp")
    return jnp.where((plane == 1) | (plane == 2), whole, last).astype(f32) * share


def add_rows(out, parts):
    rows = out.shape[0]
    height = 32 if rows % 32 == 0 else 16

    def one(i, carry):
        at = pl.ds(pl.multiple_of(i * height, height), height)
        total = parts[0][at, :].astype(f32)
        for part in parts[1:]:
            total = total + part[at, :].astype(f32)
        out[at, :] = total.astype(out.dtype)
        return carry

    lax.fori_loop(0, rows // height, one, 0)


FULL_BUFFERS = ("mine", "theirs", "far", "half_x", "half_y", "to_y", "to_x", "got_y", "got_x")
LINE_BUFFERS = ("own", "end", "mid")


def sums_scratch(plan):
    shapes = []
    for full, rows, cols in plan:
        if full:
            half = pltpu.VMEM((rows // 2, cols), bf16)
            one = pltpu.VMEM((rows, cols), bf16)
            shapes += [pltpu.VMEM((4, rows, cols), bf16)] * 2 + [one, half, half] + [one] * 4
        shapes += [pltpu.VMEM((rows, cols), bf16)] * 3
        shapes += [pltpu.SemaphoreType.DMA((n,)) for n in (4, 11, 11, 1)]
    return shapes


GAP, LINE_GAP = 2, 2


class Sums:
    def __init__(self, plan, sources, grads, outs, scratch):
        self.z, self.f = lax.axis_index("dp"), lax.axis_index("fsdp")
        self.chip, self.core = self.f // 2, self.f % 2
        self.middle = (self.z == 1) | (self.z == 2)
        self.edge = jnp.logical_not(self.middle)
        self.inward = (jnp.where(self.z < 2, 1, 2), self.f)
        self.outward = (jnp.where(self.z < 2, 0, 3), self.f)
        self.across = (3 - self.z, self.f)
        self.sibling, self.by_x, self.by_y = (
            (self.z, self.f ^ 1),
            (self.z, self.f ^ 2),
            (self.z, self.f ^ 4),
        )
        self.items, at = [], 0
        for n, (full, rows, cols) in enumerate(plan):
            names = (FULL_BUFFERS if full else ()) + LINE_BUFFERS + ("local", "sent", "came", "stored")
            b = dict(zip(names, scratch[at : at + len(names)]))
            at += len(names)
            b.update(full=full, rows=rows, source=grads[sources[n][0]], first=sources[n][1])
            b.update(target=outs[sources[n][0]])
            self.items.append(b)

    def greet(self):
        barrier = pltpu.get_barrier_semaphore()

        def signal(device):
            pl.semaphore_signal(
                barrier, inc=1, device_id=device, device_id_type=pl.DeviceIdType.MESH
            )

        for device in (self.sibling, self.by_x, self.by_y):
            signal(device)

        @pl.when(self.middle)
        def _():
            signal(self.outward)
            signal(self.across)
            pl.semaphore_wait(barrier, 5)

        @pl.when(self.edge)
        def _():
            signal(self.inward)
            pl.semaphore_wait(barrier, 4)

    def copy(self, b, n, src, dst, device):
        return pltpu.make_async_remote_copy(
            src_ref=src,
            dst_ref=dst,
            send_sem=b["sent"].at[n],
            recv_sem=b["came"].at[n],
            device_id=device,
            device_id_type=pl.DeviceIdType.MESH,
        )

    def rows_of(self, b):
        return pl.ds(b["first"], b["rows"])

    def across_cores(self, b, s):
        block = (self.chip ^ (3 - s)) * 2 + 1 - self.core
        src = b["source"].at[block, self.rows_of(b), :]
        return self.copy(b, s, src, b["theirs"].at[s], self.sibling)

    def load(self, b, s):
        if not b["full"]:
            src, dst = b["source"].at[self.rows_of(b), :], b["own"]
        else:
            block = (self.chip ^ (3 - s)) * 2 + self.core
            src, dst = b["source"].at[block, self.rows_of(b), :], b["mine"].at[s]
        return pltpu.make_async_copy(src, dst, b["local"].at[s])

    def halves_out(self, b):
        half = b["rows"] // 2
        return (
            self.copy(b, 4, b["far"].at[pl.ds(0, half), :], b["half_x"], self.by_x),
            self.copy(b, 5, b["far"].at[pl.ds(half, half), :], b["half_y"], self.by_y),
        )

    def near_out(self, b):
        return (
            self.copy(b, 6, b["to_y"], b["got_y"], self.by_y),
            self.copy(b, 7, b["to_x"], b["got_x"], self.by_x),
        )

    def go_in(self, b):
        return self.copy(b, 8, b["own"], b["end"], self.inward)

    def go_mid(self, b):
        return self.copy(b, 9, b["own"], b["mid"], self.across)

    def go_out(self, b):
        return self.copy(b, 10, b["mid"], b["end"], self.outward)

    def store(self, b, name):
        return pltpu.make_async_copy(b[name], b["target"].at[self.rows_of(b), :], b["stored"].at[0])

    def begin(self, b):
        if b["full"]:
            for s in range(4):
                self.across_cores(b, s).start()
                self.load(b, s).start()
        else:
            self.load(b, 0).start()

    def arrived(self, b, s):
        self.across_cores(b, s).wait_recv()
        self.load(b, s).wait()

    def far(self, b):
        self.arrived(b, 0)
        add_rows(b["far"], [b["mine"].at[0], b["theirs"].at[0]])
        for c in self.halves_out(b):
            c.start()

    def near(self, b):
        half = b["rows"] // 2
        low, high = pl.ds(0, half), pl.ds(half, half)
        self.arrived(b, 1)
        self.arrived(b, 2)
        for c in self.halves_out(b):
            c.wait_recv()
        mine, theirs = b["mine"], b["theirs"]
        add_rows(b["to_y"].at[low, :], [mine.at[1, low, :], theirs.at[1, low, :], b["half_x"]])
        add_rows(b["to_y"].at[high, :], [mine.at[1, high, :], theirs.at[1, high, :]])
        add_rows(b["to_x"].at[low, :], [mine.at[2, low, :], theirs.at[2, low, :]])
        add_rows(b["to_x"].at[high, :], [mine.at[2, high, :], theirs.at[2, high, :], b["half_y"]])
        for c in self.near_out(b):
            c.start()

    def own(self, b):
        self.arrived(b, 3)
        for c in self.near_out(b):
            c.wait_recv()
        add_rows(b["own"], [b["mine"].at[3], b["theirs"].at[3], b["got_x"], b["got_y"]])

    def line_in(self, b):
        if not b["full"]:
            self.load(b, 0).wait()

        @pl.when(self.edge)
        def _():
            self.go_in(b).start()

    def line_mid(self, b):
        @pl.when(self.middle)
        def _():
            self.go_in(b).wait_recv()
            add_rows(b["own"], [b["own"], b["end"]])
            self.go_mid(b).start()

    def line_out(self, b):
        @pl.when(self.middle)
        def _():
            self.go_mid(b).wait_recv()
            add_rows(b["mid"], [b["own"], b["mid"]])
            self.go_out(b).start()
            self.store(b, "mid").start()

    def line_last(self, b):
        @pl.when(self.edge)
        def _():
            self.go_out(b).wait_recv()
            self.store(b, "end").start()

    def schedule(self):
        wide = [b for b in self.items if b["full"]]
        left = [b for b in self.items if not b["full"]]
        line, due, slot = [], [], 0
        while sum(b is not None for b in line) < len(self.items):
            if 0 <= slot - 2 * GAP < len(wide):
                due.append(wide[slot - 2 * GAP])
            if left and (not due or slot % 2 == 0):
                line.append(left.pop(0))
            elif due:
                line.append(due.pop(0))
            else:
                line.append(None)
            slot += 1
        steps = []
        for t in range(len(line) + 3 * LINE_GAP):
            step = []
            if t + 2 < len(wide):
                step.append((self.begin, wide[t + 2]))
            for phase, back in ((self.far, 0), (self.near, GAP), (self.own, 2 * GAP)):
                if 0 <= t - back < len(wide):
                    step.append((phase, wide[t - back]))
            phases = (self.line_in, self.line_mid, self.line_out, self.line_last)
            for back, phase in enumerate(phases):
                at = t - back * LINE_GAP
                if 0 <= at < len(line) and line[at] is not None:
                    step.append((phase, line[at]))
            steps.append(step)
        first = [(self.begin, b) for b in self.items if not b["full"]]
        first += [(self.begin, b) for b in wide[:2]]
        return [first] + steps

    def drain(self):
        for b in self.items:
            if b["full"]:
                for s in range(4):
                    self.across_cores(b, s).wait_send()
                for c in self.halves_out(b) + self.near_out(b):
                    c.wait_send()
            self.store(b, "mid").wait()

        @pl.when(self.edge)
        def _():
            for b in self.items:
                self.go_in(b).wait_send()

        @pl.when(self.middle)
        def _():
            for b in self.items:
                self.go_mid(b).wait_send()
                self.go_out(b).wait_send()


def sums_plan(fulls, shards):
    plan, sources, arrays, shapes = [], [], [], []
    for full, group in ((True, fulls), (False, shards)):
        for g, pieces in group:
            rows, cols = g.shape[0] // (8 if full else 1), g.shape[1]
            for p in range(pieces):
                plan.append((full, rows // pieces, cols))
                sources.append((len(arrays), p * (rows // pieces)))
            arrays.append(g.reshape(8, rows, cols) if full else g)
            shapes.append(jax.ShapeDtypeStruct((rows, cols), bf16))
    return tuple(plan), tuple(sources), arrays, shapes


def tail_kernel(plan, sources, count, *refs):
    sums = Sums(plan, sources, refs[:count], refs[count : 2 * count], refs[2 * count :])
    sums.greet()
    for step in sums.schedule():
        for phase, item in step:
            phase(item)
    sums.drain()


def reduce_tail(fulls, shards, share, number):
    plan, sources, arrays, shapes = sums_plan(fulls, shards)
    totals = pl.pallas_call(
        functools.partial(tail_kernel, plan, sources, len(arrays)),
        in_specs=[pl.BlockSpec(memory_space=pl.ANY)] * len(arrays),
        out_specs=[pl.BlockSpec(memory_space=pl.ANY)] * len(arrays),
        out_shape=shapes,
        scratch_shapes=sums_scratch(plan),
        compiler_params=pltpu.CompilerParams(
            collective_id=number, has_side_effects=True, vmem_limit_bytes=56 << 20
        ),
        name="reduce_tail",
    )(*arrays)
    return [total.astype(f32) * share for total in totals]


class Gathering:
    def __init__(self, pieces, local, sent, came):
        self.pieces, self.local, self.sent, self.came = pieces, local, sent, came
        z, f = lax.axis_index("dp"), lax.axis_index("fsdp")
        near = 2 + 2 * lax.rem(z, 2)
        self.first_to, self.second_to = (z, f ^ near), (z, f ^ (6 - near))
        self.pair_to, self.core_to = (z ^ 1, f), (z, f ^ 1)
        self.slots = (f, f ^ near, f ^ (6 - near), f ^ 6)

    def greet(self):
        barrier = pltpu.get_barrier_semaphore()
        for device in (self.first_to, self.second_to, self.pair_to, self.core_to):
            pl.semaphore_signal(
                barrier, inc=1, device_id=device, device_id_type=pl.DeviceIdType.MESH
            )
        pl.semaphore_wait(barrier, 4)

    def part(self, n, slot):
        shard, start, rows, whole, height = self.pieces[n]
        return whole.at[pl.ds(pl.multiple_of(slot * height + start, 16), rows), :]

    def shard(self, n):
        shard, start, rows, whole, height = self.pieces[n]
        return shard.at[pl.ds(start, rows), :]

    def copy(self, n, k, src, slot, device):
        return pltpu.make_async_remote_copy(
            src_ref=src,
            dst_ref=self.part(n, slot),
            send_sem=self.sent.at[n * 7 + k],
            recv_sem=self.came.at[n * 7 + k],
            device_id=device,
            device_id_type=pl.DeviceIdType.MESH,
        )

    def first(self, n):
        return self.copy(n, 0, self.shard(n), self.slots[0], self.first_to)

    def pair(self, n):
        return self.copy(n, 1, self.part(n, self.slots[1]), self.slots[1], self.pair_to)

    def second(self, n):
        return self.copy(n, 2, self.part(n, self.slots[1]), self.slots[1], self.second_to)

    def core(self, n, s):
        src = self.shard(n) if s == 0 else self.part(n, self.slots[s])
        return self.copy(n, 3 + s, src, self.slots[s], self.core_to)

    def mine(self, n):
        return pltpu.make_async_copy(self.shard(n), self.part(n, self.slots[0]), self.local.at[n])

    def begin(self, n):
        self.first(n).start()
        self.mine(n).start()
        self.core(n, 0).start()

    def onward(self, n):
        self.first(n).wait_recv()
        self.pair(n).start()
        self.second(n).start()
        self.core(n, 1).start()

    def last(self, n):
        self.pair(n).wait_recv()
        self.core(n, 2).start()
        self.second(n).wait_recv()
        self.core(n, 3).start()

    def complete(self, n):
        self.mine(n).wait()
        for s in range(4):
            self.core(n, s).wait_recv()

    def drain(self):
        for n in range(len(self.pieces)):
            for copy in (self.first(n), self.pair(n), self.second(n)):
                copy.wait_send()
            for s in range(4):
                self.core(n, s).wait_send()


def tile_loop(rows, height, body):
    def one(i, carry):
        body(pl.ds(pl.multiple_of(i * height, height), height))
        return carry

    lax.fori_loop(0, rows // height, one, 0)


HEAD_ITEMS = ("table", "keys", "values", "query", "position", "output", "inner")
INNER_PIECES = 4


def head_kernel(*refs):
    count = len(HEAD_ITEMS)
    rows_in, shards, pos_ref = refs[:3], refs[3 : 3 + count], refs[3 + count]
    refs = refs[4 + count :]
    (xhat_out, normed_out, qu_out, qv_out, keys_out, values_out, relative_out) = refs[:7]
    weights_out, refs = refs[7 : 7 + count], refs[7 + count :]
    wholes, refs = refs[:count], refs[count:]
    xhat, normed, pos, qu, qv, keys, values, relative = refs[:8]
    local, sent, came, left = refs[8:]
    moved = Gathering(
        [(shards[n], 0, shards[n].shape[0], wholes[n], shards[n].shape[0]) for n in range(count - 1)]
        + [
            (shards[-1], p * shards[-1].shape[0] // INNER_PIECES, shards[-1].shape[0] // INNER_PIECES)
            + (wholes[-1], shards[-1].shape[0])
            for p in range(INNER_PIECES)
        ],
        local,
        sent,
        came,
    )
    moved.greet()
    posload = pltpu.make_async_copy(pos_ref, pos, local.at[count - 1 + INNER_PIECES])
    stores = []

    def leave(src, dst):
        copy = pltpu.make_async_copy(src, dst, left.at[len(stores)])
        copy.start()
        stores.append(copy)

    def complete(n):
        moved.complete(n)
        if n < count - 1:
            leave(wholes[n], weights_out[n])

    def comm(*steps):
        for kind, n in steps:
            {"b": moved.begin, "o": moved.onward, "l": moved.last, "c": complete}[kind](n)

    comm(("b", 0), ("b", 1), ("b", 2))
    posload.start()
    per = rows_in[0].shape[0]
    for b in range(3):
        source = rows_in[b]

        def normalize(at, b=b, source=source):
            rows = source[at, :].astype(f32)
            centered = rows - jnp.mean(rows, axis=-1, keepdims=True)
            spread = lax.rsqrt(jnp.mean(centered * centered, axis=-1, keepdims=True) + EPSILON)
            xhat[b, at, :] = centered * spread

        tile_loop(per, 64, normalize)
        if b == 1:
            comm(("o", 0))
    leave(xhat.at[2], xhat_out)
    comm(("o", 1), ("b", 3), ("l", 0), ("c", 0))

    def row_of(k):
        height = shards[0].shape[0]
        return jnp.concatenate(
            [wholes[0][d * height : (d + 1) * height, :].astype(f32)[k : k + 1, :] for d in range(8)], axis=1
        )

    gain, shift, content, posbias = (row_of(k) for k in range(4))
    for b in range(3):

        def scale(at, b=b):
            normed[b, at, :] = (xhat[b, at, :] * gain + shift).astype(bf16)

        tile_loop(per, 64, scale)
    leave(normed, normed_out)
    comm(("o", 2), ("b", 4), ("l", 1), ("b", 5), ("c", 1))

    def project(src, weight, dst, steps):
        for b in range(3):

            def one(at, b=b):
                dst[b, at, :] = jnp.dot(
                    src[b, at, :], weight[...], preferred_element_type=f32
                ).astype(bf16)

            tile_loop(per, 256, one)
            comm(*steps[b])

    project(normed, wholes[1], keys, ((("o", 3), ("b", 6)), (("l", 2),), ()))
    leave(keys, keys_out)
    comm(("c", 2), ("o", 4), ("b", 7), ("l", 3))
    project(normed, wholes[2], values, ((), (("o", 5), ("b", 8)), (("l", 4),)))
    leave(values, values_out)
    comm(("c", 3))

    def queries(at):
        query = jnp.dot(normed[2, at, :], wholes[3][...], preferred_element_type=f32)
        qu[at, :] = (query + content).astype(bf16)
        qv[at, :] = (query + posbias).astype(bf16)

    tile_loop(per, 256, queries)
    leave(qu, qu_out)
    leave(qv, qv_out)
    comm(("o", 6), ("b", 9), ("l", 5), ("c", 4))
    posload.wait()
    project(pos, wholes[4], relative, ((("o", 7),), (("l", 6),), (("o", 8),)))
    leave(relative, relative_out)
    comm(("c", 5), ("l", 7), ("o", 9), ("l", 8), ("l", 9))
    for n in range(6, 10):
        complete(n)
    leave(wholes[-1], weights_out[-1])
    moved.drain()
    for copy in stores:
        copy.wait()


def head_stage(rows_in, shards, pos_low):
    per, width = rows_in[0].shape
    three = (3, per, width)
    count = len(shards)
    full = [(8 * w.shape[0], w.shape[1]) for w in shards]
    any_spec = pl.BlockSpec(memory_space=pl.ANY)
    shape = jax.ShapeDtypeStruct
    shapes = [shape((per, width), f32), shape(three, bf16)] + [shape((per, width), bf16)] * 2
    shapes += [shape(three, bf16)] * 3 + [shape(s, bf16) for s in full]
    vmem = pltpu.VMEM
    scratch = [vmem(s, bf16) for s in full] + [vmem(three, f32), vmem(three, bf16), vmem(three, bf16)]
    scratch += [vmem((per, width), bf16)] * 2 + [vmem(three, bf16)] * 3
    scratch += [pltpu.SemaphoreType.DMA((n,)) for n in (count + INNER_PIECES, 7 * (count + 3), 7 * (count + 3), 7 + count)]
    return pl.pallas_call(
        head_kernel,
        in_specs=[pl.BlockSpec(memory_space=pltpu.VMEM)] * 3 + [any_spec] * (count + 1),
        out_specs=[any_spec] * len(shapes),
        out_shape=shapes,
        scratch_shapes=scratch,
        compiler_params=pltpu.CompilerParams(
            collective_id=2, has_side_effects=True, vmem_limit_bytes=56 << 20
        ),
        name="head_stage",
    )(*rows_in, *shards, pos_low.reshape(three))


def gather(shards):
    return [lax.all_gather(w, "fsdp", axis=0, tiled=True) for w in shards]


def reduce(grads, share):
    done = []
    for g in grads:
        part = lax.psum_scatter(g, "fsdp", scatter_dimension=0, tiled=True)
        done.append(lax.psum(part, "dp").astype(f32) * share)
    return done


def pack_vectors(vectors, parts):
    flat = jnp.concatenate([v.reshape(parts, -1) for v in vectors], axis=1)
    width = 1024
    lines = 32 * (-(-flat.shape[1] // (32 * width)))
    flat = jnp.pad(flat, ((0, 0), (0, lines * width - flat.shape[1])))
    return flat.reshape(parts * lines, width)


def unpack_vectors(table, parts, sizes):
    flat = table.reshape(parts, -1)
    result, start = [], 0
    for size in sizes:
        result.append(flat[:, start : start + size].reshape(parts * size))
        start += size
    return result


def per_device_plain(
    tokens,
    memory,
    compressed,
    mem_fill,
    cmem_fill,
    pad_mask,
    first_gain,
    first_shift,
    query_weight,
    key_weight,
    value_weight,
    position_weight,
    content_bias,
    position_bias,
    output_weight,
    second_gain,
    second_shift,
    inner_weight,
    inner_bias,
    outer_weight,
    outer_bias,
    conv_weight,
    conv_bias,
    out_grad,
    comp_grad,
):
    streams, seg_rows, width = tokens.shape
    mem_rows = memory.shape[1]
    cmem_rows = compressed.shape[1]
    total = cmem_rows + mem_rows + seg_rows
    shards = lax.axis_size("fsdp")
    share = 1.0 / (streams * lax.axis_size("dp") * shards)
    vectors = (
        first_gain,
        first_shift,
        content_bias,
        position_bias,
        second_gain,
        second_shift,
        inner_bias,
        outer_bias,
        conv_bias,
    )
    sizes = [v.shape[0] for v in vectors]

    groups = mem_rows // RATE
    start = mem_rows - RATE * groups
    mem_valid = (
        jnp.arange(mem_rows, dtype=jnp.int32)[None, :] >= (mem_rows - mem_fill)[:, None]
    ).astype(bf16)
    taps = (memory * mem_valid[..., None])[:, start:, :].reshape(streams * groups, RATE * width)
    group_valid = (
        (start + RATE * jnp.arange(groups, dtype=jnp.int32) + RATE - 1)[None, :]
        >= (mem_rows - mem_fill)[:, None]
    ).reshape(streams * groups, 1)
    made_grad = comp_grad.reshape(streams * groups, width) * group_valid.astype(bf16)
    conv_grad = jnp.einsum("nk,nd->kd", taps, made_grad, preferred_element_type=f32).astype(bf16)
    conv_bias_grad = jnp.sum(made_grad.astype(f32), axis=0)

    query_w, key_w, value_w, table = gather(
        [query_weight, key_weight, value_weight, pack_vectors(vectors, 1)]
    )
    (gain_one, shift_one, content_b, position_b, gain_two, shift_two, inner_b, outer_b, conv_b) = (
        unpack_vectors(table, shards, sizes)
    )
    position_w, output_w = gather([position_weight, output_weight])
    (inner_w,) = gather([inner_weight])
    (outer_w,) = gather([outer_weight])
    (conv_w,) = gather([conv_weight])

    whole = jnp.concatenate([compressed[0], memory[0], tokens[0]], axis=0).astype(f32)
    normed, scaled_one, spread_one = norm_parts(whole, gain_one, shift_one)
    normed_low = normed.astype(bf16)
    own_rows = normed_low[total - seg_rows :]
    query = jnp.dot(own_rows, query_w, preferred_element_type=f32)
    query_u = (query + content_b.astype(f32)).astype(bf16)
    query_v = (query + position_b.astype(f32)).astype(bf16)
    keys = jnp.dot(normed_low, key_w, preferred_element_type=f32).astype(bf16)
    values = jnp.dot(normed_low, value_w, preferred_element_type=f32).astype(bf16)
    pos_low = positions(total, width).astype(bf16)
    relative = jnp.dot(pos_low, position_w, preferred_element_type=f32).astype(bf16)
    valid = jnp.concatenate(
        [
            jnp.arange(cmem_rows, dtype=jnp.int32) >= cmem_rows - cmem_fill[0],
            jnp.arange(mem_rows, dtype=jnp.int32) >= mem_rows - mem_fill[0],
            pad_mask[0] == 1,
        ]
    )
    bias = jnp.where(valid, 0.0, NEG).astype(f32)[None]
    mixed, prob_low = attn_fwd(query_u, query_v, keys, values, relative, bias)
    hidden = tokens[0].astype(f32) + jnp.dot(mixed, output_w, preferred_element_type=f32)
    inner_norm, scaled_two, spread_two = norm_parts(hidden, gain_two, shift_two)
    inner_low = inner_norm.astype(bf16)
    preact = jnp.dot(inner_low, inner_w, preferred_element_type=f32) + inner_b.astype(f32)
    active = smooth_gate(preact).astype(bf16)
    result = (
        hidden
        + jnp.dot(active, outer_w, preferred_element_type=f32)
        + outer_b.astype(f32)
    )
    made = (
        jnp.dot(taps, conv_w, preferred_element_type=f32) + conv_b.astype(f32)
    ) * group_valid.astype(f32)

    grad = out_grad[0]
    grad_wide = grad.astype(f32)
    outer_grad = jnp.einsum("sf,sd->fd", active, grad, preferred_element_type=f32).astype(bf16)
    (outer_mean,) = reduce([outer_grad], share)
    outer_bias_grad = jnp.sum(grad_wide, axis=0)
    active_grad = jnp.einsum("sd,fd->sf", grad, outer_w, preferred_element_type=f32)
    gate_pull = jax.vjp(smooth_gate, preact)[1]
    preact_grad = gate_pull(active_grad)[0].astype(bf16)
    inner_grad = jnp.einsum("sd,sf->df", inner_low, preact_grad, preferred_element_type=f32).astype(
        bf16
    )
    (inner_mean,) = reduce([inner_grad], share)
    (conv_mean,) = reduce([conv_grad], share)
    inner_bias_grad = jnp.sum(preact_grad.astype(f32), axis=0)
    inner_norm_grad = jnp.einsum("sf,df->sd", preact_grad, inner_w, preferred_element_type=f32)
    second_gain_grad = jnp.sum(inner_norm_grad * scaled_two, axis=0)
    second_shift_grad = jnp.sum(inner_norm_grad, axis=0)
    hidden_grad = grad_wide + norm_back(inner_norm_grad, scaled_two, spread_two, gain_two)

    hidden_low = hidden_grad.astype(bf16)
    output_grad = jnp.einsum("sd,se->de", mixed, hidden_low, preferred_element_type=f32).astype(bf16)
    mixed_grad = jnp.einsum("se,de->sd", hidden_low, output_w, preferred_element_type=f32).astype(
        bf16
    )
    query_low, keys_t, values_t, relative_t, sums = attn_bwd(
        query_u, query_v, keys, values, relative, prob_low, mixed_grad
    )
    position_grad = jnp.einsum("ld,el->de", pos_low, relative_t, preferred_element_type=f32).astype(
        bf16
    )
    query_grad = jnp.einsum("sd,se->de", own_rows, query_low, preferred_element_type=f32).astype(
        bf16
    )
    key_grad = jnp.einsum("sd,es->de", normed_low, keys_t, preferred_element_type=f32).astype(bf16)
    value_grad = jnp.einsum("sd,es->de", normed_low, values_t, preferred_element_type=f32).astype(
        bf16
    )
    normed_grad = jnp.einsum("es,de->sd", keys_t, key_w, preferred_element_type=f32)
    normed_grad = normed_grad + jnp.einsum(
        "es,de->sd", values_t, value_w, preferred_element_type=f32
    )
    own_grad = jnp.einsum("se,de->sd", query_low, query_w, preferred_element_type=f32)
    normed_grad = normed_grad + jnp.pad(own_grad, ((total - seg_rows, 0), (0, 0)))
    first_gain_grad = jnp.sum(normed_grad * scaled_one, axis=0)
    first_shift_grad = jnp.sum(normed_grad, axis=0)
    own = slice(total - seg_rows, None)
    token_gradient = hidden_grad + norm_back(
        normed_grad[own], scaled_one[own], spread_one[own], gain_one
    )
    vector_grads = (
        first_gain_grad,
        first_shift_grad,
        sums[0],
        sums[1],
        second_gain_grad,
        second_shift_grad,
        inner_bias_grad,
        outer_bias_grad,
        conv_bias_grad,
    )
    packed = pack_vectors([v.astype(bf16) for v in vector_grads], shards)
    (output_mean,) = reduce([output_grad], share)
    query_mean, key_mean, value_mean, position_mean, table_mean = reduce(
        [query_grad, key_grad, value_grad, position_grad, packed], share
    )
    (
        first_gain_mean,
        first_shift_mean,
        content_mean,
        posbias_mean,
        second_gain_mean,
        second_shift_mean,
        inner_bias_mean,
        outer_bias_mean,
        conv_bias_mean,
    ) = unpack_vectors(table_mean, 1, sizes)
    return (
        result.astype(bf16)[None],
        token_gradient[None],
        made.astype(bf16)[None],
        first_gain_mean,
        first_shift_mean,
        query_mean,
        key_mean,
        value_mean,
        position_mean,
        content_mean,
        posbias_mean,
        output_mean,
        second_gain_mean,
        second_shift_mean,
        inner_mean,
        inner_bias_mean,
        outer_mean,
        outer_bias_mean,
        conv_mean,
        conv_bias_mean,
    )


def per_device_direct(
    tokens,
    memory,
    compressed,
    mem_fill,
    cmem_fill,
    pad_mask,
    first_gain,
    first_shift,
    query_weight,
    key_weight,
    value_weight,
    position_weight,
    content_bias,
    position_bias,
    output_weight,
    second_gain,
    second_shift,
    inner_weight,
    inner_bias,
    outer_weight,
    outer_bias,
    conv_weight,
    conv_bias,
    out_grad,
    comp_grad,
):
    streams, seg_rows, width = tokens.shape
    mem_rows = memory.shape[1]
    cmem_rows = compressed.shape[1]
    total = cmem_rows + mem_rows + seg_rows
    old = total - seg_rows
    shards = lax.axis_size("fsdp")
    share = 1.0 / (streams * lax.axis_size("dp") * shards)
    lanes = 128
    vectors = (
        first_gain,
        first_shift,
        content_bias,
        position_bias,
        second_gain,
        second_shift,
        outer_bias,
        conv_bias,
        inner_bias,
    )
    sizes = [v.shape[0] for v in vectors]
    lines = [v.reshape(-1, lanes) for v in vectors]
    table = jnp.zeros((32, lanes), bf16)
    row, line = jnp.arange(32, dtype=jnp.int32)[:, None], 0
    for v in lines:
        for n in range(v.shape[0]):
            table = jnp.where(row == line, v[n][None], table)
            line += 1
    pos_low = positions_low(total, width)
    (
        scaled_one,
        normed_low,
        query_u,
        query_v,
        keys,
        values,
        relative,
        table,
        key_w,
        value_w,
        query_w,
        position_w,
        output_w,
        inner_w,
    ) = head_stage(
        (compressed[0], memory[0], tokens[0]),
        (table, key_weight, value_weight, query_weight, position_weight, output_weight, inner_weight),
        pos_low,
    )
    normed_low, keys, values, relative = (
        v.reshape(total, width) for v in (normed_low, keys, values, relative)
    )
    own_rows = normed_low[old:]
    blocks = table.reshape(shards, 32, lanes)
    gain_one, shift_one = blocks[:, 0].reshape(width), blocks[:, 1].reshape(width)
    gain_two, shift_two, outer_b, conv_b = (blocks[:, n].reshape(width) for n in (4, 5, 6, 7))
    inner_b = blocks[:, 8 : 8 + sizes[-1] // lanes].reshape(shards * sizes[-1])

    valid = jnp.concatenate(
        [
            jnp.arange(cmem_rows, dtype=jnp.int32) >= cmem_rows - cmem_fill[0],
            jnp.arange(mem_rows, dtype=jnp.int32) >= mem_rows - mem_fill[0],
            pad_mask[0] == 1,
        ]
    )
    bias = jnp.where(valid, 0.0, NEG).astype(f32)[None]
    groups = mem_rows // RATE
    start = mem_rows - RATE * groups
    mem_valid = (jnp.arange(mem_rows, dtype=jnp.int32) >= mem_rows - mem_fill[0]).astype(bf16)
    taps = (memory[0] * mem_valid[:, None])[start:, :].reshape(groups, RATE * width)
    group_valid = (
        start + RATE * jnp.arange(groups, dtype=jnp.int32) + RATE - 1 >= mem_rows - mem_fill[0]
    )[:, None]
    made_grad = comp_grad[0] * group_valid.astype(bf16)
    conv_grad = jnp.einsum("nk,nd->kd", taps, made_grad, preferred_element_type=f32).astype(bf16)
    conv_bias_grad = jnp.sum(made_grad.astype(f32), axis=0)

    conv_grad, taps, query_u = cut(conv_grad, taps, query_u)
    outer_weight, query_u = cut(outer_weight, query_u)
    outer_w = lax.all_gather(outer_weight, "fsdp", axis=0, tiled=True)
    mixed, prob_low = attn_fwd(query_u, query_v, keys, values, relative, bias)
    hidden = tokens[0].astype(f32) + jnp.dot(mixed, output_w, preferred_element_type=f32)
    inner_norm, scaled_two, spread_two = norm_parts(hidden, gain_two, shift_two)
    inner_low = inner_norm.astype(bf16)
    preact = jnp.dot(inner_low, inner_w, preferred_element_type=f32) + inner_b.astype(f32)
    active = smooth_gate(preact).astype(bf16)
    grad = out_grad[0]
    grad_wide = grad.astype(f32)
    active, preact = cut(active, preact)
    outer_grad = jnp.einsum("sf,sd->fd", active, grad, preferred_element_type=f32).astype(bf16)
    outer_bias_grad = jnp.sum(grad_wide, axis=0)

    outer_w, outer_grad, conv_grad = cut(outer_w, outer_grad, conv_grad)
    conv_part = lax.psum_scatter(conv_grad, "fsdp", scatter_dimension=0, tiled=True)
    outer_part = lax.psum_scatter(outer_grad, "fsdp", scatter_dimension=0, tiled=True)
    active_grad = jnp.einsum("sd,fd->sf", grad, outer_w, preferred_element_type=f32)
    gate_pull = jax.vjp(smooth_gate, preact)[1]
    preact_grad = gate_pull(active_grad)[0].astype(bf16)
    inner_bias_grad = jnp.sum(preact_grad.astype(f32), axis=0)
    inner_grad = jnp.einsum("sd,sf->df", inner_low, preact_grad, preferred_element_type=f32).astype(
        bf16
    )
    inner_norm_grad = jnp.einsum("sf,df->sd", preact_grad, inner_w, preferred_element_type=f32)
    second_gain_grad = jnp.sum(inner_norm_grad * scaled_two, axis=0)
    second_shift_grad = jnp.sum(inner_norm_grad, axis=0)
    hidden_grad = grad_wide + norm_back(inner_norm_grad, scaled_two, spread_two, gain_two)
    hidden_low = hidden_grad.astype(bf16)
    mixed_grad = jnp.einsum("se,de->sd", hidden_low, output_w, preferred_element_type=f32).astype(
        bf16
    )
    query_g, keys_g, values_g, relative_g, sums = attn_bwd(
        query_u, query_v, keys, values, relative, prob_low, mixed_grad
    )
    conv_part, query_g, conv_weight = cut(conv_part, query_g, conv_weight)
    conv_end = inward_hop(conv_part)
    conv_w = lax.all_gather(conv_weight, "fsdp", axis=0, tiled=True)
    key_grad = jnp.einsum("sd,es->de", normed_low, keys_g, preferred_element_type=f32).astype(bf16)
    value_grad = jnp.einsum("sd,es->de", normed_low, values_g, preferred_element_type=f32).astype(bf16)
    position_grad = jnp.einsum("ld,el->de", pos_low, relative_g, preferred_element_type=f32).astype(
        bf16
    )
    key_grad, value_grad, position_grad, conv_end, query_g = cut(
        key_grad, value_grad, position_grad, conv_end, query_g
    )
    conv_pair = add(conv_part, conv_end)
    conv_mid = middle_hop(conv_pair)
    query_grad = jnp.einsum("sd,se->de", own_rows, query_g, preferred_element_type=f32).astype(bf16)
    columns = (
        (query_w, jnp.sum(query_g.astype(f32), axis=0)),
        (key_w, jnp.sum(keys_g.astype(f32), axis=1)),
        (value_w, jnp.sum(values_g.astype(f32), axis=1)),
    )
    first_shift_grad = sum(jnp.sum(w.astype(f32) * column[None, :], axis=1) for w, column in columns)
    own_grad = jnp.einsum("se,de->sd", query_g, query_w, preferred_element_type=f32)
    own_grad = own_grad + jnp.einsum(
        "es,de->sd", keys_g[:, old:], key_w, preferred_element_type=f32
    )
    own_grad = own_grad + jnp.einsum(
        "es,de->sd", values_g[:, old:], value_w, preferred_element_type=f32
    )
    inner = own_grad * gain_one.astype(f32)
    own = tokens[0].astype(f32)
    spread_own = lax.rsqrt(
        jnp.mean((own - jnp.mean(own, axis=-1, keepdims=True)) ** 2, axis=-1, keepdims=True) + EPSILON
    )
    token_gradient = hidden_grad + spread_own * (
        inner
        - jnp.mean(inner, axis=-1, keepdims=True)
        - scaled_one * jnp.mean(inner * scaled_one, axis=-1, keepdims=True)
    )
    conv_mid, own_grad, active, hidden_low = cut(conv_mid, own_grad, active, hidden_low)
    conv_sum = add(conv_pair, conv_mid)
    conv_last = outward_hop(conv_sum)
    output_grad = jnp.einsum("sd,se->de", mixed, hidden_low, preferred_element_type=f32).astype(bf16)
    vector_grads = (
        first_shift_grad,
        sums[0],
        sums[1],
        second_gain_grad,
        second_shift_grad,
        outer_bias_grad,
        conv_bias_grad,
        inner_bias_grad,
    )
    packed = jnp.concatenate([v.reshape(shards, -1, lanes) for v in vector_grads], axis=1)
    packed = jnp.pad(packed, ((0, 0), (0, 32 - packed.shape[1]), (0, 0))).astype(bf16)
    result = (
        hidden + jnp.dot(active, outer_w, preferred_element_type=f32) + outer_b.astype(f32)
    ).astype(bf16)
    made = (
        (jnp.dot(taps, conv_w, preferred_element_type=f32) + conv_b.astype(f32))
        * group_valid.astype(f32)
    ).astype(bf16)
    (
        output_mean,
        query_mean,
        key_mean,
        value_mean,
        position_mean,
        inner_mean,
        table_mean,
        outer_mean,
    ) = reduce_tail(
        [(g, 2) for g in (output_grad, query_grad, key_grad, value_grad, position_grad)]
        + [(inner_grad, 4)]
        + [(packed.reshape(shards * 32, lanes), 1)],
        [(outer_part, 4)],
        share,
        1,
    )
    conv_last, query_mean = cut(conv_last, query_mean)
    conv_mean = finish(conv_sum, conv_last, share)
    (
        first_shift_mean,
        content_mean,
        posbias_mean,
        second_gain_mean,
        second_shift_mean,
        outer_bias_mean,
        conv_bias_mean,
    ) = (table_mean[n] for n in range(7))
    inner_bias_mean = table_mean[7 : 7 + sizes[-1] // lanes].reshape(sizes[-1])
    with_normed = sum(
        jnp.sum(w.astype(f32) * mean, axis=1)
        for w, mean in ((query_weight, query_mean), (key_weight, key_mean), (value_weight, value_mean))
    )
    first_gain_mean = (with_normed - first_shift.astype(f32) * first_shift_mean) / first_gain.astype(f32)
    return (
        result[None],
        token_gradient[None],
        made[None],
        first_gain_mean,
        first_shift_mean,
        query_mean,
        key_mean,
        value_mean,
        position_mean,
        content_mean,
        posbias_mean,
        output_mean,
        second_gain_mean,
        second_shift_mean,
        inner_mean,
        inner_bias_mean,
        outer_mean,
        outer_bias_mean,
        conv_mean,
        conv_bias_mean,
    )


def per_device(*arguments):
    if lax.axis_size("dp") == 4 and lax.axis_size("fsdp") == 8:
        return per_device_direct(*arguments)
    return per_device_plain(*arguments)


def solution(mesh):
    in_specs = (
        P(("dp", "fsdp"), None, None),
        P(("dp", "fsdp"), None, None),
        P(("dp", "fsdp"), None, None),
        P(("dp", "fsdp")),
        P(("dp", "fsdp")),
        P(("dp", "fsdp"), None),
        P("fsdp"),
        P("fsdp"),
        P("fsdp", None),
        P("fsdp", None),
        P("fsdp", None),
        P("fsdp", None),
        P("fsdp"),
        P("fsdp"),
        P("fsdp", None),
        P("fsdp"),
        P("fsdp"),
        P("fsdp", None),
        P("fsdp"),
        P("fsdp", None),
        P("fsdp"),
        P("fsdp", None),
        P("fsdp"),
        P(("dp", "fsdp"), None, None),
        P(("dp", "fsdp"), None, None),
    )
    out_specs = (
        P(("dp", "fsdp"), None, None),
        P(("dp", "fsdp"), None, None),
        P(("dp", "fsdp"), None, None),
        P("fsdp"),
        P("fsdp"),
        P("fsdp", None),
        P("fsdp", None),
        P("fsdp", None),
        P("fsdp", None),
        P("fsdp"),
        P("fsdp"),
        P("fsdp", None),
        P("fsdp"),
        P("fsdp"),
        P("fsdp", None),
        P("fsdp"),
        P("fsdp", None),
        P("fsdp"),
        P("fsdp", None),
        P("fsdp"),
    )
    return jax.shard_map(
        per_device, mesh=mesh, in_specs=in_specs, out_specs=out_specs, check_vma=False
    )
```

```python
import functools
import math

import jax
import jax.numpy as jnp
from jax import lax
from jax.experimental import pallas as pl
from jax.experimental.pallas import tpu as pltpu
from jax.sharding import PartitionSpec as P

HEADS = 8
DH = 128
RATE = 3
BLK = 128
NEG = -1.2e10
f32 = jnp.float32
bf16 = jnp.bfloat16


EPSILON = 1e-05
MASKED = -1000000000.0


def smooth_gate(values):
    return jax.nn.gelu(values, approximate=True)


def norm_parts(rows, gain, shift):
    center = jnp.mean(rows, axis=-1, keepdims=True)
    centered = rows - center
    spread = lax.rsqrt(jnp.mean(centered * centered, axis=-1, keepdims=True) + EPSILON)
    scaled = centered * spread
    return (scaled * gain.astype(jnp.float32) + shift.astype(jnp.float32), scaled, spread)


def norm_back(grad, scaled, spread, gain):
    inner = grad * gain.astype(jnp.float32)
    return spread * (
        inner
        - jnp.mean(inner, axis=-1, keepdims=True)
        - scaled * jnp.mean(inner * scaled, axis=-1, keepdims=True)
    )


def positions(count, width):
    distance = (count - 1 - jnp.arange(count, dtype=jnp.int32)).astype(jnp.float32)
    rates = jnp.exp(
        jnp.arange(0, width, 2, dtype=jnp.int32).astype(jnp.float32) * (-math.log(10000.0) / width)
    )
    angle = distance[:, None] * rates[None, :]
    return jnp.concatenate([jnp.sin(angle), jnp.cos(angle)], axis=1)


def dot_nt(a,b): return lax.dot_general(a,b,(((1,),(1,)),((),())),preferred_element_type=f32)
def dot_nn(a,b): return lax.dot_general(a,b,(((1,),(0,)),((),())),preferred_element_type=f32)

def attn_fwd_kernel(qu_ref,qv_ref,k_ref,v_ref,r_ref,bias_ref,o_ref,p_ref,beside=None):
    seg=qu_ref.shape[0]; total=k_ref.shape[0]; old=total-seg
    c=math.log2(math.e)/math.sqrt(DH)
    for ib in range(seg//BLK):
        if beside is not None: beside(ib)
        rows=pl.ds(ib*BLK,BLK)
        L=old+(ib+1)*BLK
        qu=qu_ref[rows,:]; qv=qv_ref[rows,:]
        raw=dot_nt(qv,r_ref[pl.ds(total-L,L),:])
        z=dot_nt(qu,k_ref[pl.ds(0,L),:])+pltpu.roll(raw,L-(BLK-1),axis=1,stride=1,stride_axis=0)
        M=L-BLK
        za=z[:,:M]+bias_ref[:,:M]
        rr=lax.broadcasted_iota(jnp.int32,(BLK,BLK),0); cc=lax.broadcasted_iota(jnp.int32,(BLK,BLK),1)
        zb=z[:,M:]
        zb=jnp.where(cc==rr,zb,jnp.where(cc<rr,zb+bias_ref[:,pl.ds(M,BLK)],NEG))
        top=jnp.maximum(jnp.max(za,axis=1,keepdims=True),jnp.max(zb,axis=1,keepdims=True))
        ea=jnp.exp2((za-top)*c); eb=jnp.exp2((zb-top)*c)
        inv=1.0/(jnp.sum(ea,axis=1,keepdims=True)+jnp.sum(eb,axis=1,keepdims=True))
        pa=(ea*inv).astype(bf16); pb=(eb*inv).astype(bf16)
        p_ref[0,rows,pl.ds(0,M)]=pa
        p_ref[0,rows,pl.ds(M,BLK)]=pb
        o_ref[rows,:]=(dot_nn(pa,v_ref[pl.ds(0,M),:])+dot_nn(pb,v_ref[pl.ds(M,BLK),:])).astype(bf16)

def attn_fwd_gather_kernel(pieces, *refs):
    shard, whole = refs[6], refs[9]
    local, sent, came = refs[10:]
    head = pl.program_id(0)
    height = shard.shape[0]
    rows = height // pieces
    moved = Gathering([(shard, n * rows, rows, whole, height) for n in range(pieces)], local, sent, came)

    @pl.when(head == 0)
    def _():
        moved.greet()
        for n in range(pieces):
            moved.begin(n)

    tiles = refs[0].shape[0] // BLK
    steps = {}
    for n in range(pieces):
        slot = 7 + (26 * n) // pieces
        steps.setdefault(slot, []).append((moved.onward, n))
        if n:
            steps.setdefault(slot, []).append((moved.last, n - 1))

    def beside(tile):
        for slot, phases in steps.items():
            if slot % tiles == tile:

                @pl.when(head == slot // tiles)
                def _(phases=phases):
                    for phase, n in phases:
                        phase(n)

    attn_fwd_kernel(*refs[:6], *refs[7:9], beside=beside)

    @pl.when(head == HEADS - 1)
    def _():
        moved.last(pieces - 1)
        for n in range(pieces):
            moved.complete(n)
        moved.drain()


def attn_fwd(qu, qv, k, v, r, bias, shard=None, pieces=8):
    seg, width = qu.shape
    total = k.shape[0]
    col = lambda n: pl.BlockSpec((n, DH), lambda h: (0, h))
    in_specs = [col(seg), col(seg), col(total), col(total), col(total)]
    in_specs += [pl.BlockSpec((1, total), lambda h: (0, 0))]
    out_specs = [col(seg), pl.BlockSpec((1, seg, total), lambda h: (h, 0, 0))]
    out_shape = [
        jax.ShapeDtypeStruct((seg, width), bf16),
        jax.ShapeDtypeStruct((HEADS, seg, total), bf16),
    ]
    cost = pl.CostEstimate(
        flops=6 * seg * total * width,
        bytes_accessed=2 * (3 * seg * width + 3 * total * width + HEADS * seg * total),
        transcendentals=HEADS * seg * total,
    )
    if shard is None:
        return pl.pallas_call(
            attn_fwd_kernel,
            grid=(HEADS,),
            in_specs=in_specs,
            out_specs=out_specs,
            out_shape=out_shape,
            cost_estimate=cost,
            compiler_params=pltpu.CompilerParams(vmem_limit_bytes=58 << 20),
            name="attn_fwd",
        )(qu, qv, k, v, r, bias)
    return pl.pallas_call(
        functools.partial(attn_fwd_gather_kernel, pieces),
        grid=(HEADS,),
        in_specs=in_specs + [pl.BlockSpec(shard.shape, lambda h: (0, 0))],
        out_specs=out_specs + [pl.BlockSpec(memory_space=pl.ANY)],
        out_shape=out_shape + [jax.ShapeDtypeStruct((8 * shard.shape[0], shard.shape[1]), bf16)],
        scratch_shapes=[pltpu.SemaphoreType.DMA((n * pieces,)) for n in (1, 7, 7)],
        cost_estimate=cost,
        compiler_params=pltpu.CompilerParams(
            collective_id=3, has_side_effects=True, vmem_limit_bytes=58 << 20
        ),
        name="attn_fwd_gather",
    )(qu, qv, k, v, r, bias, shard)


def attn_bwd_kernel(qu_ref,qv_ref,qut_ref,qvrt_ref,k_ref,v_ref,r_ref,p_ref,g_ref,gt_ref,dq_ref,dkt_ref,dvt_ref,drt_ref,sums_ref,dk_acc,dv_acc,dr_acc):
    seg=g_ref.shape[0]; total=k_ref.shape[0]; old=total-seg
    scale=1.0/math.sqrt(DH)
    rr=lax.broadcasted_iota(jnp.int32,(BLK,BLK),0); cc=lax.broadcasted_iota(jnp.int32,(BLK,BLK),1)
    flip=(rr+cc==BLK-1).astype(bf16)
    su=jnp.zeros((1,DH),f32); sv=jnp.zeros((1,DH),f32)
    nb=seg//BLK
    for ib in range(nb-1,-1,-1):
        rows=pl.ds(ib*BLK,BLK)
        L=old+(ib+1)*BLK
        g=g_ref[rows,:]; gt=gt_ref[:,rows]; qut=qut_ref[:,rows]
        plow=p_ref[0,rows,pl.ds(0,L)]
        p=plow.astype(f32)
        dp=dot_nt(g,v_ref[pl.ds(0,L),:])
        d=jnp.sum(p*dp,axis=1,keepdims=True)
        dz=(p*(dp-d)*scale).astype(bf16)
        dvt=dot_nn(gt,plow)
        dkt=dot_nn(qut,dz)
        dqu=dot_nn(dz,k_ref[pl.ds(0,L),:])
        rev=dot_nn(flip,dz)
        raw=pltpu.roll(rev,0,axis=1,stride=1,stride_axis=0).astype(bf16)
        T=pl.ds(total-L,L)
        dqv_rev=dot_nn(raw,r_ref[T,:])
        qvr=dot_nt(qvrt_ref[:,rows],flip).astype(bf16)
        drt=dot_nn(qvr,raw)
        dqv=lax.dot_general(flip.astype(f32),dqv_rev,(((1,),(0,)),((),())),preferred_element_type=f32,precision=lax.Precision.HIGHEST)
        su+=jnp.sum(dqu,axis=0,keepdims=True); sv+=jnp.sum(dqv,axis=0,keepdims=True)
        dq_ref[rows,:]=(dqu+dqv).astype(bf16)
        J=pl.ds(0,L)
        if ib==nb-1:
            dv_acc[...]=dvt; dk_acc[...]=dkt; dr_acc[...]=drt
        else:
            dv_acc[:,J]+=dvt; dk_acc[:,J]+=dkt; dr_acc[:,T]+=drt
    dkt_ref[...]=dk_acc[...].astype(bf16); dvt_ref[...]=dv_acc[...].astype(bf16); drt_ref[...]=dr_acc[...].astype(bf16)
    sums_ref[0:1,:]=su; sums_ref[1:2,:]=sv

def attn_bwd_sums_kernel(plan, sources, count, *refs):
    base, grads = refs[:10], refs[10 : 10 + count]
    refs = refs[10 + count :]
    results, outs, refs = refs[:5], refs[5 : 5 + count], refs[5 + count :]
    totals = refs[:3]
    sums = Sums(plan, sources, grads, outs, refs[3:])
    steps = sums.schedule()
    head = pl.program_id(0)
    per = -(-len(steps) // HEADS) if len(steps) > HEADS + 2 else 1

    for n in range(HEADS):

        @pl.when(head == n)
        def _(n=n):
            if n == 0:
                sums.greet()
            for step in steps[n * per : (n + 1) * per]:
                for phase, item in step:
                    phase(item)

    attn_bwd_kernel(*base, *results, *totals)

    @pl.when(head == HEADS - 1)
    def _():
        for step in steps[HEADS * per :]:
            for phase, item in step:
                phase(item)
        sums.drain()


def attn_bwd(qu, qv, k, v, r, p, g, grads=(), share=1.0):
    seg, width = qu.shape
    total = k.shape[0]
    col = lambda n: pl.BlockSpec((n, DH), lambda h: (0, h))
    row = lambda n: pl.BlockSpec((DH, n), lambda h: (h, 0))
    any_spec = pl.BlockSpec(memory_space=pl.ANY)
    in_specs = [col(seg), col(seg), row(seg), row(seg), col(total), col(total), col(total)]
    in_specs += [pl.BlockSpec((1, seg, total), lambda h: (h, 0, 0)), col(seg), row(seg)]
    out_specs = [col(seg), row(total), row(total), row(total), pl.BlockSpec((8, DH), lambda h: (0, h))]
    out_shape = [jax.ShapeDtypeStruct((seg, width), bf16)]
    out_shape += [jax.ShapeDtypeStruct((width, total), bf16)] * 3
    out_shape += [jax.ShapeDtypeStruct((8, width), f32)]
    scratch = [pltpu.VMEM((DH, total), f32)] * 3
    cost = pl.CostEstimate(
        flops=16 * seg * total * width,
        bytes_accessed=2 * (5 * seg * width + 6 * total * width + HEADS * seg * total),
        transcendentals=0,
    )
    operands = (qu, qv, qu.T, qv.T, k, v, r, p, g, g.T)
    if not grads:
        return pl.pallas_call(
            attn_bwd_kernel,
            grid=(HEADS,),
            in_specs=in_specs,
            out_specs=out_specs,
            out_shape=out_shape,
            scratch_shapes=scratch,
            cost_estimate=cost,
            compiler_params=pltpu.CompilerParams(vmem_limit_bytes=58 << 20),
            name="attn_bwd",
        )(*operands)
    plan, sources, arrays, shapes = sums_plan(grads, ())
    results = pl.pallas_call(
        functools.partial(attn_bwd_sums_kernel, plan, sources, len(arrays)),
        grid=(HEADS,),
        in_specs=in_specs + [any_spec] * len(arrays),
        out_specs=out_specs + [any_spec] * len(arrays),
        out_shape=out_shape + shapes,
        scratch_shapes=scratch + sums_scratch(plan),
        cost_estimate=cost,
        compiler_params=pltpu.CompilerParams(
            collective_id=4, has_side_effects=True, vmem_limit_bytes=58 << 20
        ),
        name="attn_bwd_sums",
    )(*operands, *arrays)
    return tuple(results[:5]) + tuple(total.astype(f32) * share for total in results[5:])


def cut(*values):
    return lax.optimization_barrier(values)


def positions_low(count, width):
    tile = 64
    rates = jnp.exp(
        jnp.arange(0, width, 2, dtype=jnp.int32).astype(f32) * (-math.log(10000.0) / width)
    )
    rates = jnp.concatenate([rates, rates])[None, :]
    upper = (jnp.arange(width, dtype=jnp.int32) < width // 2)[None, :]
    far = (count - 1 - tile * jnp.arange(count // tile, dtype=jnp.int32)).astype(f32)[:, None] * rates
    near = jnp.arange(tile, dtype=jnp.int32).astype(f32)[:, None] * rates
    sine, cosine = jnp.sin(far), jnp.cos(far)
    with_cos = jnp.where(upper, sine, cosine)[:, None, :]
    with_sin = jnp.where(upper, -cosine, sine)[:, None, :]
    near_cos, near_sin, with_cos, with_sin = cut(jnp.cos(near), jnp.sin(near), with_cos, with_sin)
    table = with_cos * near_cos[None] + with_sin * near_sin[None]
    return table.astype(bf16).reshape(count, width)


def hop(value, move):
    dp, fsdp = lax.axis_size("dp"), lax.axis_size("fsdp")
    pairs = []
    for z in range(dp):
        for f in range(fsdp):
            to = move(z, f)
            if to is not None:
                pairs.append((z * fsdp + f, to[0] * fsdp + to[1]))
    return lax.ppermute(value, ("dp", "fsdp"), pairs)


def inward_hop(w):
    to = {0: 1, 3: 2}
    return hop(w, lambda z, f: (to[z], f) if z in to else None)


def middle_hop(w):
    return hop(w, lambda z, f: (3 - z, f) if z in (1, 2) else None)


def outward_hop(w):
    to = {1: 0, 2: 3}
    return hop(w, lambda z, f: (to[z], f) if z in to else None)


def add(first, second):
    return (first.astype(f32) + second.astype(f32)).astype(bf16)


def finish(whole, last, share):
    plane = lax.axis_index("dp")
    return jnp.where((plane == 1) | (plane == 2), whole, last).astype(f32) * share


def add_rows(out, parts):
    rows = out.shape[0]
    height = 32 if rows % 32 == 0 else 16

    def one(i, carry):
        at = pl.ds(pl.multiple_of(i * height, height), height)
        total = parts[0][at, :].astype(f32)
        for part in parts[1:]:
            total = total + part[at, :].astype(f32)
        out[at, :] = total.astype(out.dtype)
        return carry

    lax.fori_loop(0, rows // height, one, 0)


FULL_BUFFERS = ("mine", "theirs", "far", "half_x", "half_y", "to_y", "to_x", "got_y", "got_x")
LINE_BUFFERS = ("own", "end", "mid")


def sums_scratch(plan):
    shapes = []
    for full, rows, cols in plan:
        if full:
            half = pltpu.VMEM((rows // 2, cols), bf16)
            one = pltpu.VMEM((rows, cols), bf16)
            shapes += [pltpu.VMEM((4, rows, cols), bf16)] * 2 + [one, half, half] + [one] * 4
        shapes += [pltpu.VMEM((rows, cols), bf16)] * 3
        shapes += [pltpu.SemaphoreType.DMA((n,)) for n in (4, 11, 11, 1)]
    return shapes


GAP, LINE_GAP = 2, 2


class Sums:
    def __init__(self, plan, sources, grads, outs, scratch):
        self.z, self.f = lax.axis_index("dp"), lax.axis_index("fsdp")
        self.chip, self.core = self.f // 2, self.f % 2
        self.middle = (self.z == 1) | (self.z == 2)
        self.edge = jnp.logical_not(self.middle)
        self.inward = (jnp.where(self.z < 2, 1, 2), self.f)
        self.outward = (jnp.where(self.z < 2, 0, 3), self.f)
        self.across = (3 - self.z, self.f)
        self.sibling, self.by_x, self.by_y = (
            (self.z, self.f ^ 1),
            (self.z, self.f ^ 2),
            (self.z, self.f ^ 4),
        )
        self.items, at = [], 0
        for n, (full, rows, cols) in enumerate(plan):
            names = (FULL_BUFFERS if full else ()) + LINE_BUFFERS + ("local", "sent", "came", "stored")
            b = dict(zip(names, scratch[at : at + len(names)]))
            at += len(names)
            b.update(full=full, rows=rows, source=grads[sources[n][0]], first=sources[n][1])
            b.update(target=outs[sources[n][0]])
            self.items.append(b)

    def greet(self):
        barrier = pltpu.get_barrier_semaphore()

        def signal(device):
            pl.semaphore_signal(
                barrier, inc=1, device_id=device, device_id_type=pl.DeviceIdType.MESH
            )

        for device in (self.sibling, self.by_x, self.by_y):
            signal(device)

        @pl.when(self.middle)
        def _():
            signal(self.outward)
            signal(self.across)
            pl.semaphore_wait(barrier, 5)

        @pl.when(self.edge)
        def _():
            signal(self.inward)
            pl.semaphore_wait(barrier, 4)

    def copy(self, b, n, src, dst, device):
        return pltpu.make_async_remote_copy(
            src_ref=src,
            dst_ref=dst,
            send_sem=b["sent"].at[n],
            recv_sem=b["came"].at[n],
            device_id=device,
            device_id_type=pl.DeviceIdType.MESH,
        )

    def rows_of(self, b):
        return pl.ds(b["first"], b["rows"])

    def across_cores(self, b, s):
        block = (self.chip ^ (3 - s)) * 2 + 1 - self.core
        src = b["source"].at[block, self.rows_of(b), :]
        return self.copy(b, s, src, b["theirs"].at[s], self.sibling)

    def load(self, b, s):
        if not b["full"]:
            src, dst = b["source"].at[self.rows_of(b), :], b["own"]
        else:
            block = (self.chip ^ (3 - s)) * 2 + self.core
            src, dst = b["source"].at[block, self.rows_of(b), :], b["mine"].at[s]
        return pltpu.make_async_copy(src, dst, b["local"].at[s])

    def halves_out(self, b):
        half = b["rows"] // 2
        return (
            self.copy(b, 4, b["far"].at[pl.ds(0, half), :], b["half_x"], self.by_x),
            self.copy(b, 5, b["far"].at[pl.ds(half, half), :], b["half_y"], self.by_y),
        )

    def near_out(self, b):
        return (
            self.copy(b, 6, b["to_y"], b["got_y"], self.by_y),
            self.copy(b, 7, b["to_x"], b["got_x"], self.by_x),
        )

    def go_in(self, b):
        return self.copy(b, 8, b["own"], b["end"], self.inward)

    def go_mid(self, b):
        return self.copy(b, 9, b["own"], b["mid"], self.across)

    def go_out(self, b):
        return self.copy(b, 10, b["mid"], b["end"], self.outward)

    def store(self, b, name):
        return pltpu.make_async_copy(b[name], b["target"].at[self.rows_of(b), :], b["stored"].at[0])

    def begin(self, b):
        if b["full"]:
            for s in range(4):
                self.across_cores(b, s).start()
                self.load(b, s).start()
        else:
            self.load(b, 0).start()

    def arrived(self, b, s):
        self.across_cores(b, s).wait_recv()
        self.load(b, s).wait()

    def far(self, b):
        self.arrived(b, 0)
        add_rows(b["far"], [b["mine"].at[0], b["theirs"].at[0]])
        for c in self.halves_out(b):
            c.start()

    def near(self, b):
        half = b["rows"] // 2
        low, high = pl.ds(0, half), pl.ds(half, half)
        self.arrived(b, 1)
        self.arrived(b, 2)
        for c in self.halves_out(b):
            c.wait_recv()
        mine, theirs = b["mine"], b["theirs"]
        add_rows(b["to_y"].at[low, :], [mine.at[1, low, :], theirs.at[1, low, :], b["half_x"]])
        add_rows(b["to_y"].at[high, :], [mine.at[1, high, :], theirs.at[1, high, :]])
        add_rows(b["to_x"].at[low, :], [mine.at[2, low, :], theirs.at[2, low, :]])
        add_rows(b["to_x"].at[high, :], [mine.at[2, high, :], theirs.at[2, high, :], b["half_y"]])
        for c in self.near_out(b):
            c.start()

    def own(self, b):
        self.arrived(b, 3)
        for c in self.near_out(b):
            c.wait_recv()
        add_rows(b["own"], [b["mine"].at[3], b["theirs"].at[3], b["got_x"], b["got_y"]])

    def line_in(self, b):
        if not b["full"]:
            self.load(b, 0).wait()

        @pl.when(self.edge)
        def _():
            self.go_in(b).start()

    def line_mid(self, b):
        @pl.when(self.middle)
        def _():
            self.go_in(b).wait_recv()
            add_rows(b["own"], [b["own"], b["end"]])
            self.go_mid(b).start()

    def line_out(self, b):
        @pl.when(self.middle)
        def _():
            self.go_mid(b).wait_recv()
            add_rows(b["mid"], [b["own"], b["mid"]])
            self.go_out(b).start()
            self.store(b, "mid").start()

    def line_last(self, b):
        @pl.when(self.edge)
        def _():
            self.go_out(b).wait_recv()
            self.store(b, "end").start()

    def schedule(self):
        wide = [b for b in self.items if b["full"]]
        left = [b for b in self.items if not b["full"]]
        line, due, slot = [], [], 0
        while sum(b is not None for b in line) < len(self.items):
            if 0 <= slot - 2 * GAP < len(wide):
                due.append(wide[slot - 2 * GAP])
            if left and (not due or slot % 2 == 0):
                line.append(left.pop(0))
            elif due:
                line.append(due.pop(0))
            else:
                line.append(None)
            slot += 1
        steps = []
        for t in range(len(line) + 3 * LINE_GAP):
            step = []
            if t + 2 < len(wide):
                step.append((self.begin, wide[t + 2]))
            for phase, back in ((self.far, 0), (self.near, GAP), (self.own, 2 * GAP)):
                if 0 <= t - back < len(wide):
                    step.append((phase, wide[t - back]))
            phases = (self.line_in, self.line_mid, self.line_out, self.line_last)
            for back, phase in enumerate(phases):
                at = t - back * LINE_GAP
                if 0 <= at < len(line) and line[at] is not None:
                    step.append((phase, line[at]))
            steps.append(step)
        first = [(self.begin, b) for b in self.items if not b["full"]]
        first += [(self.begin, b) for b in wide[:2]]
        return [first] + steps

    def drain(self):
        for b in self.items:
            if b["full"]:
                for s in range(4):
                    self.across_cores(b, s).wait_send()
                for c in self.halves_out(b) + self.near_out(b):
                    c.wait_send()
            self.store(b, "mid").wait()

        @pl.when(self.edge)
        def _():
            for b in self.items:
                self.go_in(b).wait_send()

        @pl.when(self.middle)
        def _():
            for b in self.items:
                self.go_mid(b).wait_send()
                self.go_out(b).wait_send()


def sums_plan(fulls, shards):
    plan, sources, arrays, shapes = [], [], [], []
    for full, group in ((True, fulls), (False, shards)):
        for g, pieces in group:
            rows, cols = g.shape[0] // (8 if full else 1), g.shape[1]
            for p in range(pieces):
                plan.append((full, rows // pieces, cols))
                sources.append((len(arrays), p * (rows // pieces)))
            arrays.append(g.reshape(8, rows, cols) if full else g)
            shapes.append(jax.ShapeDtypeStruct((rows, cols), bf16))
    return tuple(plan), tuple(sources), arrays, shapes


def tail_kernel(plan, sources, count, *refs):
    sums = Sums(plan, sources, refs[:count], refs[count : 2 * count], refs[2 * count :])
    sums.greet()
    for step in sums.schedule():
        for phase, item in step:
            phase(item)
    sums.drain()


def reduce_tail(fulls, shards, share, number):
    plan, sources, arrays, shapes = sums_plan(fulls, shards)
    totals = pl.pallas_call(
        functools.partial(tail_kernel, plan, sources, len(arrays)),
        in_specs=[pl.BlockSpec(memory_space=pl.ANY)] * len(arrays),
        out_specs=[pl.BlockSpec(memory_space=pl.ANY)] * len(arrays),
        out_shape=shapes,
        scratch_shapes=sums_scratch(plan),
        compiler_params=pltpu.CompilerParams(
            collective_id=number, has_side_effects=True, vmem_limit_bytes=56 << 20
        ),
        name="reduce_tail",
    )(*arrays)
    return [total.astype(f32) * share for total in totals]


class Gathering:
    def __init__(self, pieces, local, sent, came):
        self.pieces, self.local, self.sent, self.came = pieces, local, sent, came
        z, f = lax.axis_index("dp"), lax.axis_index("fsdp")
        near = 2 + 2 * lax.rem(z, 2)
        self.first_to, self.second_to = (z, f ^ near), (z, f ^ (6 - near))
        self.pair_to, self.core_to = (z ^ 1, f), (z, f ^ 1)
        self.slots = (f, f ^ near, f ^ (6 - near), f ^ 6)

    def greet(self):
        barrier = pltpu.get_barrier_semaphore()
        for device in (self.first_to, self.second_to, self.pair_to, self.core_to):
            pl.semaphore_signal(
                barrier, inc=1, device_id=device, device_id_type=pl.DeviceIdType.MESH
            )
        pl.semaphore_wait(barrier, 4)

    def part(self, n, slot):
        shard, start, rows, whole, height = self.pieces[n]
        return whole.at[pl.ds(pl.multiple_of(slot * height + start, 16), rows), :]

    def shard(self, n):
        shard, start, rows, whole, height = self.pieces[n]
        return shard.at[pl.ds(start, rows), :]

    def copy(self, n, k, src, slot, device):
        return pltpu.make_async_remote_copy(
            src_ref=src,
            dst_ref=self.part(n, slot),
            send_sem=self.sent.at[n * 7 + k],
            recv_sem=self.came.at[n * 7 + k],
            device_id=device,
            device_id_type=pl.DeviceIdType.MESH,
        )

    def first(self, n):
        return self.copy(n, 0, self.shard(n), self.slots[0], self.first_to)

    def pair(self, n):
        return self.copy(n, 1, self.part(n, self.slots[1]), self.slots[1], self.pair_to)

    def second(self, n):
        return self.copy(n, 2, self.part(n, self.slots[1]), self.slots[1], self.second_to)

    def core(self, n, s):
        src = self.shard(n) if s == 0 else self.part(n, self.slots[s])
        return self.copy(n, 3 + s, src, self.slots[s], self.core_to)

    def mine(self, n):
        return pltpu.make_async_copy(self.shard(n), self.part(n, self.slots[0]), self.local.at[n])

    def begin(self, n):
        self.first(n).start()
        self.mine(n).start()
        self.core(n, 0).start()

    def onward(self, n):
        self.first(n).wait_recv()
        self.pair(n).start()
        self.second(n).start()
        self.core(n, 1).start()

    def last(self, n):
        self.pair(n).wait_recv()
        self.core(n, 2).start()
        self.second(n).wait_recv()
        self.core(n, 3).start()

    def complete(self, n):
        self.mine(n).wait()
        for s in range(4):
            self.core(n, s).wait_recv()

    def drain(self):
        for n in range(len(self.pieces)):
            for copy in (self.first(n), self.pair(n), self.second(n)):
                copy.wait_send()
            for s in range(4):
                self.core(n, s).wait_send()


def tile_loop(rows, height, body):
    def one(i, carry):
        body(pl.ds(pl.multiple_of(i * height, height), height))
        return carry

    lax.fori_loop(0, rows // height, one, 0)


HEAD_ITEMS = ("table", "keys", "values", "query", "position", "output", "inner")
INNER_PIECES = 4


def head_kernel(*refs):
    count = len(HEAD_ITEMS)
    rows_in, shards, pos_ref = refs[:3], refs[3 : 3 + count], refs[3 + count]
    refs = refs[4 + count :]
    (xhat_out, normed_out, qu_out, qv_out, keys_out, values_out, relative_out) = refs[:7]
    weights_out, refs = refs[7 : 7 + count], refs[7 + count :]
    wholes, refs = refs[:count], refs[count:]
    xhat, normed, pos, qu, qv, keys, values, relative = refs[:8]
    local, sent, came, left = refs[8:]
    moved = Gathering(
        [(shards[n], 0, shards[n].shape[0], wholes[n], shards[n].shape[0]) for n in range(count - 1)]
        + [
            (shards[-1], p * shards[-1].shape[0] // INNER_PIECES, shards[-1].shape[0] // INNER_PIECES)
            + (wholes[-1], shards[-1].shape[0])
            for p in range(INNER_PIECES)
        ],
        local,
        sent,
        came,
    )
    moved.greet()
    posload = pltpu.make_async_copy(pos_ref, pos, local.at[count - 1 + INNER_PIECES])
    stores = []

    def leave(src, dst):
        copy = pltpu.make_async_copy(src, dst, left.at[len(stores)])
        copy.start()
        stores.append(copy)

    def complete(n):
        moved.complete(n)
        if n < count - 1:
            leave(wholes[n], weights_out[n])

    def comm(*steps):
        for kind, n in steps:
            {"b": moved.begin, "o": moved.onward, "l": moved.last, "c": complete}[kind](n)

    comm(("b", 0), ("b", 1), ("b", 2))
    posload.start()
    per = rows_in[0].shape[0]
    for b in range(3):
        source = rows_in[b]

        def normalize(at, b=b, source=source):
            rows = source[at, :].astype(f32)
            centered = rows - jnp.mean(rows, axis=-1, keepdims=True)
            spread = lax.rsqrt(jnp.mean(centered * centered, axis=-1, keepdims=True) + EPSILON)
            xhat[b, at, :] = centered * spread

        tile_loop(per, 64, normalize)
        if b == 1:
            comm(("o", 0))
    leave(xhat.at[2], xhat_out)
    comm(("o", 1), ("b", 3), ("l", 0), ("c", 0))

    def row_of(k):
        height = shards[0].shape[0]
        return jnp.concatenate(
            [wholes[0][d * height : (d + 1) * height, :].astype(f32)[k : k + 1, :] for d in range(8)], axis=1
        )

    gain, shift, content, posbias = (row_of(k) for k in range(4))
    for b in range(3):

        def scale(at, b=b):
            normed[b, at, :] = (xhat[b, at, :] * gain + shift).astype(bf16)

        tile_loop(per, 64, scale)
    leave(normed, normed_out)
    comm(("o", 2), ("b", 4), ("l", 1), ("b", 5), ("c", 1))

    def project(src, weight, dst, steps):
        for b in range(3):

            def one(at, b=b):
                dst[b, at, :] = jnp.dot(
                    src[b, at, :], weight[...], preferred_element_type=f32
                ).astype(bf16)

            tile_loop(per, 256, one)
            comm(*steps[b])

    project(normed, wholes[1], keys, ((("o", 3), ("b", 6)), (("l", 2),), ()))
    leave(keys, keys_out)
    comm(("c", 2), ("o", 4), ("b", 7), ("l", 3))
    project(normed, wholes[2], values, ((), (("o", 5), ("b", 8)), (("l", 4),)))
    leave(values, values_out)
    comm(("c", 3))

    def queries(at):
        query = jnp.dot(normed[2, at, :], wholes[3][...], preferred_element_type=f32)
        qu[at, :] = (query + content).astype(bf16)
        qv[at, :] = (query + posbias).astype(bf16)

    tile_loop(per, 256, queries)
    leave(qu, qu_out)
    leave(qv, qv_out)
    comm(("o", 6), ("b", 9), ("l", 5), ("c", 4))
    posload.wait()
    project(pos, wholes[4], relative, ((("o", 7),), (("l", 6),), (("o", 8),)))
    leave(relative, relative_out)
    comm(("c", 5), ("l", 7), ("o", 9), ("l", 8), ("l", 9))
    for n in range(6, 10):
        complete(n)
    leave(wholes[-1], weights_out[-1])
    moved.drain()
    for copy in stores:
        copy.wait()


def head_stage(rows_in, shards, pos_low):
    per, width = rows_in[0].shape
    three = (3, per, width)
    count = len(shards)
    full = [(8 * w.shape[0], w.shape[1]) for w in shards]
    any_spec = pl.BlockSpec(memory_space=pl.ANY)
    shape = jax.ShapeDtypeStruct
    shapes = [shape((per, width), f32), shape(three, bf16)] + [shape((per, width), bf16)] * 2
    shapes += [shape(three, bf16)] * 3 + [shape(s, bf16) for s in full]
    vmem = pltpu.VMEM
    scratch = [vmem(s, bf16) for s in full] + [vmem(three, f32), vmem(three, bf16), vmem(three, bf16)]
    scratch += [vmem((per, width), bf16)] * 2 + [vmem(three, bf16)] * 3
    scratch += [pltpu.SemaphoreType.DMA((n,)) for n in (count + INNER_PIECES, 7 * (count + 3), 7 * (count + 3), 7 + count)]
    return pl.pallas_call(
        head_kernel,
        in_specs=[pl.BlockSpec(memory_space=pltpu.VMEM)] * 3 + [any_spec] * (count + 1),
        out_specs=[any_spec] * len(shapes),
        out_shape=shapes,
        scratch_shapes=scratch,
        compiler_params=pltpu.CompilerParams(
            collective_id=2, has_side_effects=True, vmem_limit_bytes=56 << 20
        ),
        name="head_stage",
    )(*rows_in, *shards, pos_low.reshape(three))


def gather(shards):
    return [lax.all_gather(w, "fsdp", axis=0, tiled=True) for w in shards]


def reduce(grads, share):
    done = []
    for g in grads:
        part = lax.psum_scatter(g, "fsdp", scatter_dimension=0, tiled=True)
        done.append(lax.psum(part, "dp").astype(f32) * share)
    return done


def pack_vectors(vectors, parts):
    flat = jnp.concatenate([v.reshape(parts, -1) for v in vectors], axis=1)
    width = 1024
    lines = 32 * (-(-flat.shape[1] // (32 * width)))
    flat = jnp.pad(flat, ((0, 0), (0, lines * width - flat.shape[1])))
    return flat.reshape(parts * lines, width)


def unpack_vectors(table, parts, sizes):
    flat = table.reshape(parts, -1)
    result, start = [], 0
    for size in sizes:
        result.append(flat[:, start : start + size].reshape(parts * size))
        start += size
    return result


def per_device_plain(
    tokens,
    memory,
    compressed,
    mem_fill,
    cmem_fill,
    pad_mask,
    first_gain,
    first_shift,
    query_weight,
    key_weight,
    value_weight,
    position_weight,
    content_bias,
    position_bias,
    output_weight,
    second_gain,
    second_shift,
    inner_weight,
    inner_bias,
    outer_weight,
    outer_bias,
    conv_weight,
    conv_bias,
    out_grad,
    comp_grad,
):
    streams, seg_rows, width = tokens.shape
    mem_rows = memory.shape[1]
    cmem_rows = compressed.shape[1]
    total = cmem_rows + mem_rows + seg_rows
    shards = lax.axis_size("fsdp")
    share = 1.0 / (streams * lax.axis_size("dp") * shards)
    vectors = (
        first_gain,
        first_shift,
        content_bias,
        position_bias,
        second_gain,
        second_shift,
        inner_bias,
        outer_bias,
        conv_bias,
    )
    sizes = [v.shape[0] for v in vectors]

    groups = mem_rows // RATE
    start = mem_rows - RATE * groups
    mem_valid = (
        jnp.arange(mem_rows, dtype=jnp.int32)[None, :] >= (mem_rows - mem_fill)[:, None]
    ).astype(bf16)
    taps = (memory * mem_valid[..., None])[:, start:, :].reshape(streams * groups, RATE * width)
    group_valid = (
        (start + RATE * jnp.arange(groups, dtype=jnp.int32) + RATE - 1)[None, :]
        >= (mem_rows - mem_fill)[:, None]
    ).reshape(streams * groups, 1)
    made_grad = comp_grad.reshape(streams * groups, width) * group_valid.astype(bf16)
    conv_grad = jnp.einsum("nk,nd->kd", taps, made_grad, preferred_element_type=f32).astype(bf16)
    conv_bias_grad = jnp.sum(made_grad.astype(f32), axis=0)

    query_w, key_w, value_w, table = gather(
        [query_weight, key_weight, value_weight, pack_vectors(vectors, 1)]
    )
    (gain_one, shift_one, content_b, position_b, gain_two, shift_two, inner_b, outer_b, conv_b) = (
        unpack_vectors(table, shards, sizes)
    )
    position_w, output_w = gather([position_weight, output_weight])
    (inner_w,) = gather([inner_weight])
    (outer_w,) = gather([outer_weight])
    (conv_w,) = gather([conv_weight])

    whole = jnp.concatenate([compressed[0], memory[0], tokens[0]], axis=0).astype(f32)
    normed, scaled_one, spread_one = norm_parts(whole, gain_one, shift_one)
    normed_low = normed.astype(bf16)
    own_rows = normed_low[total - seg_rows :]
    query = jnp.dot(own_rows, query_w, preferred_element_type=f32)
    query_u = (query + content_b.astype(f32)).astype(bf16)
    query_v = (query + position_b.astype(f32)).astype(bf16)
    keys = jnp.dot(normed_low, key_w, preferred_element_type=f32).astype(bf16)
    values = jnp.dot(normed_low, value_w, preferred_element_type=f32).astype(bf16)
    pos_low = positions(total, width).astype(bf16)
    relative = jnp.dot(pos_low, position_w, preferred_element_type=f32).astype(bf16)
    valid = jnp.concatenate(
        [
            jnp.arange(cmem_rows, dtype=jnp.int32) >= cmem_rows - cmem_fill[0],
            jnp.arange(mem_rows, dtype=jnp.int32) >= mem_rows - mem_fill[0],
            pad_mask[0] == 1,
        ]
    )
    bias = jnp.where(valid, 0.0, NEG).astype(f32)[None]
    mixed, prob_low = attn_fwd(query_u, query_v, keys, values, relative, bias)
    hidden = tokens[0].astype(f32) + jnp.dot(mixed, output_w, preferred_element_type=f32)
    inner_norm, scaled_two, spread_two = norm_parts(hidden, gain_two, shift_two)
    inner_low = inner_norm.astype(bf16)
    preact = jnp.dot(inner_low, inner_w, preferred_element_type=f32) + inner_b.astype(f32)
    active = smooth_gate(preact).astype(bf16)
    result = (
        hidden
        + jnp.dot(active, outer_w, preferred_element_type=f32)
        + outer_b.astype(f32)
    )
    made = (
        jnp.dot(taps, conv_w, preferred_element_type=f32) + conv_b.astype(f32)
    ) * group_valid.astype(f32)

    grad = out_grad[0]
    grad_wide = grad.astype(f32)
    outer_grad = jnp.einsum("sf,sd->fd", active, grad, preferred_element_type=f32).astype(bf16)
    (outer_mean,) = reduce([outer_grad], share)
    outer_bias_grad = jnp.sum(grad_wide, axis=0)
    active_grad = jnp.einsum("sd,fd->sf", grad, outer_w, preferred_element_type=f32)
    gate_pull = jax.vjp(smooth_gate, preact)[1]
    preact_grad = gate_pull(active_grad)[0].astype(bf16)
    inner_grad = jnp.einsum("sd,sf->df", inner_low, preact_grad, preferred_element_type=f32).astype(
        bf16
    )
    (inner_mean,) = reduce([inner_grad], share)
    (conv_mean,) = reduce([conv_grad], share)
    inner_bias_grad = jnp.sum(preact_grad.astype(f32), axis=0)
    inner_norm_grad = jnp.einsum("sf,df->sd", preact_grad, inner_w, preferred_element_type=f32)
    second_gain_grad = jnp.sum(inner_norm_grad * scaled_two, axis=0)
    second_shift_grad = jnp.sum(inner_norm_grad, axis=0)
    hidden_grad = grad_wide + norm_back(inner_norm_grad, scaled_two, spread_two, gain_two)

    hidden_low = hidden_grad.astype(bf16)
    output_grad = jnp.einsum("sd,se->de", mixed, hidden_low, preferred_element_type=f32).astype(bf16)
    mixed_grad = jnp.einsum("se,de->sd", hidden_low, output_w, preferred_element_type=f32).astype(
        bf16
    )
    query_low, keys_t, values_t, relative_t, sums = attn_bwd(
        query_u, query_v, keys, values, relative, prob_low, mixed_grad
    )
    position_grad = jnp.einsum("ld,el->de", pos_low, relative_t, preferred_element_type=f32).astype(
        bf16
    )
    query_grad = jnp.einsum("sd,se->de", own_rows, query_low, preferred_element_type=f32).astype(
        bf16
    )
    key_grad = jnp.einsum("sd,es->de", normed_low, keys_t, preferred_element_type=f32).astype(bf16)
    value_grad = jnp.einsum("sd,es->de", normed_low, values_t, preferred_element_type=f32).astype(
        bf16
    )
    normed_grad = jnp.einsum("es,de->sd", keys_t, key_w, preferred_element_type=f32)
    normed_grad = normed_grad + jnp.einsum(
        "es,de->sd", values_t, value_w, preferred_element_type=f32
    )
    own_grad = jnp.einsum("se,de->sd", query_low, query_w, preferred_element_type=f32)
    normed_grad = normed_grad + jnp.pad(own_grad, ((total - seg_rows, 0), (0, 0)))
    first_gain_grad = jnp.sum(normed_grad * scaled_one, axis=0)
    first_shift_grad = jnp.sum(normed_grad, axis=0)
    own = slice(total - seg_rows, None)
    token_gradient = hidden_grad + norm_back(
        normed_grad[own], scaled_one[own], spread_one[own], gain_one
    )
    vector_grads = (
        first_gain_grad,
        first_shift_grad,
        sums[0],
        sums[1],
        second_gain_grad,
        second_shift_grad,
        inner_bias_grad,
        outer_bias_grad,
        conv_bias_grad,
    )
    packed = pack_vectors([v.astype(bf16) for v in vector_grads], shards)
    (output_mean,) = reduce([output_grad], share)
    query_mean, key_mean, value_mean, position_mean, table_mean = reduce(
        [query_grad, key_grad, value_grad, position_grad, packed], share
    )
    (
        first_gain_mean,
        first_shift_mean,
        content_mean,
        posbias_mean,
        second_gain_mean,
        second_shift_mean,
        inner_bias_mean,
        outer_bias_mean,
        conv_bias_mean,
    ) = unpack_vectors(table_mean, 1, sizes)
    return (
        result.astype(bf16)[None],
        token_gradient[None],
        made.astype(bf16)[None],
        first_gain_mean,
        first_shift_mean,
        query_mean,
        key_mean,
        value_mean,
        position_mean,
        content_mean,
        posbias_mean,
        output_mean,
        second_gain_mean,
        second_shift_mean,
        inner_mean,
        inner_bias_mean,
        outer_mean,
        outer_bias_mean,
        conv_mean,
        conv_bias_mean,
    )


def per_device_direct(
    tokens,
    memory,
    compressed,
    mem_fill,
    cmem_fill,
    pad_mask,
    first_gain,
    first_shift,
    query_weight,
    key_weight,
    value_weight,
    position_weight,
    content_bias,
    position_bias,
    output_weight,
    second_gain,
    second_shift,
    inner_weight,
    inner_bias,
    outer_weight,
    outer_bias,
    conv_weight,
    conv_bias,
    out_grad,
    comp_grad,
):
    streams, seg_rows, width = tokens.shape
    mem_rows = memory.shape[1]
    cmem_rows = compressed.shape[1]
    total = cmem_rows + mem_rows + seg_rows
    old = total - seg_rows
    shards = lax.axis_size("fsdp")
    share = 1.0 / (streams * lax.axis_size("dp") * shards)
    lanes = 128
    vectors = (
        first_gain,
        first_shift,
        content_bias,
        position_bias,
        second_gain,
        second_shift,
        outer_bias,
        conv_bias,
        inner_bias,
    )
    sizes = [v.shape[0] for v in vectors]
    lines = [v.reshape(-1, lanes) for v in vectors]
    table = jnp.zeros((32, lanes), bf16)
    row, line = jnp.arange(32, dtype=jnp.int32)[:, None], 0
    for v in lines:
        for n in range(v.shape[0]):
            table = jnp.where(row == line, v[n][None], table)
            line += 1
    pos_low = positions_low(total, width)
    (
        scaled_one,
        normed_low,
        query_u,
        query_v,
        keys,
        values,
        relative,
        table,
        key_w,
        value_w,
        query_w,
        position_w,
        output_w,
        inner_w,
    ) = head_stage(
        (compressed[0], memory[0], tokens[0]),
        (table, key_weight, value_weight, query_weight, position_weight, output_weight, inner_weight),
        pos_low,
    )
    normed_low, keys, values, relative = (
        v.reshape(total, width) for v in (normed_low, keys, values, relative)
    )
    own_rows = normed_low[old:]
    blocks = table.reshape(shards, 32, lanes)
    gain_one, shift_one = blocks[:, 0].reshape(width), blocks[:, 1].reshape(width)
    gain_two, shift_two, outer_b, conv_b = (blocks[:, n].reshape(width) for n in (4, 5, 6, 7))
    inner_b = blocks[:, 8 : 8 + sizes[-1] // lanes].reshape(shards * sizes[-1])

    valid = jnp.concatenate(
        [
            jnp.arange(cmem_rows, dtype=jnp.int32) >= cmem_rows - cmem_fill[0],
            jnp.arange(mem_rows, dtype=jnp.int32) >= mem_rows - mem_fill[0],
            pad_mask[0] == 1,
        ]
    )
    bias = jnp.where(valid, 0.0, NEG).astype(f32)[None]
    outer_weight, query_u = cut(outer_weight, query_u)
    outer_w = lax.all_gather(outer_weight, "fsdp", axis=0, tiled=True)
    mixed, prob_low = attn_fwd(query_u, query_v, keys, values, relative, bias)
    hidden = tokens[0].astype(f32) + jnp.dot(mixed, output_w, preferred_element_type=f32)
    inner_norm, scaled_two, spread_two = norm_parts(hidden, gain_two, shift_two)
    inner_low = inner_norm.astype(bf16)
    preact = jnp.dot(inner_low, inner_w, preferred_element_type=f32) + inner_b.astype(f32)
    active = smooth_gate(preact).astype(bf16)
    grad = out_grad[0]
    grad_wide = grad.astype(f32)
    active, preact = cut(active, preact)
    outer_grad = jnp.einsum("sf,sd->fd", active, grad, preferred_element_type=f32).astype(bf16)
    outer_bias_grad = jnp.sum(grad_wide, axis=0)

    groups = mem_rows // RATE
    start = mem_rows - RATE * groups
    mem_valid = (jnp.arange(mem_rows, dtype=jnp.int32) >= mem_rows - mem_fill[0]).astype(bf16)
    taps = (memory[0] * mem_valid[:, None])[start:, :].reshape(groups, RATE * width)
    group_valid = (
        start + RATE * jnp.arange(groups, dtype=jnp.int32) + RATE - 1 >= mem_rows - mem_fill[0]
    )[:, None]
    made_grad = comp_grad[0] * group_valid.astype(bf16)
    made_grad, active = cut(made_grad, active)
    conv_grad = jnp.einsum("nk,nd->kd", taps, made_grad, preferred_element_type=f32).astype(bf16)
    conv_bias_grad = jnp.sum(made_grad.astype(f32), axis=0)

    outer_w, outer_grad, conv_grad = cut(outer_w, outer_grad, conv_grad)
    conv_part = lax.psum_scatter(conv_grad, "fsdp", scatter_dimension=0, tiled=True)
    outer_part = lax.psum_scatter(outer_grad, "fsdp", scatter_dimension=0, tiled=True)
    active_grad = jnp.einsum("sd,fd->sf", grad, outer_w, preferred_element_type=f32)
    gate_pull = jax.vjp(smooth_gate, preact)[1]
    preact_grad = gate_pull(active_grad)[0].astype(bf16)
    inner_bias_grad = jnp.sum(preact_grad.astype(f32), axis=0)
    inner_grad = jnp.einsum("sd,sf->df", inner_low, preact_grad, preferred_element_type=f32).astype(
        bf16
    )
    inner_norm_grad = jnp.einsum("sf,df->sd", preact_grad, inner_w, preferred_element_type=f32)
    second_gain_grad = jnp.sum(inner_norm_grad * scaled_two, axis=0)
    second_shift_grad = jnp.sum(inner_norm_grad, axis=0)
    hidden_grad = grad_wide + norm_back(inner_norm_grad, scaled_two, spread_two, gain_two)
    hidden_low = hidden_grad.astype(bf16)
    mixed_grad = jnp.einsum("se,de->sd", hidden_low, output_w, preferred_element_type=f32).astype(
        bf16
    )
    query_g, keys_g, values_g, relative_g, sums = attn_bwd(
        query_u, query_v, keys, values, relative, prob_low, mixed_grad
    )
    conv_part, query_g, conv_weight = cut(conv_part, query_g, conv_weight)
    conv_end = inward_hop(conv_part)
    conv_w = lax.all_gather(conv_weight, "fsdp", axis=0, tiled=True)
    key_grad = jnp.einsum("sd,es->de", normed_low, keys_g, preferred_element_type=f32).astype(bf16)
    value_grad = jnp.einsum("sd,es->de", normed_low, values_g, preferred_element_type=f32).astype(bf16)
    position_grad = jnp.einsum("ld,el->de", pos_low, relative_g, preferred_element_type=f32).astype(
        bf16
    )
    key_grad, value_grad, position_grad, conv_end, query_g = cut(
        key_grad, value_grad, position_grad, conv_end, query_g
    )
    conv_pair = add(conv_part, conv_end)
    conv_mid = middle_hop(conv_pair)
    query_grad = jnp.einsum("sd,se->de", own_rows, query_g, preferred_element_type=f32).astype(bf16)
    trio = (
        (query_w, query_grad, jnp.sum(query_g.astype(f32), axis=0)),
        (key_w, key_grad, jnp.sum(keys_g.astype(f32), axis=1)),
        (value_w, value_grad, jnp.sum(values_g.astype(f32), axis=1)),
    )
    first_shift_grad = sum(
        jnp.sum(w.astype(f32) * column[None, :], axis=1) for w, _, column in trio
    )
    with_normed = sum(jnp.sum(w.astype(f32) * g.astype(f32), axis=1) for w, g, _ in trio)
    first_gain_grad = (with_normed - shift_one.astype(f32) * first_shift_grad) / gain_one.astype(f32)
    own_grad = jnp.einsum("se,de->sd", query_g, query_w, preferred_element_type=f32)
    own_grad = own_grad + jnp.einsum(
        "es,de->sd", keys_g[:, old:], key_w, preferred_element_type=f32
    )
    own_grad = own_grad + jnp.einsum(
        "es,de->sd", values_g[:, old:], value_w, preferred_element_type=f32
    )
    inner = own_grad * gain_one.astype(f32)
    own = tokens[0].astype(f32)
    spread_own = lax.rsqrt(
        jnp.mean((own - jnp.mean(own, axis=-1, keepdims=True)) ** 2, axis=-1, keepdims=True) + EPSILON
    )
    token_gradient = hidden_grad + spread_own * (
        inner
        - jnp.mean(inner, axis=-1, keepdims=True)
        - scaled_one * jnp.mean(inner * scaled_one, axis=-1, keepdims=True)
    )
    conv_mid, own_grad, active, hidden_low = cut(conv_mid, own_grad, active, hidden_low)
    conv_sum = add(conv_pair, conv_mid)
    conv_last = outward_hop(conv_sum)
    output_grad = jnp.einsum("sd,se->de", mixed, hidden_low, preferred_element_type=f32).astype(bf16)
    vector_grads = (
        first_gain_grad,
        first_shift_grad,
        sums[0],
        sums[1],
        second_gain_grad,
        second_shift_grad,
        outer_bias_grad,
        conv_bias_grad,
        inner_bias_grad,
    )
    packed = jnp.concatenate([v.reshape(shards, -1, lanes) for v in vector_grads], axis=1)
    packed = jnp.pad(packed, ((0, 0), (0, 32 - packed.shape[1]), (0, 0))).astype(bf16)
    result = (
        hidden + jnp.dot(active, outer_w, preferred_element_type=f32) + outer_b.astype(f32)
    ).astype(bf16)
    made = (
        (jnp.dot(taps, conv_w, preferred_element_type=f32) + conv_b.astype(f32))
        * group_valid.astype(f32)
    ).astype(bf16)
    (
        output_mean,
        query_mean,
        key_mean,
        value_mean,
        position_mean,
        inner_mean,
        table_mean,
        outer_mean,
    ) = reduce_tail(
        [(g, 2) for g in (output_grad, query_grad, key_grad, value_grad, position_grad)]
        + [(inner_grad, 4)]
        + [(packed.reshape(shards * 32, lanes), 1)],
        [(outer_part, 4)],
        share,
        1,
    )
    conv_last, query_mean = cut(conv_last, query_mean)
    conv_mean = finish(conv_sum, conv_last, share)
    (
        first_gain_mean,
        first_shift_mean,
        content_mean,
        posbias_mean,
        second_gain_mean,
        second_shift_mean,
        outer_bias_mean,
        conv_bias_mean,
    ) = (table_mean[n] for n in range(8))
    inner_bias_mean = table_mean[8 : 8 + sizes[-1] // lanes].reshape(sizes[-1])
    return (
        result[None],
        token_gradient[None],
        made[None],
        first_gain_mean,
        first_shift_mean,
        query_mean,
        key_mean,
        value_mean,
        position_mean,
        content_mean,
        posbias_mean,
        output_mean,
        second_gain_mean,
        second_shift_mean,
        inner_mean,
        inner_bias_mean,
        outer_mean,
        outer_bias_mean,
        conv_mean,
        conv_bias_mean,
    )


def per_device(*arguments):
    if lax.axis_size("dp") == 4 and lax.axis_size("fsdp") == 8:
        return per_device_direct(*arguments)
    return per_device_plain(*arguments)


def solution(mesh):
    in_specs = (
        P(("dp", "fsdp"), None, None),
        P(("dp", "fsdp"), None, None),
        P(("dp", "fsdp"), None, None),
        P(("dp", "fsdp")),
        P(("dp", "fsdp")),
        P(("dp", "fsdp"), None),
        P("fsdp"),
        P("fsdp"),
        P("fsdp", None),
        P("fsdp", None),
        P("fsdp", None),
        P("fsdp", None),
        P("fsdp"),
        P("fsdp"),
        P("fsdp", None),
        P("fsdp"),
        P("fsdp"),
        P("fsdp", None),
        P("fsdp"),
        P("fsdp", None),
        P("fsdp"),
        P("fsdp", None),
        P("fsdp"),
        P(("dp", "fsdp"), None, None),
        P(("dp", "fsdp"), None, None),
    )
    out_specs = (
        P(("dp", "fsdp"), None, None),
        P(("dp", "fsdp"), None, None),
        P(("dp", "fsdp"), None, None),
        P("fsdp"),
        P("fsdp"),
        P("fsdp", None),
        P("fsdp", None),
        P("fsdp", None),
        P("fsdp", None),
        P("fsdp"),
        P("fsdp"),
        P("fsdp", None),
        P("fsdp"),
        P("fsdp"),
        P("fsdp", None),
        P("fsdp"),
        P("fsdp", None),
        P("fsdp"),
        P("fsdp", None),
        P("fsdp"),
    )
    return jax.shard_map(
        per_device, mesh=mesh, in_specs=in_specs, out_specs=out_specs, check_vma=False
    )
```

```python
import functools
import math

import jax
import jax.numpy as jnp
from jax import lax
from jax.experimental import pallas as pl
from jax.experimental.pallas import tpu as pltpu
from jax.sharding import PartitionSpec as P

HEADS = 8
DH = 128
RATE = 3
BLK = 128
NEG = -1.2e10
f32 = jnp.float32
bf16 = jnp.bfloat16


EPSILON = 1e-05
MASKED = -1000000000.0


def smooth_gate(values):
    return jax.nn.gelu(values, approximate=True)


def norm_parts(rows, gain, shift):
    center = jnp.mean(rows, axis=-1, keepdims=True)
    centered = rows - center
    spread = lax.rsqrt(jnp.mean(centered * centered, axis=-1, keepdims=True) + EPSILON)
    scaled = centered * spread
    return (scaled * gain.astype(jnp.float32) + shift.astype(jnp.float32), scaled, spread)


def norm_back(grad, scaled, spread, gain):
    inner = grad * gain.astype(jnp.float32)
    return spread * (
        inner
        - jnp.mean(inner, axis=-1, keepdims=True)
        - scaled * jnp.mean(inner * scaled, axis=-1, keepdims=True)
    )


def positions(count, width):
    distance = (count - 1 - jnp.arange(count, dtype=jnp.int32)).astype(jnp.float32)
    rates = jnp.exp(
        jnp.arange(0, width, 2, dtype=jnp.int32).astype(jnp.float32) * (-math.log(10000.0) / width)
    )
    angle = distance[:, None] * rates[None, :]
    return jnp.concatenate([jnp.sin(angle), jnp.cos(angle)], axis=1)


def dot_nt(a,b): return lax.dot_general(a,b,(((1,),(1,)),((),())),preferred_element_type=f32)
def dot_nn(a,b): return lax.dot_general(a,b,(((1,),(0,)),((),())),preferred_element_type=f32)

def attn_fwd_kernel(qu_ref,qv_ref,k_ref,v_ref,r_ref,bias_ref,o_ref,p_ref,beside=None):
    seg=qu_ref.shape[0]; total=k_ref.shape[0]; old=total-seg
    c=math.log2(math.e)/math.sqrt(DH)
    for ib in range(seg//BLK):
        if beside is not None: beside(ib)
        rows=pl.ds(ib*BLK,BLK)
        L=old+(ib+1)*BLK
        qu=qu_ref[rows,:]; qv=qv_ref[rows,:]
        raw=dot_nt(qv,r_ref[pl.ds(total-L,L),:])
        z=dot_nt(qu,k_ref[pl.ds(0,L),:])+pltpu.roll(raw,L-(BLK-1),axis=1,stride=1,stride_axis=0)
        M=L-BLK
        za=z[:,:M]+bias_ref[:,:M]
        rr=lax.broadcasted_iota(jnp.int32,(BLK,BLK),0); cc=lax.broadcasted_iota(jnp.int32,(BLK,BLK),1)
        zb=z[:,M:]
        zb=jnp.where(cc==rr,zb,jnp.where(cc<rr,zb+bias_ref[:,pl.ds(M,BLK)],NEG))
        top=jnp.maximum(jnp.max(za,axis=1,keepdims=True),jnp.max(zb,axis=1,keepdims=True))
        ea=jnp.exp2((za-top)*c); eb=jnp.exp2((zb-top)*c)
        inv=1.0/(jnp.sum(ea,axis=1,keepdims=True)+jnp.sum(eb,axis=1,keepdims=True))
        pa=(ea*inv).astype(bf16); pb=(eb*inv).astype(bf16)
        p_ref[0,rows,pl.ds(0,M)]=pa
        p_ref[0,rows,pl.ds(M,BLK)]=pb
        o_ref[rows,:]=(dot_nn(pa,v_ref[pl.ds(0,M),:])+dot_nn(pb,v_ref[pl.ds(M,BLK),:])).astype(bf16)

def attn_fwd_gather_kernel(pieces, *refs):
    shard, whole = refs[6], refs[9]
    local, sent, came = refs[10:]
    head = pl.program_id(0)
    height = shard.shape[0]
    rows = height // pieces
    moved = Gathering([(shard, n * rows, rows, whole, height) for n in range(pieces)], local, sent, came)

    @pl.when(head == 0)
    def _():
        moved.greet()
        for n in range(pieces):
            moved.begin(n)

    tiles = refs[0].shape[0] // BLK
    steps = {}
    for n in range(pieces):
        slot = 7 + (26 * n) // pieces
        steps.setdefault(slot, []).append((moved.onward, n))
        if n:
            steps.setdefault(slot, []).append((moved.last, n - 1))

    def beside(tile):
        for slot, phases in steps.items():
            if slot % tiles == tile:

                @pl.when(head == slot // tiles)
                def _(phases=phases):
                    for phase, n in phases:
                        phase(n)

    attn_fwd_kernel(*refs[:6], *refs[7:9], beside=beside)

    @pl.when(head == HEADS - 1)
    def _():
        moved.last(pieces - 1)
        for n in range(pieces):
            moved.complete(n)
        moved.drain()


def attn_fwd(qu, qv, k, v, r, bias, shard=None, pieces=8):
    seg, width = qu.shape
    total = k.shape[0]
    col = lambda n: pl.BlockSpec((n, DH), lambda h: (0, h))
    in_specs = [col(seg), col(seg), col(total), col(total), col(total)]
    in_specs += [pl.BlockSpec((1, total), lambda h: (0, 0))]
    out_specs = [col(seg), pl.BlockSpec((1, seg, total), lambda h: (h, 0, 0))]
    out_shape = [
        jax.ShapeDtypeStruct((seg, width), bf16),
        jax.ShapeDtypeStruct((HEADS, seg, total), bf16),
    ]
    cost = pl.CostEstimate(
        flops=6 * seg * total * width,
        bytes_accessed=2 * (3 * seg * width + 3 * total * width + HEADS * seg * total),
        transcendentals=HEADS * seg * total,
    )
    if shard is None:
        return pl.pallas_call(
            attn_fwd_kernel,
            grid=(HEADS,),
            in_specs=in_specs,
            out_specs=out_specs,
            out_shape=out_shape,
            cost_estimate=cost,
            compiler_params=pltpu.CompilerParams(vmem_limit_bytes=58 << 20),
            name="attn_fwd",
        )(qu, qv, k, v, r, bias)
    return pl.pallas_call(
        functools.partial(attn_fwd_gather_kernel, pieces),
        grid=(HEADS,),
        in_specs=in_specs + [pl.BlockSpec(shard.shape, lambda h: (0, 0))],
        out_specs=out_specs + [pl.BlockSpec(memory_space=pl.ANY)],
        out_shape=out_shape + [jax.ShapeDtypeStruct((8 * shard.shape[0], shard.shape[1]), bf16)],
        scratch_shapes=[pltpu.SemaphoreType.DMA((n * pieces,)) for n in (1, 7, 7)],
        cost_estimate=cost,
        compiler_params=pltpu.CompilerParams(
            collective_id=3, has_side_effects=True, vmem_limit_bytes=58 << 20
        ),
        name="attn_fwd_gather",
    )(qu, qv, k, v, r, bias, shard)


def attn_bwd_kernel(qu_ref,qv_ref,qut_ref,qvrt_ref,k_ref,v_ref,r_ref,p_ref,g_ref,gt_ref,dq_ref,dkt_ref,dvt_ref,drt_ref,sums_ref,dk_acc,dv_acc,dr_acc):
    seg=g_ref.shape[0]; total=k_ref.shape[0]; old=total-seg
    scale=1.0/math.sqrt(DH)
    rr=lax.broadcasted_iota(jnp.int32,(BLK,BLK),0); cc=lax.broadcasted_iota(jnp.int32,(BLK,BLK),1)
    flip=(rr+cc==BLK-1).astype(bf16)
    su=jnp.zeros((1,DH),f32); sv=jnp.zeros((1,DH),f32)
    nb=seg//BLK
    for ib in range(nb-1,-1,-1):
        rows=pl.ds(ib*BLK,BLK)
        L=old+(ib+1)*BLK
        g=g_ref[rows,:]; gt=gt_ref[:,rows]; qut=qut_ref[:,rows]
        plow=p_ref[0,rows,pl.ds(0,L)]
        p=plow.astype(f32)
        dp=dot_nt(g,v_ref[pl.ds(0,L),:])
        d=jnp.sum(p*dp,axis=1,keepdims=True)
        dz=(p*(dp-d)*scale).astype(bf16)
        dvt=dot_nn(gt,plow)
        dkt=dot_nn(qut,dz)
        dqu=dot_nn(dz,k_ref[pl.ds(0,L),:])
        rev=dot_nn(flip,dz)
        raw=pltpu.roll(rev,0,axis=1,stride=1,stride_axis=0).astype(bf16)
        T=pl.ds(total-L,L)
        dqv_rev=dot_nn(raw,r_ref[T,:])
        qvr=dot_nt(qvrt_ref[:,rows],flip).astype(bf16)
        drt=dot_nn(qvr,raw)
        dqv=lax.dot_general(flip.astype(f32),dqv_rev,(((1,),(0,)),((),())),preferred_element_type=f32,precision=lax.Precision.HIGHEST)
        su+=jnp.sum(dqu,axis=0,keepdims=True); sv+=jnp.sum(dqv,axis=0,keepdims=True)
        dq_ref[rows,:]=(dqu+dqv).astype(bf16)
        J=pl.ds(0,L)
        if ib==nb-1:
            dv_acc[...]=dvt; dk_acc[...]=dkt; dr_acc[...]=drt
        else:
            dv_acc[:,J]+=dvt; dk_acc[:,J]+=dkt; dr_acc[:,T]+=drt
    dkt_ref[...]=dk_acc[...].astype(bf16); dvt_ref[...]=dv_acc[...].astype(bf16); drt_ref[...]=dr_acc[...].astype(bf16)
    sums_ref[0:1,:]=su; sums_ref[1:2,:]=sv

def attn_bwd_sums_kernel(plan, sources, count, *refs):
    base, grads = refs[:10], refs[10 : 10 + count]
    refs = refs[10 + count :]
    results, outs, refs = refs[:5], refs[5 : 5 + count], refs[5 + count :]
    totals = refs[:3]
    sums = Sums(plan, sources, grads, outs, refs[3:])
    steps = sums.schedule()
    head = pl.program_id(0)
    per = -(-len(steps) // HEADS) if len(steps) > HEADS + 2 else 1

    for n in range(HEADS):

        @pl.when(head == n)
        def _(n=n):
            if n == 0:
                sums.greet()
            for step in steps[n * per : (n + 1) * per]:
                for phase, item in step:
                    phase(item)

    attn_bwd_kernel(*base, *results, *totals)

    @pl.when(head == HEADS - 1)
    def _():
        for step in steps[HEADS * per :]:
            for phase, item in step:
                phase(item)
        sums.drain()


def attn_bwd(qu, qv, k, v, r, p, g, grads=(), share=1.0):
    seg, width = qu.shape
    total = k.shape[0]
    col = lambda n: pl.BlockSpec((n, DH), lambda h: (0, h))
    row = lambda n: pl.BlockSpec((DH, n), lambda h: (h, 0))
    any_spec = pl.BlockSpec(memory_space=pl.ANY)
    in_specs = [col(seg), col(seg), row(seg), row(seg), col(total), col(total), col(total)]
    in_specs += [pl.BlockSpec((1, seg, total), lambda h: (h, 0, 0)), col(seg), row(seg)]
    out_specs = [col(seg), row(total), row(total), row(total), pl.BlockSpec((8, DH), lambda h: (0, h))]
    out_shape = [jax.ShapeDtypeStruct((seg, width), bf16)]
    out_shape += [jax.ShapeDtypeStruct((width, total), bf16)] * 3
    out_shape += [jax.ShapeDtypeStruct((8, width), f32)]
    scratch = [pltpu.VMEM((DH, total), f32)] * 3
    cost = pl.CostEstimate(
        flops=16 * seg * total * width,
        bytes_accessed=2 * (5 * seg * width + 6 * total * width + HEADS * seg * total),
        transcendentals=0,
    )
    operands = (qu, qv, qu.T, qv.T, k, v, r, p, g, g.T)
    if not grads:
        return pl.pallas_call(
            attn_bwd_kernel,
            grid=(HEADS,),
            in_specs=in_specs,
            out_specs=out_specs,
            out_shape=out_shape,
            scratch_shapes=scratch,
            cost_estimate=cost,
            compiler_params=pltpu.CompilerParams(vmem_limit_bytes=58 << 20),
            name="attn_bwd",
        )(*operands)
    plan, sources, arrays, shapes = sums_plan(grads, ())
    results = pl.pallas_call(
        functools.partial(attn_bwd_sums_kernel, plan, sources, len(arrays)),
        grid=(HEADS,),
        in_specs=in_specs + [any_spec] * len(arrays),
        out_specs=out_specs + [any_spec] * len(arrays),
        out_shape=out_shape + shapes,
        scratch_shapes=scratch + sums_scratch(plan),
        cost_estimate=cost,
        compiler_params=pltpu.CompilerParams(
            collective_id=4, has_side_effects=True, vmem_limit_bytes=58 << 20
        ),
        name="attn_bwd_sums",
    )(*operands, *arrays)
    return tuple(results[:5]) + tuple(total.astype(f32) * share for total in results[5:])


def cut(*values):
    return lax.optimization_barrier(values)


def positions_low(count, width):
    tile = 64
    rates = jnp.exp(
        jnp.arange(0, width, 2, dtype=jnp.int32).astype(f32) * (-math.log(10000.0) / width)
    )
    rates = jnp.concatenate([rates, rates])[None, :]
    upper = (jnp.arange(width, dtype=jnp.int32) < width // 2)[None, :]
    far = (count - 1 - tile * jnp.arange(count // tile, dtype=jnp.int32)).astype(f32)[:, None] * rates
    near = jnp.arange(tile, dtype=jnp.int32).astype(f32)[:, None] * rates
    sine, cosine = jnp.sin(far), jnp.cos(far)
    with_cos = jnp.where(upper, sine, cosine)[:, None, :]
    with_sin = jnp.where(upper, -cosine, sine)[:, None, :]
    near_cos, near_sin, with_cos, with_sin = cut(jnp.cos(near), jnp.sin(near), with_cos, with_sin)
    table = with_cos * near_cos[None] + with_sin * near_sin[None]
    return table.astype(bf16).reshape(count, width)


def hop(value, move):
    dp, fsdp = lax.axis_size("dp"), lax.axis_size("fsdp")
    pairs = []
    for z in range(dp):
        for f in range(fsdp):
            to = move(z, f)
            if to is not None:
                pairs.append((z * fsdp + f, to[0] * fsdp + to[1]))
    return lax.ppermute(value, ("dp", "fsdp"), pairs)


def inward_hop(w):
    to = {0: 1, 3: 2}
    return hop(w, lambda z, f: (to[z], f) if z in to else None)


def middle_hop(w):
    return hop(w, lambda z, f: (3 - z, f) if z in (1, 2) else None)


def outward_hop(w):
    to = {1: 0, 2: 3}
    return hop(w, lambda z, f: (to[z], f) if z in to else None)


def add(first, second):
    return (first.astype(f32) + second.astype(f32)).astype(bf16)


def finish(whole, last, share):
    plane = lax.axis_index("dp")
    return jnp.where((plane == 1) | (plane == 2), whole, last).astype(f32) * share


def add_rows(out, parts):
    rows = out.shape[0]
    height = 32 if rows % 32 == 0 else 16

    def one(i, carry):
        at = pl.ds(pl.multiple_of(i * height, height), height)
        total = parts[0][at, :].astype(f32)
        for part in parts[1:]:
            total = total + part[at, :].astype(f32)
        out[at, :] = total.astype(out.dtype)
        return carry

    lax.fori_loop(0, rows // height, one, 0)


FULL_BUFFERS = ("mine", "theirs", "far", "half_x", "half_y", "to_y", "to_x", "got_y", "got_x")
LINE_BUFFERS = ("own", "end", "mid")


def sums_scratch(plan):
    shapes = []
    for full, rows, cols in plan:
        if full:
            half = pltpu.VMEM((rows // 2, cols), bf16)
            one = pltpu.VMEM((rows, cols), bf16)
            shapes += [pltpu.VMEM((4, rows, cols), bf16)] * 2 + [one, half, half] + [one] * 4
        shapes += [pltpu.VMEM((rows, cols), bf16)] * 3
        shapes += [pltpu.SemaphoreType.DMA((n,)) for n in (4, 11, 11, 1)]
    return shapes


GAP, LINE_GAP = 2, 2


class Sums:
    def __init__(self, plan, sources, grads, outs, scratch):
        self.z, self.f = lax.axis_index("dp"), lax.axis_index("fsdp")
        self.chip, self.core = self.f // 2, self.f % 2
        self.middle = (self.z == 1) | (self.z == 2)
        self.edge = jnp.logical_not(self.middle)
        self.inward = (jnp.where(self.z < 2, 1, 2), self.f)
        self.outward = (jnp.where(self.z < 2, 0, 3), self.f)
        self.across = (3 - self.z, self.f)
        self.sibling, self.by_x, self.by_y = (
            (self.z, self.f ^ 1),
            (self.z, self.f ^ 2),
            (self.z, self.f ^ 4),
        )
        self.items, at = [], 0
        for n, (full, rows, cols) in enumerate(plan):
            names = (FULL_BUFFERS if full else ()) + LINE_BUFFERS + ("local", "sent", "came", "stored")
            b = dict(zip(names, scratch[at : at + len(names)]))
            at += len(names)
            b.update(full=full, rows=rows, source=grads[sources[n][0]], first=sources[n][1])
            b.update(target=outs[sources[n][0]])
            self.items.append(b)

    def greet(self):
        barrier = pltpu.get_barrier_semaphore()

        def signal(device):
            pl.semaphore_signal(
                barrier, inc=1, device_id=device, device_id_type=pl.DeviceIdType.MESH
            )

        for device in (self.sibling, self.by_x, self.by_y):
            signal(device)

        @pl.when(self.middle)
        def _():
            signal(self.outward)
            signal(self.across)
            pl.semaphore_wait(barrier, 5)

        @pl.when(self.edge)
        def _():
            signal(self.inward)
            pl.semaphore_wait(barrier, 4)

    def copy(self, b, n, src, dst, device):
        return pltpu.make_async_remote_copy(
            src_ref=src,
            dst_ref=dst,
            send_sem=b["sent"].at[n],
            recv_sem=b["came"].at[n],
            device_id=device,
            device_id_type=pl.DeviceIdType.MESH,
        )

    def rows_of(self, b):
        return pl.ds(b["first"], b["rows"])

    def across_cores(self, b, s):
        block = (self.chip ^ (3 - s)) * 2 + 1 - self.core
        src = b["source"].at[block, self.rows_of(b), :]
        return self.copy(b, s, src, b["theirs"].at[s], self.sibling)

    def load(self, b, s):
        if not b["full"]:
            src, dst = b["source"].at[self.rows_of(b), :], b["own"]
        else:
            block = (self.chip ^ (3 - s)) * 2 + self.core
            src, dst = b["source"].at[block, self.rows_of(b), :], b["mine"].at[s]
        return pltpu.make_async_copy(src, dst, b["local"].at[s])

    def halves_out(self, b):
        half = b["rows"] // 2
        return (
            self.copy(b, 4, b["far"].at[pl.ds(0, half), :], b["half_x"], self.by_x),
            self.copy(b, 5, b["far"].at[pl.ds(half, half), :], b["half_y"], self.by_y),
        )

    def near_out(self, b):
        return (
            self.copy(b, 6, b["to_y"], b["got_y"], self.by_y),
            self.copy(b, 7, b["to_x"], b["got_x"], self.by_x),
        )

    def go_in(self, b):
        return self.copy(b, 8, b["own"], b["end"], self.inward)

    def go_mid(self, b):
        return self.copy(b, 9, b["own"], b["mid"], self.across)

    def go_out(self, b):
        return self.copy(b, 10, b["mid"], b["end"], self.outward)

    def store(self, b, name):
        return pltpu.make_async_copy(b[name], b["target"].at[self.rows_of(b), :], b["stored"].at[0])

    def begin(self, b):
        if b["full"]:
            for s in range(4):
                self.across_cores(b, s).start()
                self.load(b, s).start()
        else:
            self.load(b, 0).start()

    def arrived(self, b, s):
        self.across_cores(b, s).wait_recv()
        self.load(b, s).wait()

    def far(self, b):
        self.arrived(b, 0)
        add_rows(b["far"], [b["mine"].at[0], b["theirs"].at[0]])
        for c in self.halves_out(b):
            c.start()

    def near(self, b):
        half = b["rows"] // 2
        low, high = pl.ds(0, half), pl.ds(half, half)
        self.arrived(b, 1)
        self.arrived(b, 2)
        for c in self.halves_out(b):
            c.wait_recv()
        mine, theirs = b["mine"], b["theirs"]
        add_rows(b["to_y"].at[low, :], [mine.at[1, low, :], theirs.at[1, low, :], b["half_x"]])
        add_rows(b["to_y"].at[high, :], [mine.at[1, high, :], theirs.at[1, high, :]])
        add_rows(b["to_x"].at[low, :], [mine.at[2, low, :], theirs.at[2, low, :]])
        add_rows(b["to_x"].at[high, :], [mine.at[2, high, :], theirs.at[2, high, :], b["half_y"]])
        for c in self.near_out(b):
            c.start()

    def own(self, b):
        self.arrived(b, 3)
        for c in self.near_out(b):
            c.wait_recv()
        add_rows(b["own"], [b["mine"].at[3], b["theirs"].at[3], b["got_x"], b["got_y"]])

    def line_in(self, b):
        if not b["full"]:
            self.load(b, 0).wait()

        @pl.when(self.edge)
        def _():
            self.go_in(b).start()

    def line_mid(self, b):
        @pl.when(self.middle)
        def _():
            self.go_in(b).wait_recv()
            add_rows(b["own"], [b["own"], b["end"]])
            self.go_mid(b).start()

    def line_out(self, b):
        @pl.when(self.middle)
        def _():
            self.go_mid(b).wait_recv()
            add_rows(b["mid"], [b["own"], b["mid"]])
            self.go_out(b).start()
            self.store(b, "mid").start()

    def line_last(self, b):
        @pl.when(self.edge)
        def _():
            self.go_out(b).wait_recv()
            self.store(b, "end").start()

    def schedule(self):
        wide = [b for b in self.items if b["full"]]
        left = [b for b in self.items if not b["full"]]
        line, due, slot = [], [], 0
        while sum(b is not None for b in line) < len(self.items):
            if 0 <= slot - 2 * GAP < len(wide):
                due.append(wide[slot - 2 * GAP])
            if left and (not due or slot % 2 == 0):
                line.append(left.pop(0))
            elif due:
                line.append(due.pop(0))
            else:
                line.append(None)
            slot += 1
        steps = []
        for t in range(len(line) + 3 * LINE_GAP):
            step = []
            if t + 2 < len(wide):
                step.append((self.begin, wide[t + 2]))
            for phase, back in ((self.far, 0), (self.near, GAP), (self.own, 2 * GAP)):
                if 0 <= t - back < len(wide):
                    step.append((phase, wide[t - back]))
            phases = (self.line_in, self.line_mid, self.line_out, self.line_last)
            for back, phase in enumerate(phases):
                at = t - back * LINE_GAP
                if 0 <= at < len(line) and line[at] is not None:
                    step.append((phase, line[at]))
            steps.append(step)
        first = [(self.begin, b) for b in self.items if not b["full"]]
        first += [(self.begin, b) for b in wide[:2]]
        return [first] + steps

    def drain(self):
        for b in self.items:
            if b["full"]:
                for s in range(4):
                    self.across_cores(b, s).wait_send()
                for c in self.halves_out(b) + self.near_out(b):
                    c.wait_send()
            self.store(b, "mid").wait()

        @pl.when(self.edge)
        def _():
            for b in self.items:
                self.go_in(b).wait_send()

        @pl.when(self.middle)
        def _():
            for b in self.items:
                self.go_mid(b).wait_send()
                self.go_out(b).wait_send()


def sums_plan(fulls, shards):
    plan, sources, arrays, shapes = [], [], [], []
    for full, group in ((True, fulls), (False, shards)):
        for g, pieces in group:
            rows, cols = g.shape[0] // (8 if full else 1), g.shape[1]
            for p in range(pieces):
                plan.append((full, rows // pieces, cols))
                sources.append((len(arrays), p * (rows // pieces)))
            arrays.append(g.reshape(8, rows, cols) if full else g)
            shapes.append(jax.ShapeDtypeStruct((rows, cols), bf16))
    return tuple(plan), tuple(sources), arrays, shapes


def tail_kernel(plan, sources, count, *refs):
    sums = Sums(plan, sources, refs[:count], refs[count : 2 * count], refs[2 * count :])
    sums.greet()
    for step in sums.schedule():
        for phase, item in step:
            phase(item)
    sums.drain()


def reduce_tail(fulls, shards, share, number):
    plan, sources, arrays, shapes = sums_plan(fulls, shards)
    totals = pl.pallas_call(
        functools.partial(tail_kernel, plan, sources, len(arrays)),
        in_specs=[pl.BlockSpec(memory_space=pl.ANY)] * len(arrays),
        out_specs=[pl.BlockSpec(memory_space=pl.ANY)] * len(arrays),
        out_shape=shapes,
        scratch_shapes=sums_scratch(plan),
        compiler_params=pltpu.CompilerParams(
            collective_id=number, has_side_effects=True, vmem_limit_bytes=56 << 20
        ),
        name="reduce_tail",
    )(*arrays)
    return [total.astype(f32) * share for total in totals]


class Gathering:
    def __init__(self, pieces, local, sent, came):
        self.pieces, self.local, self.sent, self.came = pieces, local, sent, came
        z, f = lax.axis_index("dp"), lax.axis_index("fsdp")
        near = 2 + 2 * lax.rem(z, 2)
        self.first_to, self.second_to = (z, f ^ near), (z, f ^ (6 - near))
        self.pair_to, self.core_to = (z ^ 1, f), (z, f ^ 1)
        self.slots = (f, f ^ near, f ^ (6 - near), f ^ 6)

    def greet(self):
        barrier = pltpu.get_barrier_semaphore()
        for device in (self.first_to, self.second_to, self.pair_to, self.core_to):
            pl.semaphore_signal(
                barrier, inc=1, device_id=device, device_id_type=pl.DeviceIdType.MESH
            )
        pl.semaphore_wait(barrier, 4)

    def part(self, n, slot):
        shard, start, rows, whole, height = self.pieces[n]
        return whole.at[pl.ds(pl.multiple_of(slot * height + start, 16), rows), :]

    def shard(self, n):
        shard, start, rows, whole, height = self.pieces[n]
        return shard.at[pl.ds(start, rows), :]

    def copy(self, n, k, src, slot, device):
        return pltpu.make_async_remote_copy(
            src_ref=src,
            dst_ref=self.part(n, slot),
            send_sem=self.sent.at[n * 7 + k],
            recv_sem=self.came.at[n * 7 + k],
            device_id=device,
            device_id_type=pl.DeviceIdType.MESH,
        )

    def first(self, n):
        return self.copy(n, 0, self.shard(n), self.slots[0], self.first_to)

    def pair(self, n):
        return self.copy(n, 1, self.part(n, self.slots[1]), self.slots[1], self.pair_to)

    def second(self, n):
        return self.copy(n, 2, self.part(n, self.slots[1]), self.slots[1], self.second_to)

    def core(self, n, s):
        src = self.shard(n) if s == 0 else self.part(n, self.slots[s])
        return self.copy(n, 3 + s, src, self.slots[s], self.core_to)

    def mine(self, n):
        return pltpu.make_async_copy(self.shard(n), self.part(n, self.slots[0]), self.local.at[n])

    def begin(self, n):
        self.first(n).start()
        self.mine(n).start()
        self.core(n, 0).start()

    def onward(self, n):
        self.first(n).wait_recv()
        self.pair(n).start()
        self.second(n).start()
        self.core(n, 1).start()

    def last(self, n):
        self.pair(n).wait_recv()
        self.core(n, 2).start()
        self.second(n).wait_recv()
        self.core(n, 3).start()

    def complete(self, n):
        self.mine(n).wait()
        for s in range(4):
            self.core(n, s).wait_recv()

    def drain(self):
        for n in range(len(self.pieces)):
            for copy in (self.first(n), self.pair(n), self.second(n)):
                copy.wait_send()
            for s in range(4):
                self.core(n, s).wait_send()


def tile_loop(rows, height, body):
    def one(i, carry):
        body(pl.ds(pl.multiple_of(i * height, height), height))
        return carry

    lax.fori_loop(0, rows // height, one, 0)


HEAD_ITEMS = ("table", "keys", "values", "query", "position", "output", "inner")
INNER_PIECES = 4


def head_kernel(*refs):
    count = len(HEAD_ITEMS)
    rows_in, shards, pos_ref = refs[:3], refs[3 : 3 + count], refs[3 + count]
    refs = refs[4 + count :]
    (xhat_out, normed_out, qu_out, qv_out, keys_out, values_out, relative_out) = refs[:7]
    weights_out, refs = refs[7 : 7 + count], refs[7 + count :]
    wholes, refs = refs[:count], refs[count:]
    xhat, normed, pos, qu, qv, keys, values, relative = refs[:8]
    local, sent, came, left = refs[8:]
    moved = Gathering(
        [(shards[n], 0, shards[n].shape[0], wholes[n], shards[n].shape[0]) for n in range(count - 1)]
        + [
            (shards[-1], p * shards[-1].shape[0] // INNER_PIECES, shards[-1].shape[0] // INNER_PIECES)
            + (wholes[-1], shards[-1].shape[0])
            for p in range(INNER_PIECES)
        ],
        local,
        sent,
        came,
    )
    moved.greet()
    posload = pltpu.make_async_copy(pos_ref, pos, local.at[count - 1 + INNER_PIECES])
    stores = []

    def leave(src, dst):
        copy = pltpu.make_async_copy(src, dst, left.at[len(stores)])
        copy.start()
        stores.append(copy)

    def complete(n):
        moved.complete(n)
        if n < count - 1:
            leave(wholes[n], weights_out[n])

    def comm(*steps):
        for kind, n in steps:
            {"b": moved.begin, "o": moved.onward, "l": moved.last, "c": complete}[kind](n)

    comm(("b", 0), ("b", 1), ("b", 2))
    posload.start()
    per = rows_in[0].shape[0]
    for b in range(3):
        source = rows_in[b]

        def normalize(at, b=b, source=source):
            rows = source[at, :].astype(f32)
            centered = rows - jnp.mean(rows, axis=-1, keepdims=True)
            spread = lax.rsqrt(jnp.mean(centered * centered, axis=-1, keepdims=True) + EPSILON)
            xhat[b, at, :] = centered * spread

        tile_loop(per, 64, normalize)
        if b == 1:
            comm(("o", 0))
    leave(xhat.at[2], xhat_out)
    comm(("o", 1), ("b", 3), ("l", 0), ("c", 0))

    def row_of(k):
        height = shards[0].shape[0]
        return jnp.concatenate(
            [wholes[0][d * height : (d + 1) * height, :].astype(f32)[k : k + 1, :] for d in range(8)], axis=1
        )

    gain, shift, content, posbias = (row_of(k) for k in range(4))
    for b in range(3):

        def scale(at, b=b):
            normed[b, at, :] = (xhat[b, at, :] * gain + shift).astype(bf16)

        tile_loop(per, 64, scale)
    leave(normed, normed_out)
    comm(("o", 2), ("b", 4), ("l", 1), ("b", 5), ("c", 1))

    def project(src, weight, dst, steps):
        for b in range(3):

            def one(at, b=b):
                dst[b, at, :] = jnp.dot(
                    src[b, at, :], weight[...], preferred_element_type=f32
                ).astype(bf16)

            tile_loop(per, 256, one)
            comm(*steps[b])

    project(normed, wholes[1], keys, ((("o", 3), ("b", 6)), (("l", 2),), ()))
    leave(keys, keys_out)
    comm(("c", 2), ("o", 4), ("b", 7), ("l", 3))
    project(normed, wholes[2], values, ((), (("o", 5), ("b", 8)), (("l", 4),)))
    leave(values, values_out)
    comm(("c", 3))

    def queries(at):
        query = jnp.dot(normed[2, at, :], wholes[3][...], preferred_element_type=f32)
        qu[at, :] = (query + content).astype(bf16)
        qv[at, :] = (query + posbias).astype(bf16)

    tile_loop(per, 256, queries)
    leave(qu, qu_out)
    leave(qv, qv_out)
    comm(("o", 6), ("b", 9), ("l", 5), ("c", 4))
    posload.wait()
    project(pos, wholes[4], relative, ((("o", 7),), (("l", 6),), (("o", 8),)))
    leave(relative, relative_out)
    comm(("c", 5), ("l", 7), ("o", 9), ("l", 8), ("l", 9))
    for n in range(6, 10):
        complete(n)
    leave(wholes[-1], weights_out[-1])
    moved.drain()
    for copy in stores:
        copy.wait()


def head_stage(rows_in, shards, pos_low):
    per, width = rows_in[0].shape
    three = (3, per, width)
    count = len(shards)
    full = [(8 * w.shape[0], w.shape[1]) for w in shards]
    any_spec = pl.BlockSpec(memory_space=pl.ANY)
    shape = jax.ShapeDtypeStruct
    shapes = [shape((per, width), f32), shape(three, bf16)] + [shape((per, width), bf16)] * 2
    shapes += [shape(three, bf16)] * 3 + [shape(s, bf16) for s in full]
    vmem = pltpu.VMEM
    scratch = [vmem(s, bf16) for s in full] + [vmem(three, f32), vmem(three, bf16), vmem(three, bf16)]
    scratch += [vmem((per, width), bf16)] * 2 + [vmem(three, bf16)] * 3
    scratch += [pltpu.SemaphoreType.DMA((n,)) for n in (count + INNER_PIECES, 7 * (count + 3), 7 * (count + 3), 7 + count)]
    return pl.pallas_call(
        head_kernel,
        in_specs=[pl.BlockSpec(memory_space=pltpu.VMEM)] * 3 + [any_spec] * (count + 1),
        out_specs=[any_spec] * len(shapes),
        out_shape=shapes,
        scratch_shapes=scratch,
        compiler_params=pltpu.CompilerParams(
            collective_id=2, has_side_effects=True, vmem_limit_bytes=56 << 20
        ),
        name="head_stage",
    )(*rows_in, *shards, pos_low.reshape(three))


def gather(shards):
    return [lax.all_gather(w, "fsdp", axis=0, tiled=True) for w in shards]


def reduce(grads, share):
    done = []
    for g in grads:
        part = lax.psum_scatter(g, "fsdp", scatter_dimension=0, tiled=True)
        done.append(lax.psum(part, "dp").astype(f32) * share)
    return done


def pack_vectors(vectors, parts):
    flat = jnp.concatenate([v.reshape(parts, -1) for v in vectors], axis=1)
    width = 1024
    lines = 32 * (-(-flat.shape[1] // (32 * width)))
    flat = jnp.pad(flat, ((0, 0), (0, lines * width - flat.shape[1])))
    return flat.reshape(parts * lines, width)


def unpack_vectors(table, parts, sizes):
    flat = table.reshape(parts, -1)
    result, start = [], 0
    for size in sizes:
        result.append(flat[:, start : start + size].reshape(parts * size))
        start += size
    return result


def per_device_plain(
    tokens,
    memory,
    compressed,
    mem_fill,
    cmem_fill,
    pad_mask,
    first_gain,
    first_shift,
    query_weight,
    key_weight,
    value_weight,
    position_weight,
    content_bias,
    position_bias,
    output_weight,
    second_gain,
    second_shift,
    inner_weight,
    inner_bias,
    outer_weight,
    outer_bias,
    conv_weight,
    conv_bias,
    out_grad,
    comp_grad,
):
    streams, seg_rows, width = tokens.shape
    mem_rows = memory.shape[1]
    cmem_rows = compressed.shape[1]
    total = cmem_rows + mem_rows + seg_rows
    shards = lax.axis_size("fsdp")
    share = 1.0 / (streams * lax.axis_size("dp") * shards)
    vectors = (
        first_gain,
        first_shift,
        content_bias,
        position_bias,
        second_gain,
        second_shift,
        inner_bias,
        outer_bias,
        conv_bias,
    )
    sizes = [v.shape[0] for v in vectors]

    groups = mem_rows // RATE
    start = mem_rows - RATE * groups
    mem_valid = (
        jnp.arange(mem_rows, dtype=jnp.int32)[None, :] >= (mem_rows - mem_fill)[:, None]
    ).astype(bf16)
    taps = (memory * mem_valid[..., None])[:, start:, :].reshape(streams * groups, RATE * width)
    group_valid = (
        (start + RATE * jnp.arange(groups, dtype=jnp.int32) + RATE - 1)[None, :]
        >= (mem_rows - mem_fill)[:, None]
    ).reshape(streams * groups, 1)
    made_grad = comp_grad.reshape(streams * groups, width) * group_valid.astype(bf16)
    conv_grad = jnp.einsum("nk,nd->kd", taps, made_grad, preferred_element_type=f32).astype(bf16)
    conv_bias_grad = jnp.sum(made_grad.astype(f32), axis=0)

    query_w, key_w, value_w, table = gather(
        [query_weight, key_weight, value_weight, pack_vectors(vectors, 1)]
    )
    (gain_one, shift_one, content_b, position_b, gain_two, shift_two, inner_b, outer_b, conv_b) = (
        unpack_vectors(table, shards, sizes)
    )
    position_w, output_w = gather([position_weight, output_weight])
    (inner_w,) = gather([inner_weight])
    (outer_w,) = gather([outer_weight])
    (conv_w,) = gather([conv_weight])

    whole = jnp.concatenate([compressed[0], memory[0], tokens[0]], axis=0).astype(f32)
    normed, scaled_one, spread_one = norm_parts(whole, gain_one, shift_one)
    normed_low = normed.astype(bf16)
    own_rows = normed_low[total - seg_rows :]
    query = jnp.dot(own_rows, query_w, preferred_element_type=f32)
    query_u = (query + content_b.astype(f32)).astype(bf16)
    query_v = (query + position_b.astype(f32)).astype(bf16)
    keys = jnp.dot(normed_low, key_w, preferred_element_type=f32).astype(bf16)
    values = jnp.dot(normed_low, value_w, preferred_element_type=f32).astype(bf16)
    pos_low = positions(total, width).astype(bf16)
    relative = jnp.dot(pos_low, position_w, preferred_element_type=f32).astype(bf16)
    valid = jnp.concatenate(
        [
            jnp.arange(cmem_rows, dtype=jnp.int32) >= cmem_rows - cmem_fill[0],
            jnp.arange(mem_rows, dtype=jnp.int32) >= mem_rows - mem_fill[0],
            pad_mask[0] == 1,
        ]
    )
    bias = jnp.where(valid, 0.0, NEG).astype(f32)[None]
    mixed, prob_low = attn_fwd(query_u, query_v, keys, values, relative, bias)
    hidden = tokens[0].astype(f32) + jnp.dot(mixed, output_w, preferred_element_type=f32)
    inner_norm, scaled_two, spread_two = norm_parts(hidden, gain_two, shift_two)
    inner_low = inner_norm.astype(bf16)
    preact = jnp.dot(inner_low, inner_w, preferred_element_type=f32) + inner_b.astype(f32)
    active = smooth_gate(preact).astype(bf16)
    result = (
        hidden
        + jnp.dot(active, outer_w, preferred_element_type=f32)
        + outer_b.astype(f32)
    )
    made = (
        jnp.dot(taps, conv_w, preferred_element_type=f32) + conv_b.astype(f32)
    ) * group_valid.astype(f32)

    grad = out_grad[0]
    grad_wide = grad.astype(f32)
    outer_grad = jnp.einsum("sf,sd->fd", active, grad, preferred_element_type=f32).astype(bf16)
    (outer_mean,) = reduce([outer_grad], share)
    outer_bias_grad = jnp.sum(grad_wide, axis=0)
    active_grad = jnp.einsum("sd,fd->sf", grad, outer_w, preferred_element_type=f32)
    gate_pull = jax.vjp(smooth_gate, preact)[1]
    preact_grad = gate_pull(active_grad)[0].astype(bf16)
    inner_grad = jnp.einsum("sd,sf->df", inner_low, preact_grad, preferred_element_type=f32).astype(
        bf16
    )
    (inner_mean,) = reduce([inner_grad], share)
    (conv_mean,) = reduce([conv_grad], share)
    inner_bias_grad = jnp.sum(preact_grad.astype(f32), axis=0)
    inner_norm_grad = jnp.einsum("sf,df->sd", preact_grad, inner_w, preferred_element_type=f32)
    second_gain_grad = jnp.sum(inner_norm_grad * scaled_two, axis=0)
    second_shift_grad = jnp.sum(inner_norm_grad, axis=0)
    hidden_grad = grad_wide + norm_back(inner_norm_grad, scaled_two, spread_two, gain_two)

    hidden_low = hidden_grad.astype(bf16)
    output_grad = jnp.einsum("sd,se->de", mixed, hidden_low, preferred_element_type=f32).astype(bf16)
    mixed_grad = jnp.einsum("se,de->sd", hidden_low, output_w, preferred_element_type=f32).astype(
        bf16
    )
    query_low, keys_t, values_t, relative_t, sums = attn_bwd(
        query_u, query_v, keys, values, relative, prob_low, mixed_grad
    )
    position_grad = jnp.einsum("ld,el->de", pos_low, relative_t, preferred_element_type=f32).astype(
        bf16
    )
    query_grad = jnp.einsum("sd,se->de", own_rows, query_low, preferred_element_type=f32).astype(
        bf16
    )
    key_grad = jnp.einsum("sd,es->de", normed_low, keys_t, preferred_element_type=f32).astype(bf16)
    value_grad = jnp.einsum("sd,es->de", normed_low, values_t, preferred_element_type=f32).astype(
        bf16
    )
    normed_grad = jnp.einsum("es,de->sd", keys_t, key_w, preferred_element_type=f32)
    normed_grad = normed_grad + jnp.einsum(
        "es,de->sd", values_t, value_w, preferred_element_type=f32
    )
    own_grad = jnp.einsum("se,de->sd", query_low, query_w, preferred_element_type=f32)
    normed_grad = normed_grad + jnp.pad(own_grad, ((total - seg_rows, 0), (0, 0)))
    first_gain_grad = jnp.sum(normed_grad * scaled_one, axis=0)
    first_shift_grad = jnp.sum(normed_grad, axis=0)
    own = slice(total - seg_rows, None)
    token_gradient = hidden_grad + norm_back(
        normed_grad[own], scaled_one[own], spread_one[own], gain_one
    )
    vector_grads = (
        first_gain_grad,
        first_shift_grad,
        sums[0],
        sums[1],
        second_gain_grad,
        second_shift_grad,
        inner_bias_grad,
        outer_bias_grad,
        conv_bias_grad,
    )
    packed = pack_vectors([v.astype(bf16) for v in vector_grads], shards)
    (output_mean,) = reduce([output_grad], share)
    query_mean, key_mean, value_mean, position_mean, table_mean = reduce(
        [query_grad, key_grad, value_grad, position_grad, packed], share
    )
    (
        first_gain_mean,
        first_shift_mean,
        content_mean,
        posbias_mean,
        second_gain_mean,
        second_shift_mean,
        inner_bias_mean,
        outer_bias_mean,
        conv_bias_mean,
    ) = unpack_vectors(table_mean, 1, sizes)
    return (
        result.astype(bf16)[None],
        token_gradient[None],
        made.astype(bf16)[None],
        first_gain_mean,
        first_shift_mean,
        query_mean,
        key_mean,
        value_mean,
        position_mean,
        content_mean,
        posbias_mean,
        output_mean,
        second_gain_mean,
        second_shift_mean,
        inner_mean,
        inner_bias_mean,
        outer_mean,
        outer_bias_mean,
        conv_mean,
        conv_bias_mean,
    )


def per_device_direct(
    tokens,
    memory,
    compressed,
    mem_fill,
    cmem_fill,
    pad_mask,
    first_gain,
    first_shift,
    query_weight,
    key_weight,
    value_weight,
    position_weight,
    content_bias,
    position_bias,
    output_weight,
    second_gain,
    second_shift,
    inner_weight,
    inner_bias,
    outer_weight,
    outer_bias,
    conv_weight,
    conv_bias,
    out_grad,
    comp_grad,
):
    streams, seg_rows, width = tokens.shape
    mem_rows = memory.shape[1]
    cmem_rows = compressed.shape[1]
    total = cmem_rows + mem_rows + seg_rows
    old = total - seg_rows
    shards = lax.axis_size("fsdp")
    share = 1.0 / (streams * lax.axis_size("dp") * shards)
    lanes = 128
    vectors = (
        first_gain,
        first_shift,
        content_bias,
        position_bias,
        second_gain,
        second_shift,
        outer_bias,
        conv_bias,
        inner_bias,
    )
    sizes = [v.shape[0] for v in vectors]
    lines = [v.reshape(-1, lanes) for v in vectors]
    table = jnp.zeros((32, lanes), bf16)
    row, line = jnp.arange(32, dtype=jnp.int32)[:, None], 0
    for v in lines:
        for n in range(v.shape[0]):
            table = jnp.where(row == line, v[n][None], table)
            line += 1
    pos_low = positions_low(total, width)
    (
        scaled_one,
        normed_low,
        query_u,
        query_v,
        keys,
        values,
        relative,
        table,
        key_w,
        value_w,
        query_w,
        position_w,
        output_w,
        inner_w,
    ) = head_stage(
        (compressed[0], memory[0], tokens[0]),
        (table, key_weight, value_weight, query_weight, position_weight, output_weight, inner_weight),
        pos_low,
    )
    normed_low, keys, values, relative = (
        v.reshape(total, width) for v in (normed_low, keys, values, relative)
    )
    own_rows = normed_low[old:]
    blocks = table.reshape(shards, 32, lanes)
    gain_one, shift_one = blocks[:, 0].reshape(width), blocks[:, 1].reshape(width)
    gain_two, shift_two, outer_b, conv_b = (blocks[:, n].reshape(width) for n in (4, 5, 6, 7))
    inner_b = blocks[:, 8 : 8 + sizes[-1] // lanes].reshape(shards * sizes[-1])

    valid = jnp.concatenate(
        [
            jnp.arange(cmem_rows, dtype=jnp.int32) >= cmem_rows - cmem_fill[0],
            jnp.arange(mem_rows, dtype=jnp.int32) >= mem_rows - mem_fill[0],
            pad_mask[0] == 1,
        ]
    )
    bias = jnp.where(valid, 0.0, NEG).astype(f32)[None]
    outer_weight, query_u = cut(outer_weight, query_u)
    outer_w = lax.all_gather(outer_weight, "fsdp", axis=0, tiled=True)
    mixed, prob_low = attn_fwd(query_u, query_v, keys, values, relative, bias)
    hidden = tokens[0].astype(f32) + jnp.dot(mixed, output_w, preferred_element_type=f32)
    inner_norm, scaled_two, spread_two = norm_parts(hidden, gain_two, shift_two)
    inner_low = inner_norm.astype(bf16)
    preact = jnp.dot(inner_low, inner_w, preferred_element_type=f32) + inner_b.astype(f32)
    active = smooth_gate(preact).astype(bf16)
    grad = out_grad[0]
    grad_wide = grad.astype(f32)
    active, preact = cut(active, preact)
    outer_grad = jnp.einsum("sf,sd->fd", active, grad, preferred_element_type=f32).astype(bf16)
    outer_bias_grad = jnp.sum(grad_wide, axis=0)

    groups = mem_rows // RATE
    start = mem_rows - RATE * groups
    mem_valid = (jnp.arange(mem_rows, dtype=jnp.int32) >= mem_rows - mem_fill[0]).astype(bf16)
    taps = (memory[0] * mem_valid[:, None])[start:, :].reshape(groups, RATE * width)
    group_valid = (
        start + RATE * jnp.arange(groups, dtype=jnp.int32) + RATE - 1 >= mem_rows - mem_fill[0]
    )[:, None]
    made_grad = comp_grad[0] * group_valid.astype(bf16)
    made_grad, active = cut(made_grad, active)
    conv_grad = jnp.einsum("nk,nd->kd", taps, made_grad, preferred_element_type=f32).astype(bf16)
    conv_bias_grad = jnp.sum(made_grad.astype(f32), axis=0)

    outer_w, outer_grad, conv_grad = cut(outer_w, outer_grad, conv_grad)
    conv_part = lax.psum_scatter(conv_grad, "fsdp", scatter_dimension=0, tiled=True)
    outer_part = lax.psum_scatter(outer_grad, "fsdp", scatter_dimension=0, tiled=True)
    active_grad = jnp.einsum("sd,fd->sf", grad, outer_w, preferred_element_type=f32)
    gate_pull = jax.vjp(smooth_gate, preact)[1]
    preact_grad = gate_pull(active_grad)[0].astype(bf16)
    inner_bias_grad = jnp.sum(preact_grad.astype(f32), axis=0)
    inner_grad = jnp.einsum("sd,sf->df", inner_low, preact_grad, preferred_element_type=f32).astype(
        bf16
    )
    inner_norm_grad = jnp.einsum("sf,df->sd", preact_grad, inner_w, preferred_element_type=f32)
    second_gain_grad = jnp.sum(inner_norm_grad * scaled_two, axis=0)
    second_shift_grad = jnp.sum(inner_norm_grad, axis=0)
    hidden_grad = grad_wide + norm_back(inner_norm_grad, scaled_two, spread_two, gain_two)
    hidden_low = hidden_grad.astype(bf16)
    mixed_grad = jnp.einsum("se,de->sd", hidden_low, output_w, preferred_element_type=f32).astype(
        bf16
    )
    query_g, keys_g, values_g, relative_g, sums = attn_bwd(
        query_u, query_v, keys, values, relative, prob_low, mixed_grad
    )
    conv_part, query_g, conv_weight = cut(conv_part, query_g, conv_weight)
    conv_end = inward_hop(conv_part)
    conv_w = lax.all_gather(conv_weight, "fsdp", axis=0, tiled=True)
    key_grad = jnp.einsum("sd,es->de", normed_low, keys_g, preferred_element_type=f32).astype(bf16)
    value_grad = jnp.einsum("sd,es->de", normed_low, values_g, preferred_element_type=f32).astype(bf16)
    position_grad = jnp.einsum("ld,el->de", pos_low, relative_g, preferred_element_type=f32).astype(
        bf16
    )
    key_grad, value_grad, position_grad, conv_end, query_g = cut(
        key_grad, value_grad, position_grad, conv_end, query_g
    )
    conv_pair = add(conv_part, conv_end)
    conv_mid = middle_hop(conv_pair)
    query_grad = jnp.einsum("sd,se->de", own_rows, query_g, preferred_element_type=f32).astype(bf16)
    trio = (
        (query_w, query_grad, jnp.sum(query_g.astype(f32), axis=0)),
        (key_w, key_grad, jnp.sum(keys_g.astype(f32), axis=1)),
        (value_w, value_grad, jnp.sum(values_g.astype(f32), axis=1)),
    )
    first_shift_grad = sum(
        jnp.sum(w.astype(f32) * column[None, :], axis=1) for w, _, column in trio
    )
    with_normed = sum(jnp.sum(w.astype(f32) * g.astype(f32), axis=1) for w, g, _ in trio)
    first_gain_grad = (with_normed - shift_one.astype(f32) * first_shift_grad) / gain_one.astype(f32)
    own_grad = jnp.einsum("se,de->sd", query_g, query_w, preferred_element_type=f32)
    own_grad = own_grad + jnp.einsum(
        "es,de->sd", keys_g[:, old:], key_w, preferred_element_type=f32
    )
    own_grad = own_grad + jnp.einsum(
        "es,de->sd", values_g[:, old:], value_w, preferred_element_type=f32
    )
    inner = own_grad * gain_one.astype(f32)
    own = tokens[0].astype(f32)
    spread_own = lax.rsqrt(
        jnp.mean((own - jnp.mean(own, axis=-1, keepdims=True)) ** 2, axis=-1, keepdims=True) + EPSILON
    )
    token_gradient = hidden_grad + spread_own * (
        inner
        - jnp.mean(inner, axis=-1, keepdims=True)
        - scaled_one * jnp.mean(inner * scaled_one, axis=-1, keepdims=True)
    )
    conv_mid, own_grad, active, hidden_low = cut(conv_mid, own_grad, active, hidden_low)
    conv_sum = add(conv_pair, conv_mid)
    conv_last = outward_hop(conv_sum)
    output_grad = jnp.einsum("sd,se->de", mixed, hidden_low, preferred_element_type=f32).astype(bf16)
    vector_grads = (
        first_gain_grad,
        first_shift_grad,
        sums[0],
        sums[1],
        second_gain_grad,
        second_shift_grad,
        outer_bias_grad,
        conv_bias_grad,
        inner_bias_grad,
    )
    packed = jnp.concatenate([v.reshape(shards, -1, lanes) for v in vector_grads], axis=1)
    packed = jnp.pad(packed, ((0, 0), (0, 32 - packed.shape[1]), (0, 0))).astype(bf16)
    result = (
        hidden + jnp.dot(active, outer_w, preferred_element_type=f32) + outer_b.astype(f32)
    ).astype(bf16)
    made = (
        (jnp.dot(taps, conv_w, preferred_element_type=f32) + conv_b.astype(f32))
        * group_valid.astype(f32)
    ).astype(bf16)
    (
        output_mean,
        query_mean,
        key_mean,
        value_mean,
        position_mean,
        inner_mean,
        table_mean,
        outer_mean,
    ) = reduce_tail(
        [(g, 1) for g in (output_grad, query_grad, key_grad, value_grad, position_grad)]
        + [(inner_grad, 4)]
        + [(packed.reshape(shards * 32, lanes), 1)],
        [(outer_part, 4)],
        share,
        1,
    )
    conv_last, query_mean = cut(conv_last, query_mean)
    conv_mean = finish(conv_sum, conv_last, share)
    (
        first_gain_mean,
        first_shift_mean,
        content_mean,
        posbias_mean,
        second_gain_mean,
        second_shift_mean,
        outer_bias_mean,
        conv_bias_mean,
    ) = (table_mean[n] for n in range(8))
    inner_bias_mean = table_mean[8 : 8 + sizes[-1] // lanes].reshape(sizes[-1])
    return (
        result[None],
        token_gradient[None],
        made[None],
        first_gain_mean,
        first_shift_mean,
        query_mean,
        key_mean,
        value_mean,
        position_mean,
        content_mean,
        posbias_mean,
        output_mean,
        second_gain_mean,
        second_shift_mean,
        inner_mean,
        inner_bias_mean,
        outer_mean,
        outer_bias_mean,
        conv_mean,
        conv_bias_mean,
    )


def per_device(*arguments):
    if lax.axis_size("dp") == 4 and lax.axis_size("fsdp") == 8:
        return per_device_direct(*arguments)
    return per_device_plain(*arguments)


def solution(mesh):
    in_specs = (
        P(("dp", "fsdp"), None, None),
        P(("dp", "fsdp"), None, None),
        P(("dp", "fsdp"), None, None),
        P(("dp", "fsdp")),
        P(("dp", "fsdp")),
        P(("dp", "fsdp"), None),
        P("fsdp"),
        P("fsdp"),
        P("fsdp", None),
        P("fsdp", None),
        P("fsdp", None),
        P("fsdp", None),
        P("fsdp"),
        P("fsdp"),
        P("fsdp", None),
        P("fsdp"),
        P("fsdp"),
        P("fsdp", None),
        P("fsdp"),
        P("fsdp", None),
        P("fsdp"),
        P("fsdp", None),
        P("fsdp"),
        P(("dp", "fsdp"), None, None),
        P(("dp", "fsdp"), None, None),
    )
    out_specs = (
        P(("dp", "fsdp"), None, None),
        P(("dp", "fsdp"), None, None),
        P(("dp", "fsdp"), None, None),
        P("fsdp"),
        P("fsdp"),
        P("fsdp", None),
        P("fsdp", None),
        P("fsdp", None),
        P("fsdp", None),
        P("fsdp"),
        P("fsdp"),
        P("fsdp", None),
        P("fsdp"),
        P("fsdp"),
        P("fsdp", None),
        P("fsdp"),
        P("fsdp", None),
        P("fsdp"),
        P("fsdp", None),
        P("fsdp"),
    )
    return jax.shard_map(
        per_device, mesh=mesh, in_specs=in_specs, out_specs=out_specs, check_vma=False
    )
```
